512 devices in a mesh: row: 8 (over y_hi, core), col: 16 (over z, y_lo), vec: 4 (over x).
Axes of the slice: x: 4, y: 8 (y_hi: 4, y_lo: 2; y = y_hi * 2 + y_lo), z: 8, core: 2. Of those that a mesh axis runs over, the one named last changes fastest.
Arguments:
- particles: bfloat16 [16384, 512], P(('row', 'col', 'vec')), may hold values from -6 to 6
- start_basis: float32 [16384, 64], P(('row', 'col', 'vec')), may hold values from -6 to 6
Outputs:
- basis: float32 [16384, 64], P(('row', 'col', 'vec'))
- factor: float32 [64, 64], replicated
The draws below stay inside these ranges and needn't reach their ends.
All inputs are finite; a program needn't handle non-finite values.
Results may differ from the reference program's by a relative error of at most 0.0003.
Values may be sent and summed in bfloat16 or wider, within the bound.
A program may use at most 64 MiB of HBM per device.

```python
import math
import jax
import jax.numpy as jnp
from jax import lax

FEAT = 512
EIG = 64
ITERS = 2
PARTICLES = 16384


def steps_of(rng, dims, split, low, largest):
    gain = 1.0
    for dim, parts in split:
        draws = jax.random.uniform(jax.random.fold_in(jax.random.fold_in(rng, 6), dim), (parts,), jnp.float32, low / len(split), largest / len(split))
        gain = gain * jnp.repeat(jnp.exp(draws), dims[dim] // parts).reshape((-1,) + (1,) * (len(dims) - 1 - dim))
    return gain


def gaussian(rng, shape, scale, reach, split=(), kind=jnp.bfloat16):
    entries = scale * jax.random.normal(rng, shape, jnp.float32)
    if split:
        entries = entries * steps_of(rng, shape, split, -0.22, 0.18)
    return jnp.clip(entries, -reach, reach).astype(kind)


def setup_inputs(seed: int = 0) -> dict:
    keys = jax.random.split(jax.random.key(seed), 3)
    particles = gaussian(keys[0], (PARTICLES, FEAT), 1.0, 6.0, ((0, 512),))
    start_basis = gaussian(keys[1], (PARTICLES, EIG), 1.0, 6.0, ((0, 512),), jnp.float32)
    return dict(particles=particles, start_basis=start_basis)


def reference(particles, start_basis):
    total_rows = PARTICLES
    block_rows = math.gcd(total_rows, 512)
    block_count = total_rows // block_rows
    spread = 2.0 * FEAT
    particles_f = particles.astype(jnp.float32)
    squares = lax.optimization_barrier(jnp.sum(particles_f * particles_f, axis=1))
    all_ids = jnp.arange(total_rows, dtype=jnp.int32)
    block_list = jnp.arange(block_count, dtype=jnp.int32)

    def kernel_rows(block_idx):
        offset = (block_idx * block_rows).astype(jnp.int32)
        row_block = lax.dynamic_slice_in_dim(particles, offset, block_rows, 0)
        row_sq = lax.dynamic_slice_in_dim(squares, offset, block_rows, 0)
        inner_dots = jnp.dot(row_block.astype(jnp.float32), particles.T.astype(jnp.float32), preferred_element_type=jnp.float32)
        distance = row_sq[:, None] + squares[None, :] - 2.0 * inner_dots
        row_ids = offset + jnp.arange(block_rows, dtype=jnp.int32)
        return jnp.where(row_ids[:, None] == all_ids[None, :], jnp.float32(0.0), jnp.exp(-distance / spread))
    degree = lax.map(lambda block_idx: lax.optimization_barrier(jnp.sum(kernel_rows(block_idx), axis=1)), block_list).reshape(total_rows)
    degree_sum = jnp.sum(degree)
    inv_root = 1.0 / jnp.sqrt(degree)
    root_vec = jnp.sqrt(degree) / jnp.sqrt(degree_sum)
    basis_now = start_basis
    factor = jnp.zeros((EIG, EIG), jnp.float32)
    for sweep in range(ITERS):
        scaled = basis_now * inv_root[:, None]
        product = lax.map(lambda block_idx: jnp.dot(kernel_rows(block_idx), scaled, precision=lax.Precision.HIGHEST), block_list).reshape(total_rows, EIG)
        aligned = jnp.dot(root_vec, basis_now, precision=lax.Precision.HIGHEST)
        deflated = product * inv_root[:, None] - root_vec[:, None] * aligned[None, :]
        gram_mat = jnp.dot(deflated.T, deflated, precision=lax.Precision.HIGHEST)
        factor = jnp.linalg.cholesky(gram_mat)
        solved = jax.scipy.linalg.solve_triangular(factor, deflated.T, lower=True)
        basis_now = solved.T * math.sqrt(float(total_rows))
    return (basis_now, factor)
```

```python
import functools
import math

import jax
import jax.numpy as jnp
from jax import lax
from jax.experimental import pallas as pl
from jax.experimental.pallas import tpu as pltpu
from jax.sharding import PartitionSpec as P

ITERS = 2
MESH_AXES = ("row", "col", "vec")
MESH = pl.DeviceIdType.MESH
HIGH = lax.Precision.HIGHEST


SIZES = {}


def group_pos(axes):
    me = 0
    for a in axes:
        me = me * SIZES[a] + lax.axis_index(a)
    return me


def group_size(axes):
    return math.prod(SIZES[a] for a in axes)


def peer_id(axes, k):
    coords = {}
    rem = k
    for a in reversed(axes):
        n = SIZES[a]
        coords[a] = rem % n
        rem = rem // n
    return tuple(coords[a] if a in coords else lax.axis_index(a) for a in MESH_AXES)


def exchange_kernel(ops, groups, *refs):
    n = len(ops)
    ins, outs, scr = refs[:n], refs[n:2 * n], refs[2 * n:]
    barrier = pltpu.get_barrier_semaphore()
    total_peers = 0
    for axes in groups:
        g = group_size(axes)
        me = group_pos(axes)
        total_peers += g - 1

        def greet(k, c, axes=axes, g=g, me=me):
            pl.semaphore_signal(barrier, inc=1, device_id=peer_id(axes, (me + k) % g), device_id_type=MESH)
            return c

        lax.fori_loop(1, g, greet, 0)
    pl.semaphore_wait(barrier, total_peers)

    pos = 0
    pending = []
    for i, (kind, axes) in enumerate(ops):
        g = group_size(axes)
        me = group_pos(axes)
        x_ref, o_ref = ins[i], outs[i]
        if kind in ("gather", "sum"):
            slots, ssem, rsem = scr[pos:pos + 3]
            pos += 3
            slots[me] = x_ref[...]

            def send(k, c, x_ref=x_ref, slots=slots, ssem=ssem, rsem=rsem, axes=axes, g=g, me=me):
                peer = (me + k) % g
                pltpu.make_async_remote_copy(
                    src_ref=x_ref, dst_ref=slots.at[me], send_sem=ssem.at[peer], recv_sem=rsem.at[me],
                    device_id=peer_id(axes, peer), device_id_type=MESH).start()
                return c

            lax.fori_loop(1, g, send, 0)
            pending.append((kind, axes, g, me, x_ref, o_ref, slots, ssem, rsem))
        else:
            rs, ag, ssem, rsem, ssem2, rsem2 = scr[pos:pos + 6]
            pos += 6
            c = x_ref.shape[0] // g
            rs[me] = x_ref[pl.ds(pl.multiple_of(me * c, c), c)]

            def send(k, cc, x_ref=x_ref, rs=rs, ssem=ssem, rsem=rsem, axes=axes, g=g, me=me, c=c):
                peer = (me + k) % g
                pltpu.make_async_remote_copy(
                    src_ref=x_ref.at[pl.ds(pl.multiple_of(peer * c, c), c)], dst_ref=rs.at[me],
                    send_sem=ssem.at[peer], recv_sem=rsem.at[me],
                    device_id=peer_id(axes, peer), device_id_type=MESH).start()
                return cc

            lax.fori_loop(1, g, send, 0)
            pending.append((kind, axes, g, me, x_ref, o_ref, (rs, ag, ssem2, rsem2), ssem, rsem))

    for kind, axes, g, me, x_ref, o_ref, slots, ssem, rsem in pending:
        if kind == "rsag":
            rs, ag, ssem2, rsem2 = slots
            c = rs.shape[1]
        else:
            rs = slots

        def wait(k, cc, x_ref=x_ref, rs=rs, ssem=ssem, rsem=rsem, axes=axes, g=g, me=me, kind=kind):
            src = (me + g - k) % g
            peer = (me + k) % g
            if kind == "rsag":
                c = rs.shape[1]
                src_ref = x_ref.at[pl.ds(0, c)]
            else:
                src_ref = x_ref
            pltpu.make_async_remote_copy(
                src_ref=src_ref, dst_ref=rs.at[src], send_sem=ssem.at[peer], recv_sem=rsem.at[src],
                device_id=peer_id(axes, peer), device_id_type=MESH).wait_recv()
            pltpu.make_async_remote_copy(
                src_ref=src_ref, dst_ref=rs.at[me], send_sem=ssem.at[peer], recv_sem=rsem.at[me],
                device_id=peer_id(axes, peer), device_id_type=MESH).wait_send()
            return cc

        lax.fori_loop(1, g, wait, 0)
        if kind == "gather":
            o_ref[...] = rs[...]
        elif kind == "sum":
            acc = rs[0]
            for s in range(1, g):
                acc = acc + rs[s]
            o_ref[...] = acc
        else:
            acc = rs[0]
            for s in range(1, g):
                acc = acc + rs[s]
            ag[me] = acc

            def send2(k, cc, ag=ag, ssem2=ssem2, rsem2=rsem2, axes=axes, g=g, me=me):
                peer = (me + k) % g
                pltpu.make_async_remote_copy(
                    src_ref=ag.at[me], dst_ref=ag.at[me], send_sem=ssem2.at[peer], recv_sem=rsem2.at[me],
                    device_id=peer_id(axes, peer), device_id_type=MESH).start()
                return cc

            lax.fori_loop(1, g, send2, 0)

            def wait2(k, cc, ag=ag, ssem2=ssem2, rsem2=rsem2, axes=axes, g=g, me=me):
                src = (me + g - k) % g
                peer = (me + k) % g
                pltpu.make_async_remote_copy(
                    src_ref=ag.at[me], dst_ref=ag.at[src], send_sem=ssem2.at[peer], recv_sem=rsem2.at[src],
                    device_id=peer_id(axes, peer), device_id_type=MESH).wait_recv()
                pltpu.make_async_remote_copy(
                    src_ref=ag.at[me], dst_ref=ag.at[me], send_sem=ssem2.at[peer], recv_sem=rsem2.at[me],
                    device_id=peer_id(axes, peer), device_id_type=MESH).wait_send()
                return cc

            lax.fori_loop(1, g, wait2, 0)
            o_ref[...] = ag[...]


_IDS = {}


def exchange(ops, xs, sizes):
    key = tuple((k, a, x.shape, str(x.dtype)) for (k, a), x in zip(ops, xs))
    if key not in _IDS:
        _IDS[key] = len(_IDS)
    groups = []
    for _, axes in ops:
        if axes not in groups:
            groups.append(axes)
    out_shapes, scratch = [], []
    for (kind, axes), x in zip(ops, xs):
        g = math.prod(sizes[a] for a in axes)
        if kind == "gather":
            out_shapes.append(jax.ShapeDtypeStruct((g,) + x.shape, x.dtype))
            scratch += [pltpu.VMEM((g,) + x.shape, x.dtype), pltpu.SemaphoreType.DMA((g,)),
                        pltpu.SemaphoreType.DMA((g,))]
        elif kind == "sum":
            out_shapes.append(jax.ShapeDtypeStruct(x.shape, x.dtype))
            scratch += [pltpu.VMEM((g,) + x.shape, x.dtype), pltpu.SemaphoreType.DMA((g,)),
                        pltpu.SemaphoreType.DMA((g,))]
        else:
            c = x.shape[0] // g
            out_shapes.append(jax.ShapeDtypeStruct((g, c) + x.shape[1:], x.dtype))
            scratch += [pltpu.VMEM((g, c) + x.shape[1:], x.dtype), pltpu.VMEM((g, c) + x.shape[1:], x.dtype),
                        pltpu.SemaphoreType.DMA((g,)), pltpu.SemaphoreType.DMA((g,)),
                        pltpu.SemaphoreType.DMA((g,)), pltpu.SemaphoreType.DMA((g,))]
    outs = pl.pallas_call(
        functools.partial(exchange_kernel, ops, groups),
        out_shape=out_shapes,
        in_specs=[pl.BlockSpec(memory_space=pltpu.VMEM)] * len(xs),
        out_specs=[pl.BlockSpec(memory_space=pltpu.VMEM)] * len(xs),
        scratch_shapes=scratch,
        compiler_params=pltpu.CompilerParams(collective_id=_IDS[key], has_side_effects=True),
    )(*xs)
    res = []
    for (kind, axes), x, o in zip(ops, xs, outs):
        if kind == "rsag":
            o = o.reshape(x.shape)
        res.append(o)
    return res


def make_local(sizes, row_axes, col_axes):
    def local(particles, start_basis):
        shard = particles.shape[0]
        width = particles.shape[1]
        eig = start_basis.shape[1]
        total = shard * math.prod(sizes.values())
        spread = 2.0 * width
        root_total = math.sqrt(float(total))

        i_feats, i_basis, j_feats, j_basis = exchange(
            [("gather", row_axes), ("gather", row_axes), ("gather", col_axes), ("gather", col_axes)],
            [particles, start_basis, particles, start_basis], sizes)
        gi = math.prod(sizes[a] for a in row_axes)
        gj = math.prod(sizes[a] for a in col_axes)
        i_feats = i_feats.reshape(gi * shard, width)
        j_feats = j_feats.reshape(gj * shard, width)
        basis_i = i_basis.reshape(gi * shard, eig)
        basis_j = j_basis.reshape(gj * shard, eig)

        def block_ids(axes):
            g = math.prod(sizes[a] for a in axes)
            k = jnp.arange(g, dtype=jnp.int32)
            coords = {}
            rem = k
            for a in reversed(axes):
                coords[a] = rem % sizes[a]
                rem = rem // sizes[a]
            flat = jnp.zeros((g,), jnp.int32)
            for a in MESH_AXES:
                cval = coords[a] if a in coords else lax.axis_index(a)
                flat = flat * sizes[a] + cval
            return (flat[:, None] * shard + jnp.arange(shard, dtype=jnp.int32)[None, :]).reshape(-1)

        ids_i = block_ids(row_axes)
        ids_j = block_ids(col_axes)
        sq_i = jnp.sum(jnp.square(i_feats.astype(jnp.float32)), axis=1)
        sq_j = jnp.sum(jnp.square(j_feats.astype(jnp.float32)), axis=1)
        dots = lax.dot_general(i_feats, j_feats, (((1,), (1,)), ((), ())), preferred_element_type=jnp.float32)
        distance = sq_i[:, None] + sq_j[None, :] - 2.0 * dots
        tile = jnp.where(ids_i[:, None] == ids_j[None, :], jnp.float32(0.0), jnp.exp(-distance / spread))

        deg_i, deg_j = exchange(
            [("sum", row_axes), ("sum", col_axes)],
            [jnp.sum(tile, axis=1)[None, :], jnp.sum(tile, axis=0)[None, :]], sizes)
        deg_i = deg_i[0]
        deg_j = deg_j[0]
        root_i = jnp.sqrt(deg_i)
        root_j = jnp.sqrt(deg_j)
        me_i = group_pos(row_axes)
        factor = None
        for sweep in range(ITERS):
            last = sweep == ITERS - 1
            scaled_i = basis_i / root_i[:, None]
            scaled_j = basis_j / root_j[:, None]
            prod_i = jnp.dot(tile, scaled_j, precision=HIGH)
            extra = jnp.dot(root_j, basis_j, precision=HIGH)[None, :]
            if sweep == 0:
                extra = jnp.concatenate([extra, jnp.broadcast_to(jnp.sum(deg_j), (1, eig))], axis=0)
            else:
                extra = jnp.concatenate([extra, jnp.zeros((1, eig), jnp.float32)], axis=0)
            extra = jnp.concatenate([extra, jnp.zeros((6, eig), jnp.float32)], axis=0)
            if not last:
                prod_j = lax.dot_general(tile, scaled_i, (((0,), (0,)), ((), ())), precision=HIGH)
                prod_i, extra, prod_j = exchange(
                    [("rsag", row_axes), ("sum", row_axes), ("rsag", col_axes)], [prod_i, extra, prod_j], sizes)
            else:
                prod_i, extra = exchange([("rsag", row_axes), ("sum", row_axes)], [prod_i, extra], sizes)
            if sweep == 0:
                degree_sum = extra[1, 0]
                inv_s = 1.0 / jnp.sqrt(degree_sum)
            aligned = extra[0] * inv_s
            defl_i = prod_i / root_i[:, None] - (root_i * inv_s)[:, None] * aligned[None, :]
            gram = lax.dot_general(defl_i, defl_i, (((0,), (0,)), ((), ())), precision=HIGH)
            (gram,) = exchange([("sum", col_axes)], [gram], sizes)
            factor = jnp.linalg.cholesky(gram)
            if not last:
                defl_j = prod_j / root_j[:, None] - (root_j * inv_s)[:, None] * aligned[None, :]
                basis_i = jax.scipy.linalg.solve_triangular(factor, defl_i.T, lower=True).T * root_total
                basis_j = jax.scipy.linalg.solve_triangular(factor, defl_j.T, lower=True).T * root_total
            else:
                own = lax.dynamic_slice_in_dim(defl_i, me_i * shard, shard, 0)
                basis_own = jax.scipy.linalg.solve_triangular(factor, own.T, lower=True).T * root_total
        return basis_own, factor

    return local


def solution(mesh):
    sizes = dict(mesh.shape)
    SIZES.update(sizes)
    placed = (P(MESH_AXES, None), P(MESH_AXES, None))
    return jax.shard_map(
        make_local(sizes, ("row", "vec"), ("col",)),
        mesh=mesh,
        in_specs=placed,
        out_specs=(P(MESH_AXES, None), P()),
        check_vma=False,
    )
```

```python
import functools
import math

import jax
import jax.numpy as jnp
from jax import lax
from jax.experimental import pallas as pl
from jax.experimental.pallas import tpu as pltpu
from jax.sharding import PartitionSpec as P

ITERS = 2
MESH_AXES = ("row", "col", "vec")
MESH = pl.DeviceIdType.MESH
HIGH = lax.Precision.HIGHEST


SIZES = {}


def group_pos(axes):
    me = 0
    for a in axes:
        me = me * SIZES[a] + lax.axis_index(a)
    return me


def group_size(axes):
    return math.prod(SIZES[a] for a in axes)


def peer_id(axes, k):
    coords = {}
    rem = k
    for a in reversed(axes):
        n = SIZES[a]
        coords[a] = rem % n
        rem = rem // n
    return tuple(coords[a] if a in coords else lax.axis_index(a) for a in MESH_AXES)


def exchange_kernel(ops, groups, *refs):
    n = len(ops)
    ins, outs, scr = refs[:n], refs[n:2 * n], refs[2 * n:]
    barrier = pltpu.get_barrier_semaphore()
    total_peers = 0
    for axes in groups:
        g = group_size(axes)
        me = group_pos(axes)
        total_peers += g - 1

        def greet(k, c, axes=axes, g=g, me=me):
            pl.semaphore_signal(barrier, inc=1, device_id=peer_id(axes, (me + k) % g), device_id_type=MESH)
            return c

        lax.fori_loop(1, g, greet, 0)
    pl.semaphore_wait(barrier, total_peers)

    pos = 0
    pending = []
    for i, (kind, axes) in enumerate(ops):
        g = group_size(axes)
        me = group_pos(axes)
        x_ref, o_ref = ins[i], outs[i]
        if kind in ("gather", "sum"):
            slots, ssem, rsem = scr[pos:pos + 3]
            pos += 3
            slots[me] = x_ref[...]

            def send(k, c, x_ref=x_ref, slots=slots, ssem=ssem, rsem=rsem, axes=axes, g=g, me=me):
                peer = (me + k) % g
                pltpu.make_async_remote_copy(
                    src_ref=x_ref, dst_ref=slots.at[me], send_sem=ssem.at[peer], recv_sem=rsem.at[me],
                    device_id=peer_id(axes, peer), device_id_type=MESH).start()
                return c

            lax.fori_loop(1, g, send, 0)
            pending.append((kind, axes, g, me, x_ref, o_ref, slots, ssem, rsem))
        else:
            rs, ag, ssem, rsem, ssem2, rsem2 = scr[pos:pos + 6]
            pos += 6
            c = x_ref.shape[0] // g
            rs[me] = x_ref[pl.ds(pl.multiple_of(me * c, c), c)]

            def send(k, cc, x_ref=x_ref, rs=rs, ssem=ssem, rsem=rsem, axes=axes, g=g, me=me, c=c):
                peer = (me + k) % g
                pltpu.make_async_remote_copy(
                    src_ref=x_ref.at[pl.ds(pl.multiple_of(peer * c, c), c)], dst_ref=rs.at[me],
                    send_sem=ssem.at[peer], recv_sem=rsem.at[me],
                    device_id=peer_id(axes, peer), device_id_type=MESH).start()
                return cc

            lax.fori_loop(1, g, send, 0)
            pending.append((kind, axes, g, me, x_ref, o_ref, (rs, ag, ssem2, rsem2), ssem, rsem))

    for kind, axes, g, me, x_ref, o_ref, slots, ssem, rsem in pending:
        if kind == "rsag":
            rs, ag, ssem2, rsem2 = slots
            c = rs.shape[1]
        else:
            rs = slots

        def wait(k, cc, x_ref=x_ref, rs=rs, ssem=ssem, rsem=rsem, axes=axes, g=g, me=me, kind=kind):
            src = (me + g - k) % g
            peer = (me + k) % g
            if kind == "rsag":
                c = rs.shape[1]
                src_ref = x_ref.at[pl.ds(0, c)]
            else:
                src_ref = x_ref
            pltpu.make_async_remote_copy(
                src_ref=src_ref, dst_ref=rs.at[src], send_sem=ssem.at[peer], recv_sem=rsem.at[src],
                device_id=peer_id(axes, peer), device_id_type=MESH).wait_recv()
            pltpu.make_async_remote_copy(
                src_ref=src_ref, dst_ref=rs.at[me], send_sem=ssem.at[peer], recv_sem=rsem.at[me],
                device_id=peer_id(axes, peer), device_id_type=MESH).wait_send()
            return cc

        lax.fori_loop(1, g, wait, 0)
        if kind == "gather":
            o_ref[...] = rs[...]
        elif kind == "sum":
            acc = rs[0]
            for s in range(1, g):
                acc = acc + rs[s]
            o_ref[...] = acc
        else:
            acc = rs[0]
            for s in range(1, g):
                acc = acc + rs[s]
            ag[me] = acc

            def send2(k, cc, ag=ag, ssem2=ssem2, rsem2=rsem2, axes=axes, g=g, me=me):
                peer = (me + k) % g
                pltpu.make_async_remote_copy(
                    src_ref=ag.at[me], dst_ref=ag.at[me], send_sem=ssem2.at[peer], recv_sem=rsem2.at[me],
                    device_id=peer_id(axes, peer), device_id_type=MESH).start()
                return cc

            lax.fori_loop(1, g, send2, 0)

            def wait2(k, cc, ag=ag, ssem2=ssem2, rsem2=rsem2, axes=axes, g=g, me=me):
                src = (me + g - k) % g
                peer = (me + k) % g
                pltpu.make_async_remote_copy(
                    src_ref=ag.at[me], dst_ref=ag.at[src], send_sem=ssem2.at[peer], recv_sem=rsem2.at[src],
                    device_id=peer_id(axes, peer), device_id_type=MESH).wait_recv()
                pltpu.make_async_remote_copy(
                    src_ref=ag.at[me], dst_ref=ag.at[me], send_sem=ssem2.at[peer], recv_sem=rsem2.at[me],
                    device_id=peer_id(axes, peer), device_id_type=MESH).wait_send()
                return cc

            lax.fori_loop(1, g, wait2, 0)
            o_ref[...] = ag[...]


_IDS = {}


def exchange(ops, xs, sizes):
    key = tuple((k, a, x.shape, str(x.dtype)) for (k, a), x in zip(ops, xs))
    if key not in _IDS:
        _IDS[key] = len(_IDS)
    groups = []
    for _, axes in ops:
        if axes not in groups:
            groups.append(axes)
    out_shapes, scratch = [], []
    for (kind, axes), x in zip(ops, xs):
        g = math.prod(sizes[a] for a in axes)
        if kind == "gather":
            out_shapes.append(jax.ShapeDtypeStruct((g,) + x.shape, x.dtype))
            scratch += [pltpu.VMEM((g,) + x.shape, x.dtype), pltpu.SemaphoreType.DMA((g,)),
                        pltpu.SemaphoreType.DMA((g,))]
        elif kind == "sum":
            out_shapes.append(jax.ShapeDtypeStruct(x.shape, x.dtype))
            scratch += [pltpu.VMEM((g,) + x.shape, x.dtype), pltpu.SemaphoreType.DMA((g,)),
                        pltpu.SemaphoreType.DMA((g,))]
        else:
            c = x.shape[0] // g
            out_shapes.append(jax.ShapeDtypeStruct((g, c) + x.shape[1:], x.dtype))
            scratch += [pltpu.VMEM((g, c) + x.shape[1:], x.dtype), pltpu.VMEM((g, c) + x.shape[1:], x.dtype),
                        pltpu.SemaphoreType.DMA((g,)), pltpu.SemaphoreType.DMA((g,)),
                        pltpu.SemaphoreType.DMA((g,)), pltpu.SemaphoreType.DMA((g,))]
    outs = pl.pallas_call(
        functools.partial(exchange_kernel, ops, groups),
        out_shape=out_shapes,
        in_specs=[pl.BlockSpec(memory_space=pltpu.VMEM)] * len(xs),
        out_specs=[pl.BlockSpec(memory_space=pltpu.VMEM)] * len(xs),
        scratch_shapes=scratch,
        compiler_params=pltpu.CompilerParams(collective_id=_IDS[key], has_side_effects=True),
    )(*xs)
    res = []
    for (kind, axes), x, o in zip(ops, xs, outs):
        if kind == "rsag":
            o = o.reshape(x.shape)
        res.append(o)
    return res


def make_local(sizes, row_axes, col_axes):
    def local(particles, start_basis):
        shard = particles.shape[0]
        width = particles.shape[1]
        eig = start_basis.shape[1]
        total = shard * math.prod(sizes.values())
        spread = 2.0 * width
        root_total = math.sqrt(float(total))

        dense_basis = start_basis.reshape(shard * eig // 128, 128)
        i_feats, i_basis, j_feats, j_basis = exchange(
            [("gather", row_axes), ("gather", row_axes), ("gather", col_axes), ("gather", col_axes)],
            [particles, dense_basis, particles, dense_basis], sizes)
        gi = math.prod(sizes[a] for a in row_axes)
        gj = math.prod(sizes[a] for a in col_axes)
        i_feats = i_feats.reshape(gi * shard, width)
        j_feats = j_feats.reshape(gj * shard, width)
        basis_i = i_basis.reshape(gi * shard, eig)
        basis_j = j_basis.reshape(gj * shard, eig)

        def block_ids(axes):
            g = math.prod(sizes[a] for a in axes)
            k = jnp.arange(g, dtype=jnp.int32)
            coords = {}
            rem = k
            for a in reversed(axes):
                coords[a] = rem % sizes[a]
                rem = rem // sizes[a]
            flat = jnp.zeros((g,), jnp.int32)
            for a in MESH_AXES:
                cval = coords[a] if a in coords else lax.axis_index(a)
                flat = flat * sizes[a] + cval
            return (flat[:, None] * shard + jnp.arange(shard, dtype=jnp.int32)[None, :]).reshape(-1)

        ids_i = block_ids(row_axes)
        ids_j = block_ids(col_axes)
        sq_i = jnp.sum(jnp.square(i_feats.astype(jnp.float32)), axis=1)
        sq_j = jnp.sum(jnp.square(j_feats.astype(jnp.float32)), axis=1)
        dots = lax.dot_general(i_feats, j_feats, (((1,), (1,)), ((), ())), preferred_element_type=jnp.float32)
        distance = sq_i[:, None] + sq_j[None, :] - 2.0 * dots
        tile = jnp.where(ids_i[:, None] == ids_j[None, :], jnp.float32(0.0), jnp.exp(-distance / spread))

        deg_i, deg_j = exchange(
            [("sum", row_axes), ("sum", col_axes)],
            [jnp.sum(tile, axis=1).reshape(-1, 128), jnp.sum(tile, axis=0).reshape(-1, 128)], sizes)
        deg_i = deg_i.reshape(-1)
        deg_j = deg_j.reshape(-1)
        root_i = jnp.sqrt(deg_i)
        root_j = jnp.sqrt(deg_j)
        me_i = group_pos(row_axes)
        factor = None
        for sweep in range(ITERS):
            last = sweep == ITERS - 1
            scaled_i = basis_i / root_i[:, None]
            scaled_j = basis_j / root_j[:, None]
            prod_i = jnp.dot(tile, scaled_j, precision=HIGH)
            extra = jnp.dot(root_j, basis_j, precision=HIGH)[None, :]
            if sweep == 0:
                extra = jnp.concatenate([extra, jnp.broadcast_to(jnp.sum(deg_j), (1, eig))], axis=0)
            else:
                extra = jnp.concatenate([extra, jnp.zeros((1, eig), jnp.float32)], axis=0)
            extra = jnp.concatenate([extra, jnp.zeros((6, eig), jnp.float32)], axis=0).reshape(-1, 128)
            dense_i = prod_i.reshape(-1, 128)
            if not last:
                prod_j = lax.dot_general(tile, scaled_i, (((0,), (0,)), ((), ())), precision=HIGH)
                dense_i, extra, dense_j = exchange(
                    [("rsag", row_axes), ("sum", row_axes), ("rsag", col_axes)],
                    [dense_i, extra, prod_j.reshape(-1, 128)], sizes)
                prod_j = dense_j.reshape(-1, eig)
            else:
                dense_i, extra = exchange([("rsag", row_axes), ("sum", row_axes)], [dense_i, extra], sizes)
            prod_i = dense_i.reshape(-1, eig)
            extra = extra.reshape(-1, eig)
            if sweep == 0:
                degree_sum = extra[1, 0]
                inv_s = 1.0 / jnp.sqrt(degree_sum)
            aligned = extra[0] * inv_s
            defl_i = prod_i / root_i[:, None] - (root_i * inv_s)[:, None] * aligned[None, :]
            gram = lax.dot_general(defl_i, defl_i, (((0,), (0,)), ((), ())), precision=HIGH)
            (gram,) = exchange([("sum", col_axes)], [gram.reshape(-1, 128)], sizes)
            gram = gram.reshape(eig, eig)
            factor = jnp.linalg.cholesky(gram)
            if not last:
                defl_j = prod_j / root_j[:, None] - (root_j * inv_s)[:, None] * aligned[None, :]
                basis_i = jax.scipy.linalg.solve_triangular(factor, defl_i.T, lower=True).T * root_total
                basis_j = jax.scipy.linalg.solve_triangular(factor, defl_j.T, lower=True).T * root_total
            else:
                own = lax.dynamic_slice_in_dim(defl_i, me_i * shard, shard, 0)
                basis_own = jax.scipy.linalg.solve_triangular(factor, own.T, lower=True).T * root_total
        return basis_own, factor

    return local


def solution(mesh):
    sizes = dict(mesh.shape)
    SIZES.update(sizes)
    placed = (P(MESH_AXES, None), P(MESH_AXES, None))
    return jax.shard_map(
        make_local(sizes, ("row", "vec"), ("col",)),
        mesh=mesh,
        in_specs=placed,
        out_specs=(P(MESH_AXES, None), P()),
        check_vma=False,
    )
```

```python
import functools
import math

import jax
import jax.numpy as jnp
from jax import lax
from jax.experimental import pallas as pl
from jax.experimental.pallas import tpu as pltpu
from jax.sharding import PartitionSpec as P

ITERS = 2
MESH_AXES = ("row", "col", "vec")
MESH = pl.DeviceIdType.MESH
HIGH = lax.Precision.HIGHEST


def group_pos(digits):
    me = 0
    for a, div, mod in digits:
        me = me * mod + (lax.axis_index(a) // div) % mod
    return me


def group_size(digits):
    return math.prod(mod for _, _, mod in digits)


def member_coords(digits, m):
    own = {a: lax.axis_index(a) for a in MESH_AXES}
    coords = dict(own)
    rem = m
    for a, div, mod in reversed(digits):
        d = rem % mod
        rem = rem // mod
        coords[a] = coords[a] - ((own[a] // div) % mod) * div + d * div
    return tuple(coords[a] for a in MESH_AXES)


def flip(me, b):
    return me + (1 - 2 * ((me // (1 << b)) % 2)) * (1 << b)


def op_rounds(kind, g):
    bits = g.bit_length() - 1
    return 2 * bits if kind == "rsag" else bits


def exchange_kernel(ops, *refs):
    n = len(ops)
    ins, outs, scr = refs[:n], refs[n:2 * n], refs[2 * n:]
    barrier = pltpu.get_barrier_semaphore()
    groups = []
    for _, digits in ops:
        if digits not in groups:
            groups.append(digits)
    count = 0
    for digits in groups:
        g = group_size(digits)
        me = group_pos(digits)
        for b in range(g.bit_length() - 1):
            pl.semaphore_signal(barrier, inc=1, device_id=member_coords(digits, flip(me, b)), device_id_type=MESH)
            count += 1
    pl.semaphore_wait(barrier, count)

    state = []
    pos = 0
    for i, (kind, digits) in enumerate(ops):
        x_ref = ins[i]
        if kind == "rsag":
            w, r, gat, ssem, rsem = scr[pos:pos + 5]
            pos += 5
            r = (r, gat)
        else:
            w, r, ssem, rsem = scr[pos:pos + 4]
            pos += 4
        if kind == "gather":
            w[group_pos(digits)] = x_ref[...]
        else:
            w[...] = x_ref[...]
        state.append((w, r, ssem, rsem))

    nrounds = max(op_rounds(kind, group_size(d)) for kind, d in ops)
    for t in range(nrounds):
        copies = []
        for i, (kind, digits) in enumerate(ops):
            g = group_size(digits)
            bits = g.bit_length() - 1
            if t >= op_rounds(kind, g):
                continue
            me = group_pos(digits)
            w, r, ssem, rsem = state[i]
            if kind == "gather":
                b = t
                partner = flip(me, b)
                span = 1 << b
                mine = pl.ds((me // span) * span, span)
                theirs = pl.ds((partner // span) * span, span)
                src, dst, land = w.at[mine], w.at[mine], w.at[theirs]
            elif kind == "sum":
                b = t
                partner = flip(me, b)
                src, dst, land = w, r.at[t], r.at[t]
            elif t < bits:
                r = r[0]
                b = bits - 1 - t
                partner = flip(me, b)
                size = w.shape[0] >> (t + 1)
                theirs = pl.ds(pl.multiple_of((partner // (1 << b)) * size, size), size)
                src, dst, land = w.at[theirs], r.at[t, pl.ds(0, size)], r.at[t, pl.ds(0, size)]
            else:
                u = t - bits
                b = u
                partner = flip(me, b)
                gat = r[1]
                size = (w.shape[0] // g) << u
                if u == 0:
                    gat[pl.ds(pl.multiple_of(me * size, size), size)] = w[pl.ds(pl.multiple_of(me * size, size), size)]
                mine = pl.ds(pl.multiple_of((me // (1 << u)) * size, size), size)
                theirs = pl.ds(pl.multiple_of((partner // (1 << u)) * size, size), size)
                src, dst, land = gat.at[mine], gat.at[mine], gat.at[theirs]
            dev = member_coords(digits, partner)
            out = pltpu.make_async_remote_copy(
                src_ref=src, dst_ref=dst, send_sem=ssem.at[t], recv_sem=rsem.at[t],
                device_id=dev, device_id_type=MESH)
            out.start()
            back = pltpu.make_async_remote_copy(
                src_ref=src, dst_ref=land, send_sem=ssem.at[t], recv_sem=rsem.at[t],
                device_id=dev, device_id_type=MESH)
            copies.append((i, kind, t, bits, out, back, me))
        for i, kind, t, bits, out, back, me in copies:
            back.wait_recv()
            out.wait_send()
            w, r, ssem, rsem = state[i]
            if kind == "sum":
                w[...] = w[...] + r[t]
            elif kind == "rsag" and t < bits:
                b = bits - 1 - t
                size = w.shape[0] >> (t + 1)
                mine = pl.ds(pl.multiple_of((me // (1 << b)) * size, size), size)
                w[mine] = w[mine] + r[0][t, pl.ds(0, size)]
    for i, (kind, _) in enumerate(ops):
        outs[i][...] = state[i][1][1][...] if kind == "rsag" else state[i][0][...]


_IDS = {}


def exchange(ops, xs):
    key = tuple((k, d, x.shape, str(x.dtype)) for (k, d), x in zip(ops, xs))
    if key not in _IDS:
        _IDS[key] = len(_IDS)
    out_shapes, scratch = [], []
    for (kind, digits), x in zip(ops, xs):
        g = group_size(digits)
        L = op_rounds(kind, g)
        if kind == "gather":
            out_shapes.append(jax.ShapeDtypeStruct((g,) + x.shape, x.dtype))
            scratch += [pltpu.VMEM((g,) + x.shape, x.dtype), pltpu.VMEM((8, 128), jnp.float32)]
        elif kind == "sum":
            out_shapes.append(jax.ShapeDtypeStruct(x.shape, x.dtype))
            scratch += [pltpu.VMEM(x.shape, x.dtype), pltpu.VMEM((L,) + x.shape, x.dtype)]
        else:
            out_shapes.append(jax.ShapeDtypeStruct(x.shape, x.dtype))
            scratch += [pltpu.VMEM(x.shape, x.dtype),
                        pltpu.VMEM((L // 2, x.shape[0] // 2) + x.shape[1:], x.dtype),
                        pltpu.VMEM(x.shape, x.dtype)]
        scratch += [pltpu.SemaphoreType.DMA((L,)), pltpu.SemaphoreType.DMA((L,))]
    outs = pl.pallas_call(
        functools.partial(exchange_kernel, ops),
        out_shape=out_shapes,
        in_specs=[pl.BlockSpec(memory_space=pltpu.VMEM)] * len(xs),
        out_specs=[pl.BlockSpec(memory_space=pltpu.VMEM)] * len(xs),
        scratch_shapes=scratch,
        compiler_params=pltpu.CompilerParams(collective_id=_IDS[key], has_side_effects=True),
    )(*xs)
    return list(outs)


def make_local(sizes, row_axes, col_axes):
    def local(particles, start_basis):
        shard = particles.shape[0]
        width = particles.shape[1]
        eig = start_basis.shape[1]
        total = shard * math.prod(sizes.values())
        spread = 2.0 * width
        root_total = math.sqrt(float(total))

        dense_basis = start_basis.reshape(shard * eig // 128, 128)
        i_feats, i_basis, j_feats, j_basis = exchange(
            [("gather", row_axes), ("gather", row_axes), ("gather", col_axes), ("gather", col_axes)],
            [particles, dense_basis, particles, dense_basis])
        gi = group_size(row_axes)
        gj = group_size(col_axes)
        i_feats = i_feats.reshape(gi * shard, width)
        j_feats = j_feats.reshape(gj * shard, width)
        basis_i = i_basis.reshape(gi * shard, eig)
        basis_j = j_basis.reshape(gj * shard, eig)

        def block_ids(digits):
            coords = member_coords(digits, jnp.arange(group_size(digits), dtype=jnp.int32))
            flat = jnp.zeros((group_size(digits),), jnp.int32)
            for a, cval in zip(MESH_AXES, coords):
                flat = flat * sizes[a] + cval
            return (flat[:, None] * shard + jnp.arange(shard, dtype=jnp.int32)[None, :]).reshape(-1)

        ids_i = block_ids(row_axes)
        ids_j = block_ids(col_axes)
        sq_i = jnp.sum(jnp.square(i_feats.astype(jnp.float32)), axis=1)
        sq_j = jnp.sum(jnp.square(j_feats.astype(jnp.float32)), axis=1)
        dots = lax.dot_general(i_feats, j_feats, (((1,), (1,)), ((), ())), preferred_element_type=jnp.float32)
        distance = sq_i[:, None] + sq_j[None, :] - 2.0 * dots
        tile = jnp.where(ids_i[:, None] == ids_j[None, :], jnp.float32(0.0), jnp.exp(-distance / spread))

        deg_i, deg_j = exchange(
            [("sum", row_axes), ("sum", col_axes)],
            [jnp.sum(tile, axis=1).reshape(-1, 128), jnp.sum(tile, axis=0).reshape(-1, 128)])
        deg_i = deg_i.reshape(-1)
        deg_j = deg_j.reshape(-1)
        root_i = jnp.sqrt(deg_i)
        root_j = jnp.sqrt(deg_j)
        me_i = group_pos(row_axes)
        factor = None
        for sweep in range(ITERS):
            last = sweep == ITERS - 1
            scaled_i = basis_i / root_i[:, None]
            scaled_j = basis_j / root_j[:, None]
            prod_i = jnp.dot(tile, scaled_j, precision=HIGH)
            extra = jnp.dot(root_j, basis_j, precision=HIGH)[None, :]
            if sweep == 0:
                extra = jnp.concatenate([extra, jnp.broadcast_to(jnp.sum(deg_j), (1, eig))], axis=0)
            else:
                extra = jnp.concatenate([extra, jnp.zeros((1, eig), jnp.float32)], axis=0)
            extra = jnp.concatenate([extra, jnp.zeros((6, eig), jnp.float32)], axis=0).reshape(-1, 128)
            dense_i = prod_i.reshape(-1, 128)
            if not last:
                prod_j = lax.dot_general(tile, scaled_i, (((0,), (0,)), ((), ())), precision=HIGH)
                dense_i, extra, dense_j = exchange(
                    [("rsag", row_axes), ("sum", row_axes), ("rsag", col_axes)],
                    [dense_i, extra, prod_j.reshape(-1, 128)])
                prod_j = dense_j.reshape(-1, eig)
            else:
                dense_i, extra = exchange([("rsag", row_axes), ("sum", row_axes)], [dense_i, extra])
            prod_i = dense_i.reshape(-1, eig)
            extra = extra.reshape(-1, eig)
            if sweep == 0:
                degree_sum = extra[1, 0]
                inv_s = 1.0 / jnp.sqrt(degree_sum)
            aligned = extra[0] * inv_s
            defl_i = prod_i / root_i[:, None] - (root_i * inv_s)[:, None] * aligned[None, :]
            gram = lax.dot_general(defl_i, defl_i, (((0,), (0,)), ((), ())), precision=HIGH)
            (gram,) = exchange([("sum", col_axes)], [gram.reshape(-1, 128)])
            gram = gram.reshape(eig, eig)
            factor = jnp.linalg.cholesky(gram)
            if not last:
                defl_j = prod_j / root_j[:, None] - (root_j * inv_s)[:, None] * aligned[None, :]
                basis_i = jax.scipy.linalg.solve_triangular(factor, defl_i.T, lower=True).T * root_total
                basis_j = jax.scipy.linalg.solve_triangular(factor, defl_j.T, lower=True).T * root_total
            else:
                own = lax.dynamic_slice_in_dim(defl_i, me_i * shard, shard, 0)
                basis_own = jax.scipy.linalg.solve_triangular(factor, own.T, lower=True).T * root_total
        return basis_own, factor

    return local


def solution(mesh):
    sizes = dict(mesh.shape)
    placed = (P(MESH_AXES, None), P(MESH_AXES, None))
    return jax.shard_map(
        make_local(sizes, (("row", 1, 2), ("row", 2, sizes["row"] // 2), ("vec", 1, sizes["vec"])), (("col", 1, sizes["col"]),)),
        mesh=mesh,
        in_specs=placed,
        out_specs=(P(MESH_AXES, None), P()),
        check_vma=False,
    )
```

```python
import functools
import math

import jax
import jax.numpy as jnp
from jax import lax
from jax.experimental import pallas as pl
from jax.experimental.pallas import tpu as pltpu
from jax.sharding import PartitionSpec as P

ITERS = 2
MESH_AXES = ("row", "col", "vec")
MESH = pl.DeviceIdType.MESH
HIGH = lax.Precision.HIGHEST


def group_pos(digits):
    me = 0
    for a, div, mod in digits:
        me = me * mod + (lax.axis_index(a) // div) % mod
    return me


def group_size(digits):
    return math.prod(mod for _, _, mod in digits)


def member_coords(digits, m):
    own = {a: lax.axis_index(a) for a in MESH_AXES}
    coords = dict(own)
    rem = m
    for a, div, mod in reversed(digits):
        d = rem % mod
        rem = rem // mod
        coords[a] = coords[a] - ((own[a] // div) % mod) * div + d * div
    return tuple(coords[a] for a in MESH_AXES)


def flip(me, b):
    return me + (1 - 2 * ((me // (1 << b)) % 2)) * (1 << b)


def op_rounds(kind, g):
    bits = g.bit_length() - 1
    return 2 * bits if kind == "rsag" else bits


def exchange_kernel(ops, *refs):
    n = len(ops)
    ins, outs, scr = refs[:n], refs[n:2 * n], refs[2 * n:]
    barrier = pltpu.get_barrier_semaphore()
    groups = []
    for _, digits in ops:
        if digits not in groups:
            groups.append(digits)
    count = 0
    for digits in groups:
        g = group_size(digits)
        me = group_pos(digits)
        for b in range(g.bit_length() - 1):
            pl.semaphore_signal(barrier, inc=1, device_id=member_coords(digits, flip(me, b)), device_id_type=MESH)
            count += 1
    pl.semaphore_wait(barrier, count)

    state = []
    pos = 0
    for i, (kind, digits) in enumerate(ops):
        x_ref = ins[i]
        if kind == "rsag":
            w, r, gat, ssem, rsem = scr[pos:pos + 5]
            pos += 5
            r = (r, gat)
        else:
            w, r, ssem, rsem = scr[pos:pos + 4]
            pos += 4
        if kind == "gather":
            w[group_pos(digits)] = x_ref[...]
        else:
            w[...] = x_ref[...]
        state.append((w, r, ssem, rsem))

    nrounds = max(op_rounds(kind, group_size(d)) for kind, d in ops)
    for t in range(nrounds):
        copies = []
        for i, (kind, digits) in enumerate(ops):
            g = group_size(digits)
            bits = g.bit_length() - 1
            if t >= op_rounds(kind, g):
                continue
            me = group_pos(digits)
            w, r, ssem, rsem = state[i]
            if kind == "gather":
                b = t
                partner = flip(me, b)
                span = 1 << b
                mine = pl.ds((me // span) * span, span)
                theirs = pl.ds((partner // span) * span, span)
                src, dst, land = w.at[mine], w.at[mine], w.at[theirs]
            elif kind == "sum":
                b = t
                partner = flip(me, b)
                src, dst, land = w, r.at[t], r.at[t]
            elif t < bits:
                r = r[0]
                b = bits - 1 - t
                partner = flip(me, b)
                size = w.shape[0] >> (t + 1)
                theirs = pl.ds(pl.multiple_of((partner // (1 << b)) * size, size), size)
                src, dst, land = w.at[theirs], r.at[t, pl.ds(0, size)], r.at[t, pl.ds(0, size)]
            else:
                u = t - bits
                b = u
                partner = flip(me, b)
                gat = r[1]
                size = (w.shape[0] // g) << u
                if u == 0:
                    gat[pl.ds(pl.multiple_of(me * size, size), size)] = w[pl.ds(pl.multiple_of(me * size, size), size)]
                mine = pl.ds(pl.multiple_of((me // (1 << u)) * size, size), size)
                theirs = pl.ds(pl.multiple_of((partner // (1 << u)) * size, size), size)
                src, dst, land = gat.at[mine], gat.at[mine], gat.at[theirs]
            dev = member_coords(digits, partner)
            out = pltpu.make_async_remote_copy(
                src_ref=src, dst_ref=dst, send_sem=ssem.at[t], recv_sem=rsem.at[t],
                device_id=dev, device_id_type=MESH)
            out.start()
            back = pltpu.make_async_remote_copy(
                src_ref=src, dst_ref=land, send_sem=ssem.at[t], recv_sem=rsem.at[t],
                device_id=dev, device_id_type=MESH)
            copies.append((i, kind, t, bits, out, back, me))
        for i, kind, t, bits, out, back, me in copies:
            back.wait_recv()
            out.wait_send()
            w, r, ssem, rsem = state[i]
            if kind == "sum":
                w[...] = w[...] + r[t]
            elif kind == "rsag" and t < bits:
                b = bits - 1 - t
                size = w.shape[0] >> (t + 1)
                mine = pl.ds(pl.multiple_of((me // (1 << b)) * size, size), size)
                w[mine] = w[mine] + r[0][t, pl.ds(0, size)]
    for i, (kind, _) in enumerate(ops):
        outs[i][...] = state[i][1][1][...] if kind == "rsag" else state[i][0][...]


def direct_kernel(ops, groups, *refs):
    n = len(ops)
    ins, outs, scr = refs[:n], refs[n:2 * n], refs[2 * n:]
    barrier = pltpu.get_barrier_semaphore()
    total_peers = 0
    for axes in groups:
        g = group_size(axes)
        me = group_pos(axes)
        total_peers += g - 1

        def greet(k, c, axes=axes, g=g, me=me):
            pl.semaphore_signal(barrier, inc=1, device_id=member_coords(axes, (me + k) % g), device_id_type=MESH)
            return c

        lax.fori_loop(1, g, greet, 0)
    pl.semaphore_wait(barrier, total_peers)

    pos = 0
    pending = []
    for i, (kind, axes) in enumerate(ops):
        g = group_size(axes)
        me = group_pos(axes)
        x_ref, o_ref = ins[i], outs[i]
        if kind in ("gather", "sum"):
            slots, ssem, rsem = scr[pos:pos + 3]
            pos += 3
            slots[me] = x_ref[...]

            def send(k, c, x_ref=x_ref, slots=slots, ssem=ssem, rsem=rsem, axes=axes, g=g, me=me):
                peer = (me + k) % g
                pltpu.make_async_remote_copy(
                    src_ref=x_ref, dst_ref=slots.at[me], send_sem=ssem.at[peer], recv_sem=rsem.at[me],
                    device_id=member_coords(axes, peer), device_id_type=MESH).start()
                return c

            lax.fori_loop(1, g, send, 0)
            pending.append((kind, axes, g, me, x_ref, o_ref, slots, ssem, rsem))
        else:
            rs, ag, ssem, rsem, ssem2, rsem2 = scr[pos:pos + 6]
            pos += 6
            c = x_ref.shape[0] // g
            rs[me] = x_ref[pl.ds(pl.multiple_of(me * c, c), c)]

            def send(k, cc, x_ref=x_ref, rs=rs, ssem=ssem, rsem=rsem, axes=axes, g=g, me=me, c=c):
                peer = (me + k) % g
                pltpu.make_async_remote_copy(
                    src_ref=x_ref.at[pl.ds(pl.multiple_of(peer * c, c), c)], dst_ref=rs.at[me],
                    send_sem=ssem.at[peer], recv_sem=rsem.at[me],
                    device_id=member_coords(axes, peer), device_id_type=MESH).start()
                return cc

            lax.fori_loop(1, g, send, 0)
            pending.append((kind, axes, g, me, x_ref, o_ref, (rs, ag, ssem2, rsem2), ssem, rsem))

    for kind, axes, g, me, x_ref, o_ref, slots, ssem, rsem in pending:
        if kind == "rsag":
            rs, ag, ssem2, rsem2 = slots
            c = rs.shape[1]
        else:
            rs = slots

        def wait(k, cc, x_ref=x_ref, rs=rs, ssem=ssem, rsem=rsem, axes=axes, g=g, me=me, kind=kind):
            src = (me + g - k) % g
            peer = (me + k) % g
            if kind == "rsag":
                c = rs.shape[1]
                src_ref = x_ref.at[pl.ds(0, c)]
            else:
                src_ref = x_ref
            pltpu.make_async_remote_copy(
                src_ref=src_ref, dst_ref=rs.at[src], send_sem=ssem.at[peer], recv_sem=rsem.at[src],
                device_id=member_coords(axes, peer), device_id_type=MESH).wait_recv()
            pltpu.make_async_remote_copy(
                src_ref=src_ref, dst_ref=rs.at[me], send_sem=ssem.at[peer], recv_sem=rsem.at[me],
                device_id=member_coords(axes, peer), device_id_type=MESH).wait_send()
            return cc

        lax.fori_loop(1, g, wait, 0)
        if kind == "gather":
            o_ref[...] = rs[...]
        elif kind == "sum":
            acc = rs[0]
            for s in range(1, g):
                acc = acc + rs[s]
            o_ref[...] = acc
        else:
            acc = rs[0]
            for s in range(1, g):
                acc = acc + rs[s]
            ag[me] = acc

            def send2(k, cc, ag=ag, ssem2=ssem2, rsem2=rsem2, axes=axes, g=g, me=me):
                peer = (me + k) % g
                pltpu.make_async_remote_copy(
                    src_ref=ag.at[me], dst_ref=ag.at[me], send_sem=ssem2.at[peer], recv_sem=rsem2.at[me],
                    device_id=member_coords(axes, peer), device_id_type=MESH).start()
                return cc

            lax.fori_loop(1, g, send2, 0)

            def wait2(k, cc, ag=ag, ssem2=ssem2, rsem2=rsem2, axes=axes, g=g, me=me):
                src = (me + g - k) % g
                peer = (me + k) % g
                pltpu.make_async_remote_copy(
                    src_ref=ag.at[me], dst_ref=ag.at[src], send_sem=ssem2.at[peer], recv_sem=rsem2.at[src],
                    device_id=member_coords(axes, peer), device_id_type=MESH).wait_recv()
                pltpu.make_async_remote_copy(
                    src_ref=ag.at[me], dst_ref=ag.at[me], send_sem=ssem2.at[peer], recv_sem=rsem2.at[me],
                    device_id=member_coords(axes, peer), device_id_type=MESH).wait_send()
                return cc

            lax.fori_loop(1, g, wait2, 0)
            o_ref[...] = ag[...]


_IDS = {}


def exchange(ops, xs):
    key = ("direct",) + tuple((k, d, x.shape, str(x.dtype)) for (k, d), x in zip(ops, xs))
    if key not in _IDS:
        _IDS[key] = len(_IDS)
    groups = []
    for _, axes in ops:
        if axes not in groups:
            groups.append(axes)
    out_shapes, scratch = [], []
    for (kind, axes), x in zip(ops, xs):
        g = group_size(axes)
        if kind == "sum":
            out_shapes.append(jax.ShapeDtypeStruct(x.shape, x.dtype))
            scratch += [pltpu.VMEM((g,) + x.shape, x.dtype), pltpu.SemaphoreType.DMA((g,)),
                        pltpu.SemaphoreType.DMA((g,))]
        else:
            c = x.shape[0] // g
            out_shapes.append(jax.ShapeDtypeStruct((g, c) + x.shape[1:], x.dtype))
            scratch += [pltpu.VMEM((g, c) + x.shape[1:], x.dtype), pltpu.VMEM((g, c) + x.shape[1:], x.dtype),
                        pltpu.SemaphoreType.DMA((g,)), pltpu.SemaphoreType.DMA((g,)),
                        pltpu.SemaphoreType.DMA((g,)), pltpu.SemaphoreType.DMA((g,))]
    outs = pl.pallas_call(
        functools.partial(direct_kernel, ops, groups),
        out_shape=out_shapes,
        in_specs=[pl.BlockSpec(memory_space=pltpu.VMEM)] * len(xs),
        out_specs=[pl.BlockSpec(memory_space=pltpu.VMEM)] * len(xs),
        scratch_shapes=scratch,
        compiler_params=pltpu.CompilerParams(collective_id=_IDS[key], has_side_effects=True),
    )(*xs)
    return [o.reshape(x.shape) for o, x in zip(outs, xs)]


def exchange_bfly(ops, xs):
    key = ("bfly",) + tuple((k, d, x.shape, str(x.dtype)) for (k, d), x in zip(ops, xs))
    if key not in _IDS:
        _IDS[key] = len(_IDS)
    out_shapes, scratch = [], []
    for (kind, digits), x in zip(ops, xs):
        g = group_size(digits)
        L = op_rounds(kind, g)
        if kind == "gather":
            out_shapes.append(jax.ShapeDtypeStruct((g,) + x.shape, x.dtype))
            scratch += [pltpu.VMEM((g,) + x.shape, x.dtype), pltpu.VMEM((8, 128), jnp.float32)]
        elif kind == "sum":
            out_shapes.append(jax.ShapeDtypeStruct(x.shape, x.dtype))
            scratch += [pltpu.VMEM(x.shape, x.dtype), pltpu.VMEM((L,) + x.shape, x.dtype)]
        else:
            out_shapes.append(jax.ShapeDtypeStruct(x.shape, x.dtype))
            scratch += [pltpu.VMEM(x.shape, x.dtype),
                        pltpu.VMEM((L // 2, x.shape[0] // 2) + x.shape[1:], x.dtype),
                        pltpu.VMEM(x.shape, x.dtype)]
        scratch += [pltpu.SemaphoreType.DMA((L,)), pltpu.SemaphoreType.DMA((L,))]
    outs = pl.pallas_call(
        functools.partial(exchange_kernel, ops),
        out_shape=out_shapes,
        in_specs=[pl.BlockSpec(memory_space=pltpu.VMEM)] * len(xs),
        out_specs=[pl.BlockSpec(memory_space=pltpu.VMEM)] * len(xs),
        scratch_shapes=scratch,
        compiler_params=pltpu.CompilerParams(collective_id=_IDS[key], has_side_effects=True),
    )(*xs)
    return list(outs)


def make_local(sizes, row_axes, col_axes):
    def local(particles, start_basis):
        shard = particles.shape[0]
        width = particles.shape[1]
        eig = start_basis.shape[1]
        total = shard * math.prod(sizes.values())
        spread = 2.0 * width
        root_total = math.sqrt(float(total))

        dense_basis = start_basis.reshape(shard * eig // 128, 128)
        i_feats, i_basis, j_feats, j_basis = exchange_bfly(
            [("gather", row_axes), ("gather", row_axes), ("gather", col_axes), ("gather", col_axes)],
            [particles, dense_basis, particles, dense_basis])
        gi = group_size(row_axes)
        gj = group_size(col_axes)
        i_feats = i_feats.reshape(gi * shard, width)
        j_feats = j_feats.reshape(gj * shard, width)
        basis_i = i_basis.reshape(gi * shard, eig)
        basis_j = j_basis.reshape(gj * shard, eig)

        def block_ids(digits):
            coords = member_coords(digits, jnp.arange(group_size(digits), dtype=jnp.int32))
            flat = jnp.zeros((group_size(digits),), jnp.int32)
            for a, cval in zip(MESH_AXES, coords):
                flat = flat * sizes[a] + cval
            return (flat[:, None] * shard + jnp.arange(shard, dtype=jnp.int32)[None, :]).reshape(-1)

        ids_i = block_ids(row_axes)
        ids_j = block_ids(col_axes)
        sq_i = jnp.sum(jnp.square(i_feats.astype(jnp.float32)), axis=1)
        sq_j = jnp.sum(jnp.square(j_feats.astype(jnp.float32)), axis=1)
        dots = lax.dot_general(i_feats, j_feats, (((1,), (1,)), ((), ())), preferred_element_type=jnp.float32)
        distance = sq_i[:, None] + sq_j[None, :] - 2.0 * dots
        tile = jnp.where(ids_i[:, None] == ids_j[None, :], jnp.float32(0.0), jnp.exp(-distance / spread))

        deg_i, deg_j = exchange(
            [("sum", row_axes), ("sum", col_axes)],
            [jnp.sum(tile, axis=1).reshape(-1, 128), jnp.sum(tile, axis=0).reshape(-1, 128)])
        deg_i = deg_i.reshape(-1)
        deg_j = deg_j.reshape(-1)
        root_i = jnp.sqrt(deg_i)
        root_j = jnp.sqrt(deg_j)
        me_i = group_pos(row_axes)
        scaled_i = basis_i / root_i[:, None]
        scaled_j = basis_j / root_j[:, None]
        prod_i = jnp.dot(tile, scaled_j, precision=HIGH)
        prod_j = lax.dot_general(tile, scaled_i, (((0,), (0,)), ((), ())), precision=HIGH)
        extra = jnp.concatenate([jnp.dot(root_j, basis_j, precision=HIGH)[None, :],
                                 jnp.broadcast_to(jnp.sum(deg_j), (1, eig)),
                                 jnp.zeros((6, eig), jnp.float32)], axis=0)
        dense_i, extra, dense_j = exchange(
            [("rsag", row_axes), ("sum", row_axes), ("rsag", col_axes)],
            [prod_i.reshape(-1, 128), extra.reshape(-1, 128), prod_j.reshape(-1, 128)])
        prod_i = dense_i.reshape(-1, eig)
        prod_j = dense_j.reshape(-1, eig)
        extra = extra.reshape(-1, eig)
        inv_s = 1.0 / jnp.sqrt(extra[1, 0])
        aligned = extra[0] * inv_s
        defl_i = prod_i / root_i[:, None] - (root_i * inv_s)[:, None] * aligned[None, :]
        defl_j = prod_j / root_j[:, None] - (root_j * inv_s)[:, None] * aligned[None, :]
        factor = None
        for sweep in range(ITERS):
            last = sweep == ITERS - 1
            need_j = sweep + 2 < ITERS
            gram = lax.dot_general(defl_i, defl_i, (((0,), (0,)), ((), ())), precision=HIGH).reshape(-1, 128)
            if last:
                (gram,) = exchange([("sum", col_axes)], [gram])
            else:
                q_i = jnp.dot(tile, defl_j / root_j[:, None], precision=HIGH)
                part = jnp.concatenate([jnp.dot(root_j, defl_j, precision=HIGH)[None, :],
                                        jnp.zeros((7, eig), jnp.float32)], axis=0)
                ops = [("sum", col_axes), ("rsag", row_axes), ("sum", row_axes)]
                xs = [gram, q_i.reshape(-1, 128), part.reshape(-1, 128)]
                if need_j:
                    q_j = lax.dot_general(tile, defl_i / root_i[:, None], (((0,), (0,)), ((), ())), precision=HIGH)
                    ops.append(("rsag", col_axes))
                    xs.append(q_j.reshape(-1, 128))
                res = exchange(ops, xs)
                gram, q_i, part = res[0], res[1].reshape(-1, eig), res[2].reshape(-1, eig)
            factor = jnp.linalg.cholesky(gram.reshape(eig, eig))
            if last:
                own = lax.dynamic_slice_in_dim(defl_i, me_i * shard, shard, 0)
                basis_own = jax.scipy.linalg.solve_triangular(factor, own.T, lower=True).T * root_total
                break
            prod_i = jax.scipy.linalg.solve_triangular(factor, q_i.T, lower=True).T * root_total
            aligned = jax.scipy.linalg.solve_triangular(factor, part[0], lower=True) * (root_total * inv_s)
            defl_i = prod_i / root_i[:, None] - (root_i * inv_s)[:, None] * aligned[None, :]
            if need_j:
                prod_j = jax.scipy.linalg.solve_triangular(factor, res[3].reshape(-1, eig).T, lower=True).T * root_total
                defl_j = prod_j / root_j[:, None] - (root_j * inv_s)[:, None] * aligned[None, :]
        return basis_own, factor

    return local


def solution(mesh):
    sizes = dict(mesh.shape)
    placed = (P(MESH_AXES, None), P(MESH_AXES, None))
    return jax.shard_map(
        make_local(sizes, (("row", 1, 2), ("row", 2, sizes["row"] // 2), ("vec", 1, sizes["vec"])), (("col", 1, sizes["col"]),)),
        mesh=mesh,
        in_specs=placed,
        out_specs=(P(MESH_AXES, None), P()),
        check_vma=False,
    )
```

```python
import functools
import math

import jax
import jax.numpy as jnp
from jax import lax
from jax.experimental import pallas as pl
from jax.experimental.pallas import tpu as pltpu
from jax.sharding import PartitionSpec as P

ITERS = 2
MESH_AXES = ("row", "col", "vec")
MESH = pl.DeviceIdType.MESH
HIGH = lax.Precision.HIGHEST


def group_pos(digits):
    me = 0
    for a, div, mod in digits:
        me = me * mod + (lax.axis_index(a) // div) % mod
    return me


def group_size(digits):
    return math.prod(mod for _, _, mod in digits)


def member_coords(digits, m):
    own = {a: lax.axis_index(a) for a in MESH_AXES}
    coords = dict(own)
    rem = m
    for a, div, mod in reversed(digits):
        d = rem % mod
        rem = rem // mod
        coords[a] = coords[a] - ((own[a] // div) % mod) * div + d * div
    return tuple(coords[a] for a in MESH_AXES)


def flip(me, b):
    return me + (1 - 2 * ((me // (1 << b)) % 2)) * (1 << b)


def op_rounds(kind, g):
    bits = g.bit_length() - 1
    return 2 * bits if kind == "rsag" else bits


def exchange_kernel(ops, *refs):
    n = len(ops)
    ins, outs, scr = refs[:n], refs[n:2 * n], refs[2 * n:]
    barrier = pltpu.get_barrier_semaphore()
    groups = []
    for _, digits in ops:
        if digits not in groups:
            groups.append(digits)
    count = 0
    for digits in groups:
        g = group_size(digits)
        me = group_pos(digits)
        for b in range(g.bit_length() - 1):
            pl.semaphore_signal(barrier, inc=1, device_id=member_coords(digits, flip(me, b)), device_id_type=MESH)
            count += 1
    pl.semaphore_wait(barrier, count)

    state = []
    pos = 0
    for i, (kind, digits) in enumerate(ops):
        x_ref = ins[i]
        if kind == "rsag":
            w, r, gat, ssem, rsem = scr[pos:pos + 5]
            pos += 5
            r = (r, gat)
        else:
            w, r, ssem, rsem = scr[pos:pos + 4]
            pos += 4
        if kind == "gather":
            w[group_pos(digits)] = x_ref[...]
        else:
            w[...] = x_ref[...]
        state.append((w, r, ssem, rsem))

    nrounds = max(op_rounds(kind, group_size(d)) for kind, d in ops)
    for t in range(nrounds):
        copies = []
        for i, (kind, digits) in enumerate(ops):
            g = group_size(digits)
            bits = g.bit_length() - 1
            if t >= op_rounds(kind, g):
                continue
            me = group_pos(digits)
            w, r, ssem, rsem = state[i]
            if kind == "gather":
                b = t
                partner = flip(me, b)
                span = 1 << b
                mine = pl.ds((me // span) * span, span)
                theirs = pl.ds((partner // span) * span, span)
                src, dst, land = w.at[mine], w.at[mine], w.at[theirs]
            elif kind == "sum":
                b = t
                partner = flip(me, b)
                src, dst, land = w, r.at[t], r.at[t]
            elif t < bits:
                r = r[0]
                b = bits - 1 - t
                partner = flip(me, b)
                size = w.shape[0] >> (t + 1)
                theirs = pl.ds(pl.multiple_of((partner // (1 << b)) * size, size), size)
                src, dst, land = w.at[theirs], r.at[t, pl.ds(0, size)], r.at[t, pl.ds(0, size)]
            else:
                u = t - bits
                b = u
                partner = flip(me, b)
                gat = r[1]
                size = (w.shape[0] // g) << u
                if u == 0:
                    gat[pl.ds(pl.multiple_of(me * size, size), size)] = w[pl.ds(pl.multiple_of(me * size, size), size)]
                mine = pl.ds(pl.multiple_of((me // (1 << u)) * size, size), size)
                theirs = pl.ds(pl.multiple_of((partner // (1 << u)) * size, size), size)
                src, dst, land = gat.at[mine], gat.at[mine], gat.at[theirs]
            dev = member_coords(digits, partner)
            out = pltpu.make_async_remote_copy(
                src_ref=src, dst_ref=dst, send_sem=ssem.at[t], recv_sem=rsem.at[t],
                device_id=dev, device_id_type=MESH)
            out.start()
            back = pltpu.make_async_remote_copy(
                src_ref=src, dst_ref=land, send_sem=ssem.at[t], recv_sem=rsem.at[t],
                device_id=dev, device_id_type=MESH)
            copies.append((i, kind, t, bits, out, back, me))
        for i, kind, t, bits, out, back, me in copies:
            back.wait_recv()
            out.wait_send()
            w, r, ssem, rsem = state[i]
            if kind == "sum":
                w[...] = w[...] + r[t]
            elif kind == "rsag" and t < bits:
                b = bits - 1 - t
                size = w.shape[0] >> (t + 1)
                mine = pl.ds(pl.multiple_of((me // (1 << b)) * size, size), size)
                w[mine] = w[mine] + r[0][t, pl.ds(0, size)]
    for i, (kind, _) in enumerate(ops):
        outs[i][...] = state[i][1][1][...] if kind == "rsag" else state[i][0][...]


def direct_kernel(ops, groups, *refs):
    n = len(ops)
    ins, outs, scr = refs[:n], refs[n:2 * n], refs[2 * n:]
    barrier = pltpu.get_barrier_semaphore()
    total_peers = 0
    for axes in groups:
        g = group_size(axes)
        me = group_pos(axes)
        total_peers += g - 1

        def greet(k, c, axes=axes, g=g, me=me):
            pl.semaphore_signal(barrier, inc=1, device_id=member_coords(axes, (me + k) % g), device_id_type=MESH)
            return c

        lax.fori_loop(1, g, greet, 0)
    pl.semaphore_wait(barrier, total_peers)

    pos = 0
    pending = []
    for i, (kind, axes) in enumerate(ops):
        g = group_size(axes)
        me = group_pos(axes)
        x_ref, o_ref = ins[i], outs[i]
        if kind in ("gather", "sum"):
            slots, ssem, rsem = scr[pos:pos + 3]
            pos += 3
            slots[me] = x_ref[...]

            def send(k, c, x_ref=x_ref, slots=slots, ssem=ssem, rsem=rsem, axes=axes, g=g, me=me):
                peer = (me + k) % g
                pltpu.make_async_remote_copy(
                    src_ref=x_ref, dst_ref=slots.at[me], send_sem=ssem.at[peer], recv_sem=rsem.at[me],
                    device_id=member_coords(axes, peer), device_id_type=MESH).start()
                return c

            lax.fori_loop(1, g, send, 0)
            pending.append((kind, axes, g, me, x_ref, o_ref, slots, ssem, rsem))
        else:
            rs, ag, ssem, rsem, ssem2, rsem2 = scr[pos:pos + 6]
            pos += 6
            c = x_ref.shape[0] // g
            rs[me] = x_ref[pl.ds(pl.multiple_of(me * c, c), c)]

            def send(k, cc, x_ref=x_ref, rs=rs, ssem=ssem, rsem=rsem, axes=axes, g=g, me=me, c=c):
                peer = (me + k) % g
                pltpu.make_async_remote_copy(
                    src_ref=x_ref.at[pl.ds(pl.multiple_of(peer * c, c), c)], dst_ref=rs.at[me],
                    send_sem=ssem.at[peer], recv_sem=rsem.at[me],
                    device_id=member_coords(axes, peer), device_id_type=MESH).start()
                return cc

            lax.fori_loop(1, g, send, 0)
            pending.append((kind, axes, g, me, x_ref, o_ref, (rs, ag, ssem2, rsem2), ssem, rsem))

    for kind, axes, g, me, x_ref, o_ref, slots, ssem, rsem in pending:
        if kind == "rsag":
            rs, ag, ssem2, rsem2 = slots
            c = rs.shape[1]
        else:
            rs = slots

        def wait(k, cc, x_ref=x_ref, rs=rs, ssem=ssem, rsem=rsem, axes=axes, g=g, me=me, kind=kind):
            src = (me + g - k) % g
            peer = (me + k) % g
            if kind == "rsag":
                c = rs.shape[1]
                src_ref = x_ref.at[pl.ds(0, c)]
            else:
                src_ref = x_ref
            pltpu.make_async_remote_copy(
                src_ref=src_ref, dst_ref=rs.at[src], send_sem=ssem.at[peer], recv_sem=rsem.at[src],
                device_id=member_coords(axes, peer), device_id_type=MESH).wait_recv()
            pltpu.make_async_remote_copy(
                src_ref=src_ref, dst_ref=rs.at[me], send_sem=ssem.at[peer], recv_sem=rsem.at[me],
                device_id=member_coords(axes, peer), device_id_type=MESH).wait_send()
            return cc

        lax.fori_loop(1, g, wait, 0)
        if kind == "gather":
            o_ref[...] = rs[...]
        elif kind == "sum":
            acc = rs[0]
            for s in range(1, g):
                acc = acc + rs[s]
            o_ref[...] = acc
        else:
            acc = rs[0]
            for s in range(1, g):
                acc = acc + rs[s]
            ag[me] = acc

            def send2(k, cc, ag=ag, ssem2=ssem2, rsem2=rsem2, axes=axes, g=g, me=me):
                peer = (me + k) % g
                pltpu.make_async_remote_copy(
                    src_ref=ag.at[me], dst_ref=ag.at[me], send_sem=ssem2.at[peer], recv_sem=rsem2.at[me],
                    device_id=member_coords(axes, peer), device_id_type=MESH).start()
                return cc

            lax.fori_loop(1, g, send2, 0)

            def wait2(k, cc, ag=ag, ssem2=ssem2, rsem2=rsem2, axes=axes, g=g, me=me):
                src = (me + g - k) % g
                peer = (me + k) % g
                pltpu.make_async_remote_copy(
                    src_ref=ag.at[me], dst_ref=ag.at[src], send_sem=ssem2.at[peer], recv_sem=rsem2.at[src],
                    device_id=member_coords(axes, peer), device_id_type=MESH).wait_recv()
                pltpu.make_async_remote_copy(
                    src_ref=ag.at[me], dst_ref=ag.at[me], send_sem=ssem2.at[peer], recv_sem=rsem2.at[me],
                    device_id=member_coords(axes, peer), device_id_type=MESH).wait_send()
                return cc

            lax.fori_loop(1, g, wait2, 0)
            o_ref[...] = ag[...]


_IDS = {}


def exchange(ops, xs):
    key = ("direct",) + tuple((k, d, x.shape, str(x.dtype)) for (k, d), x in zip(ops, xs))
    if key not in _IDS:
        _IDS[key] = len(_IDS)
    groups = []
    for _, axes in ops:
        if axes not in groups:
            groups.append(axes)
    out_shapes, scratch = [], []
    for (kind, axes), x in zip(ops, xs):
        g = group_size(axes)
        if kind == "sum":
            out_shapes.append(jax.ShapeDtypeStruct(x.shape, x.dtype))
            scratch += [pltpu.VMEM((g,) + x.shape, x.dtype), pltpu.SemaphoreType.DMA((g,)),
                        pltpu.SemaphoreType.DMA((g,))]
        else:
            c = x.shape[0] // g
            out_shapes.append(jax.ShapeDtypeStruct((g, c) + x.shape[1:], x.dtype))
            scratch += [pltpu.VMEM((g, c) + x.shape[1:], x.dtype), pltpu.VMEM((g, c) + x.shape[1:], x.dtype),
                        pltpu.SemaphoreType.DMA((g,)), pltpu.SemaphoreType.DMA((g,)),
                        pltpu.SemaphoreType.DMA((g,)), pltpu.SemaphoreType.DMA((g,))]
    outs = pl.pallas_call(
        functools.partial(direct_kernel, ops, groups),
        out_shape=out_shapes,
        in_specs=[pl.BlockSpec(memory_space=pltpu.VMEM)] * len(xs),
        out_specs=[pl.BlockSpec(memory_space=pltpu.VMEM)] * len(xs),
        scratch_shapes=scratch,
        compiler_params=pltpu.CompilerParams(collective_id=_IDS[key], has_side_effects=True),
    )(*xs)
    return [o.reshape(x.shape) for o, x in zip(outs, xs)]


def exchange_bfly(ops, xs):
    key = ("bfly",) + tuple((k, d, x.shape, str(x.dtype)) for (k, d), x in zip(ops, xs))
    if key not in _IDS:
        _IDS[key] = len(_IDS)
    out_shapes, scratch = [], []
    for (kind, digits), x in zip(ops, xs):
        g = group_size(digits)
        L = op_rounds(kind, g)
        if kind == "gather":
            out_shapes.append(jax.ShapeDtypeStruct((g,) + x.shape, x.dtype))
            scratch += [pltpu.VMEM((g,) + x.shape, x.dtype), pltpu.VMEM((8, 128), jnp.float32)]
        elif kind == "sum":
            out_shapes.append(jax.ShapeDtypeStruct(x.shape, x.dtype))
            scratch += [pltpu.VMEM(x.shape, x.dtype), pltpu.VMEM((L,) + x.shape, x.dtype)]
        else:
            out_shapes.append(jax.ShapeDtypeStruct(x.shape, x.dtype))
            scratch += [pltpu.VMEM(x.shape, x.dtype),
                        pltpu.VMEM((L // 2, x.shape[0] // 2) + x.shape[1:], x.dtype),
                        pltpu.VMEM(x.shape, x.dtype)]
        scratch += [pltpu.SemaphoreType.DMA((L,)), pltpu.SemaphoreType.DMA((L,))]
    outs = pl.pallas_call(
        functools.partial(exchange_kernel, ops),
        out_shape=out_shapes,
        in_specs=[pl.BlockSpec(memory_space=pltpu.VMEM)] * len(xs),
        out_specs=[pl.BlockSpec(memory_space=pltpu.VMEM)] * len(xs),
        scratch_shapes=scratch,
        compiler_params=pltpu.CompilerParams(collective_id=_IDS[key], has_side_effects=True),
    )(*xs)
    return list(outs)


def make_local(sizes, row_axes, col_axes):
    def local(particles, start_basis):
        shard = particles.shape[0]
        width = particles.shape[1]
        eig = start_basis.shape[1]
        total = shard * math.prod(sizes.values())
        spread = 2.0 * width
        root_total = math.sqrt(float(total))

        dense_basis = start_basis.reshape(shard * eig // 128, 128)
        i_feats, i_basis, j_feats, j_basis = exchange_bfly(
            [("gather", row_axes), ("gather", row_axes), ("gather", col_axes), ("gather", col_axes)],
            [particles, dense_basis, particles, dense_basis])
        gi = group_size(row_axes)
        gj = group_size(col_axes)
        i_feats = i_feats.reshape(gi * shard, width)
        j_feats = j_feats.reshape(gj * shard, width)
        basis_i = i_basis.reshape(gi * shard, eig)
        basis_j = j_basis.reshape(gj * shard, eig)

        def block_ids(digits):
            coords = member_coords(digits, jnp.arange(group_size(digits), dtype=jnp.int32))
            flat = jnp.zeros((group_size(digits),), jnp.int32)
            for a, cval in zip(MESH_AXES, coords):
                flat = flat * sizes[a] + cval
            return (flat[:, None] * shard + jnp.arange(shard, dtype=jnp.int32)[None, :]).reshape(-1)

        ids_i = block_ids(row_axes)
        ids_j = block_ids(col_axes)
        sq_i = jnp.sum(jnp.square(i_feats.astype(jnp.float32)), axis=1)
        sq_j = jnp.sum(jnp.square(j_feats.astype(jnp.float32)), axis=1)
        dots = lax.dot_general(i_feats, j_feats, (((1,), (1,)), ((), ())), preferred_element_type=jnp.float32)
        distance = sq_i[:, None] + sq_j[None, :] - 2.0 * dots
        tile = jnp.where(ids_i[:, None] == ids_j[None, :], jnp.float32(0.0), jnp.exp(-distance / spread))

        deg_i, deg_j = exchange(
            [("sum", row_axes), ("sum", col_axes)],
            [jnp.sum(tile, axis=1).reshape(-1, 128), jnp.sum(tile, axis=0).reshape(-1, 128)])
        deg_i = deg_i.reshape(-1)
        deg_j = deg_j.reshape(-1)
        root_i = jnp.sqrt(deg_i)
        root_j = jnp.sqrt(deg_j)
        me_i = group_pos(row_axes)

        def pack(mat, vecs):
            dense = mat.reshape(gi, -1, 128)
            tail = jnp.broadcast_to(vecs.reshape(1, 8, 128), (gi, 8, 128))
            return jnp.concatenate([dense, tail], axis=1).reshape(-1, 128)

        def unpack(res):
            res = res.reshape(gi, -1, 128)
            return res[:, :-8].reshape(-1, eig), res[0, -8:].reshape(-1, eig)

        scaled_i = basis_i / root_i[:, None]
        scaled_j = basis_j / root_j[:, None]
        prod_i = jnp.dot(tile, scaled_j, precision=HIGH)
        prod_j = lax.dot_general(tile, scaled_i, (((0,), (0,)), ((), ())), precision=HIGH)
        extra = jnp.concatenate([jnp.dot(root_j, basis_j, precision=HIGH)[None, :],
                                 jnp.broadcast_to(jnp.sum(deg_j), (1, eig)),
                                 jnp.zeros((14, eig), jnp.float32)], axis=0)
        packed, dense_j = exchange(
            [("rsag", row_axes), ("rsag", col_axes)], [pack(prod_i, extra), prod_j.reshape(-1, 128)])
        prod_i, extra = unpack(packed)
        prod_j = dense_j.reshape(-1, eig)
        inv_s = 1.0 / jnp.sqrt(extra[1, 0])
        aligned = extra[0] * inv_s
        defl_i = prod_i / root_i[:, None] - (root_i * inv_s)[:, None] * aligned[None, :]
        defl_j = prod_j / root_j[:, None] - (root_j * inv_s)[:, None] * aligned[None, :]
        factor = None
        for sweep in range(ITERS):
            last = sweep == ITERS - 1
            need_j = sweep + 2 < ITERS
            gram = lax.dot_general(defl_i, defl_i, (((0,), (0,)), ((), ())), precision=HIGH).reshape(-1, 128)
            if last:
                (gram,) = exchange([("sum", col_axes)], [gram])
            else:
                q_i = jnp.dot(tile, defl_j / root_j[:, None], precision=HIGH)
                part = jnp.concatenate([jnp.dot(root_j, defl_j, precision=HIGH)[None, :],
                                        jnp.zeros((15, eig), jnp.float32)], axis=0)
                ops = [("sum", col_axes), ("rsag", row_axes)]
                xs = [gram, pack(q_i, part)]
                if need_j:
                    q_j = lax.dot_general(tile, defl_i / root_i[:, None], (((0,), (0,)), ((), ())), precision=HIGH)
                    ops.append(("rsag", col_axes))
                    xs.append(q_j.reshape(-1, 128))
                res = exchange(ops, xs)
                gram = res[0]
                q_i, part = unpack(res[1])
                res = res[:1] + [None, None] + res[2:]
            factor = jnp.linalg.cholesky(gram.reshape(eig, eig))
            if last:
                own = lax.dynamic_slice_in_dim(defl_i, me_i * shard, shard, 0)
                basis_own = jax.scipy.linalg.solve_triangular(factor, own.T, lower=True).T * root_total
                break
            prod_i = jax.scipy.linalg.solve_triangular(factor, q_i.T, lower=True).T * root_total
            aligned = jax.scipy.linalg.solve_triangular(factor, part[0], lower=True) * (root_total * inv_s)
            defl_i = prod_i / root_i[:, None] - (root_i * inv_s)[:, None] * aligned[None, :]
            if need_j:
                prod_j = jax.scipy.linalg.solve_triangular(factor, res[3].reshape(-1, eig).T, lower=True).T * root_total
                defl_j = prod_j / root_j[:, None] - (root_j * inv_s)[:, None] * aligned[None, :]
        return basis_own, factor

    return local


def solution(mesh):
    sizes = dict(mesh.shape)
    placed = (P(MESH_AXES, None), P(MESH_AXES, None))
    return jax.shard_map(
        make_local(sizes, (("row", 1, 2), ("row", 2, sizes["row"] // 2), ("vec", 1, sizes["vec"])), (("col", 1, sizes["col"]),)),
        mesh=mesh,
        in_specs=placed,
        out_specs=(P(MESH_AXES, None), P()),
        check_vma=False,
    )
```

```python
import functools
import math

import jax
import jax.numpy as jnp
from jax import lax
from jax.experimental import pallas as pl
from jax.experimental.pallas import tpu as pltpu
from jax.sharding import PartitionSpec as P

ITERS = 2
MESH_AXES = ("row", "col", "vec")
MESH = pl.DeviceIdType.MESH
HIGH = lax.Precision.HIGHEST


def group_pos(digits):
    me = 0
    for a, div, mod in digits:
        me = me * mod + (lax.axis_index(a) // div) % mod
    return me


def group_size(digits):
    return math.prod(mod for _, _, mod in digits)


def member_coords(digits, m):
    own = {a: lax.axis_index(a) for a in MESH_AXES}
    coords = dict(own)
    rem = m
    for a, div, mod in reversed(digits):
        d = rem % mod
        rem = rem // mod
        coords[a] = coords[a] - ((own[a] // div) % mod) * div + d * div
    return tuple(coords[a] for a in MESH_AXES)


def flip(me, b):
    return me + (1 - 2 * ((me // (1 << b)) % 2)) * (1 << b)


def op_rounds(kind, g):
    bits = g.bit_length() - 1
    return 2 * bits if kind == "rsag" else bits


def exchange_kernel(ops, *refs):
    n = len(ops)
    ins, outs, scr = refs[:n], refs[n:2 * n], refs[2 * n:]
    barrier = pltpu.get_barrier_semaphore()
    groups = []
    for _, digits in ops:
        if digits not in groups:
            groups.append(digits)
    count = 0
    for digits in groups:
        g = group_size(digits)
        me = group_pos(digits)
        for b in range(g.bit_length() - 1):
            pl.semaphore_signal(barrier, inc=1, device_id=member_coords(digits, flip(me, b)), device_id_type=MESH)
            count += 1
    pl.semaphore_wait(barrier, count)

    state = []
    pos = 0
    for i, (kind, digits) in enumerate(ops):
        x_ref = ins[i]
        if kind == "rsag":
            w, r, gat, ssem, rsem = scr[pos:pos + 5]
            pos += 5
            r = (r, gat)
        else:
            w, r, ssem, rsem = scr[pos:pos + 4]
            pos += 4
        if kind == "gather":
            w[group_pos(digits)] = x_ref[...]
        else:
            w[...] = x_ref[...]
        state.append((w, r, ssem, rsem))

    nrounds = max(op_rounds(kind, group_size(d)) for kind, d in ops)
    for t in range(nrounds):
        copies = []
        for i, (kind, digits) in enumerate(ops):
            g = group_size(digits)
            bits = g.bit_length() - 1
            if t >= op_rounds(kind, g):
                continue
            me = group_pos(digits)
            w, r, ssem, rsem = state[i]
            if kind == "gather":
                b = t
                partner = flip(me, b)
                span = 1 << b
                mine = pl.ds((me // span) * span, span)
                theirs = pl.ds((partner // span) * span, span)
                src, dst, land = w.at[mine], w.at[mine], w.at[theirs]
            elif kind == "sum":
                b = t
                partner = flip(me, b)
                src, dst, land = w, r.at[t], r.at[t]
            elif t < bits:
                r = r[0]
                b = bits - 1 - t
                partner = flip(me, b)
                size = w.shape[0] >> (t + 1)
                theirs = pl.ds(pl.multiple_of((partner // (1 << b)) * size, size), size)
                src, dst, land = w.at[theirs], r.at[t, pl.ds(0, size)], r.at[t, pl.ds(0, size)]
            else:
                u = t - bits
                b = u
                partner = flip(me, b)
                gat = r[1]
                size = (w.shape[0] // g) << u
                if u == 0:
                    gat[pl.ds(pl.multiple_of(me * size, size), size)] = w[pl.ds(pl.multiple_of(me * size, size), size)]
                mine = pl.ds(pl.multiple_of((me // (1 << u)) * size, size), size)
                theirs = pl.ds(pl.multiple_of((partner // (1 << u)) * size, size), size)
                src, dst, land = gat.at[mine], gat.at[mine], gat.at[theirs]
            dev = member_coords(digits, partner)
            out = pltpu.make_async_remote_copy(
                src_ref=src, dst_ref=dst, send_sem=ssem.at[t], recv_sem=rsem.at[t],
                device_id=dev, device_id_type=MESH)
            out.start()
            back = pltpu.make_async_remote_copy(
                src_ref=src, dst_ref=land, send_sem=ssem.at[t], recv_sem=rsem.at[t],
                device_id=dev, device_id_type=MESH)
            copies.append((i, kind, t, bits, out, back, me))
        for i, kind, t, bits, out, back, me in copies:
            back.wait_recv()
            out.wait_send()
            w, r, ssem, rsem = state[i]
            if kind == "sum":
                w[...] = w[...] + r[t]
            elif kind == "rsag" and t < bits:
                b = bits - 1 - t
                size = w.shape[0] >> (t + 1)
                mine = pl.ds(pl.multiple_of((me // (1 << b)) * size, size), size)
                w[mine] = w[mine] + r[0][t, pl.ds(0, size)]
    for i, (kind, _) in enumerate(ops):
        outs[i][...] = state[i][1][1][...] if kind == "rsag" else state[i][0][...]


def direct_kernel(ops, groups, *refs):
    n = len(ops)
    ins, outs, scr = refs[:n], refs[n:2 * n], refs[2 * n:]
    barrier = pltpu.get_barrier_semaphore()
    total_peers = 0
    for axes in groups:
        g = group_size(axes)
        me = group_pos(axes)
        total_peers += g - 1

        def greet(k, c, axes=axes, g=g, me=me):
            pl.semaphore_signal(barrier, inc=1, device_id=member_coords(axes, (me + k) % g), device_id_type=MESH)
            return c

        lax.fori_loop(1, g, greet, 0)
    pl.semaphore_wait(barrier, total_peers)

    pos = 0
    pending = []
    for i, (kind, axes) in enumerate(ops):
        g = group_size(axes)
        me = group_pos(axes)
        x_ref, o_ref = ins[i], outs[i]
        if kind in ("gather", "sum"):
            slots, ssem, rsem = scr[pos:pos + 3]
            pos += 3
            slots[me] = x_ref[...]

            def send(k, c, x_ref=x_ref, slots=slots, ssem=ssem, rsem=rsem, axes=axes, g=g, me=me):
                peer = (me + k) % g
                pltpu.make_async_remote_copy(
                    src_ref=x_ref, dst_ref=slots.at[me], send_sem=ssem.at[peer], recv_sem=rsem.at[me],
                    device_id=member_coords(axes, peer), device_id_type=MESH).start()
                return c

            lax.fori_loop(1, g, send, 0)
            pending.append((kind, axes, g, me, x_ref, o_ref, slots, ssem, rsem))
        else:
            rs, ag, ssem, rsem, ssem2, rsem2 = scr[pos:pos + 6]
            pos += 6
            c = x_ref.shape[0] // g
            rs[me] = x_ref[pl.ds(pl.multiple_of(me * c, c), c)]

            def send(k, cc, x_ref=x_ref, rs=rs, ssem=ssem, rsem=rsem, axes=axes, g=g, me=me, c=c):
                peer = (me + k) % g
                pltpu.make_async_remote_copy(
                    src_ref=x_ref.at[pl.ds(pl.multiple_of(peer * c, c), c)], dst_ref=rs.at[me],
                    send_sem=ssem.at[peer], recv_sem=rsem.at[me],
                    device_id=member_coords(axes, peer), device_id_type=MESH).start()
                return cc

            lax.fori_loop(1, g, send, 0)
            pending.append((kind, axes, g, me, x_ref, o_ref, (rs, ag, ssem2, rsem2), ssem, rsem))

    for kind, axes, g, me, x_ref, o_ref, slots, ssem, rsem in pending:
        if kind == "rsag":
            rs, ag, ssem2, rsem2 = slots
            c = rs.shape[1]
        else:
            rs = slots

        def wait(k, cc, x_ref=x_ref, rs=rs, ssem=ssem, rsem=rsem, axes=axes, g=g, me=me, kind=kind):
            src = (me + g - k) % g
            peer = (me + k) % g
            if kind == "rsag":
                c = rs.shape[1]
                src_ref = x_ref.at[pl.ds(0, c)]
            else:
                src_ref = x_ref
            pltpu.make_async_remote_copy(
                src_ref=src_ref, dst_ref=rs.at[src], send_sem=ssem.at[peer], recv_sem=rsem.at[src],
                device_id=member_coords(axes, peer), device_id_type=MESH).wait_recv()
            pltpu.make_async_remote_copy(
                src_ref=src_ref, dst_ref=rs.at[me], send_sem=ssem.at[peer], recv_sem=rsem.at[me],
                device_id=member_coords(axes, peer), device_id_type=MESH).wait_send()
            return cc

        lax.fori_loop(1, g, wait, 0)
        if kind == "gather":
            o_ref[...] = rs[...]
        elif kind == "sum":
            acc = rs[0]
            for s in range(1, g):
                acc = acc + rs[s]
            o_ref[...] = acc
        else:
            acc = rs[0]
            for s in range(1, g):
                acc = acc + rs[s]
            ag[me] = acc

            def send2(k, cc, ag=ag, ssem2=ssem2, rsem2=rsem2, axes=axes, g=g, me=me):
                peer = (me + k) % g
                pltpu.make_async_remote_copy(
                    src_ref=ag.at[me], dst_ref=ag.at[me], send_sem=ssem2.at[peer], recv_sem=rsem2.at[me],
                    device_id=member_coords(axes, peer), device_id_type=MESH).start()
                return cc

            lax.fori_loop(1, g, send2, 0)

            def wait2(k, cc, ag=ag, ssem2=ssem2, rsem2=rsem2, axes=axes, g=g, me=me):
                src = (me + g - k) % g
                peer = (me + k) % g
                pltpu.make_async_remote_copy(
                    src_ref=ag.at[me], dst_ref=ag.at[src], send_sem=ssem2.at[peer], recv_sem=rsem2.at[src],
                    device_id=member_coords(axes, peer), device_id_type=MESH).wait_recv()
                pltpu.make_async_remote_copy(
                    src_ref=ag.at[me], dst_ref=ag.at[me], send_sem=ssem2.at[peer], recv_sem=rsem2.at[me],
                    device_id=member_coords(axes, peer), device_id_type=MESH).wait_send()
                return cc

            lax.fori_loop(1, g, wait2, 0)
            o_ref[...] = ag[...]


_IDS = {}


def exchange(ops, xs):
    key = ("direct",) + tuple((k, d, x.shape, str(x.dtype)) for (k, d), x in zip(ops, xs))
    if key not in _IDS:
        _IDS[key] = len(_IDS)
    groups = []
    for _, axes in ops:
        if axes not in groups:
            groups.append(axes)
    out_shapes, scratch = [], []
    for (kind, axes), x in zip(ops, xs):
        g = group_size(axes)
        if kind == "sum":
            out_shapes.append(jax.ShapeDtypeStruct(x.shape, x.dtype))
            scratch += [pltpu.VMEM((g,) + x.shape, x.dtype), pltpu.SemaphoreType.DMA((g,)),
                        pltpu.SemaphoreType.DMA((g,))]
        else:
            c = x.shape[0] // g
            out_shapes.append(jax.ShapeDtypeStruct((g, c) + x.shape[1:], x.dtype))
            scratch += [pltpu.VMEM((g, c) + x.shape[1:], x.dtype), pltpu.VMEM((g, c) + x.shape[1:], x.dtype),
                        pltpu.SemaphoreType.DMA((g,)), pltpu.SemaphoreType.DMA((g,)),
                        pltpu.SemaphoreType.DMA((g,)), pltpu.SemaphoreType.DMA((g,))]
    outs = pl.pallas_call(
        functools.partial(direct_kernel, ops, groups),
        out_shape=out_shapes,
        in_specs=[pl.BlockSpec(memory_space=pltpu.VMEM)] * len(xs),
        out_specs=[pl.BlockSpec(memory_space=pltpu.VMEM)] * len(xs),
        scratch_shapes=scratch,
        compiler_params=pltpu.CompilerParams(collective_id=_IDS[key], has_side_effects=True),
    )(*xs)
    return [o.reshape(x.shape) for o, x in zip(outs, xs)]


def exchange_bfly(ops, xs):
    key = ("bfly",) + tuple((k, d, x.shape, str(x.dtype)) for (k, d), x in zip(ops, xs))
    if key not in _IDS:
        _IDS[key] = len(_IDS)
    out_shapes, scratch = [], []
    for (kind, digits), x in zip(ops, xs):
        g = group_size(digits)
        L = op_rounds(kind, g)
        if kind == "gather":
            out_shapes.append(jax.ShapeDtypeStruct((g,) + x.shape, x.dtype))
            scratch += [pltpu.VMEM((g,) + x.shape, x.dtype), pltpu.VMEM((8, 128), jnp.float32)]
        elif kind == "sum":
            out_shapes.append(jax.ShapeDtypeStruct(x.shape, x.dtype))
            scratch += [pltpu.VMEM(x.shape, x.dtype), pltpu.VMEM((L,) + x.shape, x.dtype)]
        else:
            out_shapes.append(jax.ShapeDtypeStruct(x.shape, x.dtype))
            scratch += [pltpu.VMEM(x.shape, x.dtype),
                        pltpu.VMEM((L // 2, x.shape[0] // 2) + x.shape[1:], x.dtype),
                        pltpu.VMEM(x.shape, x.dtype)]
        scratch += [pltpu.SemaphoreType.DMA((L,)), pltpu.SemaphoreType.DMA((L,))]
    outs = pl.pallas_call(
        functools.partial(exchange_kernel, ops),
        out_shape=out_shapes,
        in_specs=[pl.BlockSpec(memory_space=pltpu.VMEM)] * len(xs),
        out_specs=[pl.BlockSpec(memory_space=pltpu.VMEM)] * len(xs),
        scratch_shapes=scratch,
        compiler_params=pltpu.CompilerParams(collective_id=_IDS[key], has_side_effects=True),
    )(*xs)
    return list(outs)


def make_local(sizes, row_axes, col_axes):
    def local(particles, start_basis):
        shard = particles.shape[0]
        width = particles.shape[1]
        eig = start_basis.shape[1]
        total = shard * math.prod(sizes.values())
        spread = 2.0 * width
        root_total = math.sqrt(float(total))

        dense_basis = start_basis.reshape(shard * eig // 128, 128)
        i_feats, i_basis, j_feats = exchange_bfly(
            [("gather", row_axes), ("gather", row_axes), ("gather", col_axes)],
            [particles, dense_basis, particles])
        gi = group_size(row_axes)
        gj = group_size(col_axes)
        i_feats = i_feats.reshape(gi * shard, width)
        j_feats = j_feats.reshape(gj * shard, width)
        basis_i = i_basis.reshape(gi * shard, eig)

        def block_ids(digits):
            coords = member_coords(digits, jnp.arange(group_size(digits), dtype=jnp.int32))
            flat = jnp.zeros((group_size(digits),), jnp.int32)
            for a, cval in zip(MESH_AXES, coords):
                flat = flat * sizes[a] + cval
            return (flat[:, None] * shard + jnp.arange(shard, dtype=jnp.int32)[None, :]).reshape(-1)

        ids_i = block_ids(row_axes)
        ids_j = block_ids(col_axes)
        sq_i = jnp.sum(jnp.square(i_feats.astype(jnp.float32)), axis=1)
        sq_j = jnp.sum(jnp.square(j_feats.astype(jnp.float32)), axis=1)
        dots = lax.dot_general(i_feats, j_feats, (((1,), (1,)), ((), ())), preferred_element_type=jnp.float32)
        distance = sq_i[:, None] + sq_j[None, :] - 2.0 * dots
        tile = jnp.where(ids_i[:, None] == ids_j[None, :], jnp.float32(0.0), jnp.exp(-distance / spread))

        deg_i, deg_j = exchange(
            [("sum", row_axes), ("sum", col_axes)],
            [jnp.sum(tile, axis=1).reshape(-1, 128), jnp.sum(tile, axis=0).reshape(-1, 128)])
        deg_i = deg_i.reshape(-1)
        deg_j = deg_j.reshape(-1)
        root_i = jnp.sqrt(deg_i)
        root_j = jnp.sqrt(deg_j)
        me_i = group_pos(row_axes)
        scaled_i = basis_i / root_i[:, None]
        prod_j = lax.dot_general(tile, scaled_i, (((0,), (0,)), ((), ())), precision=HIGH)
        extra = jnp.concatenate([jnp.dot(root_i, basis_i, precision=HIGH)[None, :],
                                 jnp.broadcast_to(jnp.sum(deg_i), (1, eig)),
                                 jnp.zeros((6, eig), jnp.float32)], axis=0)
        dense_j, extra = exchange(
            [("rsag", col_axes), ("sum", col_axes)], [prod_j.reshape(-1, 128), extra.reshape(-1, 128)])
        prod_j = dense_j.reshape(-1, eig)
        extra = extra.reshape(-1, eig)
        inv_s = 1.0 / jnp.sqrt(extra[1, 0])
        aligned = extra[0] * inv_s
        defl_j = prod_j / root_j[:, None] - (root_j * inv_s)[:, None] * aligned[None, :]

        gram = lax.dot_general(defl_j, defl_j, (((0,), (0,)), ((), ())), precision=HIGH).reshape(-1, 128)
        q_i = jnp.dot(tile, defl_j / root_j[:, None], precision=HIGH)
        part = jnp.concatenate([jnp.dot(root_j, defl_j, precision=HIGH)[None, :],
                                jnp.zeros((7, eig), jnp.float32)], axis=0)
        gram, q_i, part = exchange(
            [("rsag", row_axes), ("rsag", row_axes), ("sum", row_axes)],
            [gram, q_i.reshape(-1, 128), part.reshape(-1, 128)])
        factor = jnp.linalg.cholesky(gram.reshape(eig, eig))
        q_i = q_i.reshape(-1, eig)
        part = part.reshape(-1, eig)
        prod_i = jax.scipy.linalg.solve_triangular(factor, q_i.T, lower=True).T * root_total
        aligned = jax.scipy.linalg.solve_triangular(factor, part[0], lower=True) * (root_total * inv_s)
        defl_i = prod_i / root_i[:, None] - (root_i * inv_s)[:, None] * aligned[None, :]

        gram = lax.dot_general(defl_i, defl_i, (((0,), (0,)), ((), ())), precision=HIGH).reshape(-1, 128)
        (gram,) = exchange([("sum", col_axes)], [gram])
        factor = jnp.linalg.cholesky(gram.reshape(eig, eig))
        own = lax.dynamic_slice_in_dim(defl_i, me_i * shard, shard, 0)
        basis_own = jax.scipy.linalg.solve_triangular(factor, own.T, lower=True).T * root_total
        return basis_own, factor

    return local


def solution(mesh):
    sizes = dict(mesh.shape)
    placed = (P(MESH_AXES, None), P(MESH_AXES, None))
    return jax.shard_map(
        make_local(sizes, (("row", 1, 2), ("row", 2, sizes["row"] // 2), ("vec", 1, sizes["vec"])), (("col", 1, sizes["col"]),)),
        mesh=mesh,
        in_specs=placed,
        out_specs=(P(MESH_AXES, None), P()),
        check_vma=False,
    )
```

```python
import functools
import math

import jax
import jax.numpy as jnp
from jax import lax
from jax.experimental import pallas as pl
from jax.experimental.pallas import tpu as pltpu
from jax.sharding import PartitionSpec as P

ITERS = 2
MESH_AXES = ("row", "col", "vec")
MESH = pl.DeviceIdType.MESH
HIGH = lax.Precision.HIGHEST


def group_pos(digits):
    me = 0
    for a, div, mod in digits:
        me = me * mod + (lax.axis_index(a) // div) % mod
    return me


def group_size(digits):
    return math.prod(mod for _, _, mod in digits)


def member_coords(digits, m):
    own = {a: lax.axis_index(a) for a in MESH_AXES}
    coords = dict(own)
    rem = m
    for a, div, mod in reversed(digits):
        d = rem % mod
        rem = rem // mod
        coords[a] = coords[a] - ((own[a] // div) % mod) * div + d * div
    return tuple(coords[a] for a in MESH_AXES)


def flip(me, b):
    return me + (1 - 2 * ((me // (1 << b)) % 2)) * (1 << b)


def op_rounds(kind, g):
    bits = g.bit_length() - 1
    return 2 * bits if kind == "rsag" else bits


def exchange_kernel(ops, *refs):
    n = len(ops)
    ins, outs, scr = refs[:n], refs[n:2 * n], refs[2 * n:]
    barrier = pltpu.get_barrier_semaphore()
    groups = []
    for _, digits in ops:
        if digits not in groups:
            groups.append(digits)
    count = 0
    for digits in groups:
        g = group_size(digits)
        me = group_pos(digits)
        for b in range(g.bit_length() - 1):
            pl.semaphore_signal(barrier, inc=1, device_id=member_coords(digits, flip(me, b)), device_id_type=MESH)
            count += 1
    pl.semaphore_wait(barrier, count)

    state = []
    pos = 0
    for i, (kind, digits) in enumerate(ops):
        x_ref = ins[i]
        if kind == "rsag":
            w, r, gat, ssem, rsem = scr[pos:pos + 5]
            pos += 5
            r = (r, gat)
        else:
            w, r, ssem, rsem = scr[pos:pos + 4]
            pos += 4
        if kind == "gather":
            w[group_pos(digits)] = x_ref[...]
        else:
            w[...] = x_ref[...]
        state.append((w, r, ssem, rsem))

    nrounds = max(op_rounds(kind, group_size(d)) for kind, d in ops)
    for t in range(nrounds):
        copies = []
        for i, (kind, digits) in enumerate(ops):
            g = group_size(digits)
            bits = g.bit_length() - 1
            if t >= op_rounds(kind, g):
                continue
            me = group_pos(digits)
            w, r, ssem, rsem = state[i]
            if kind == "gather":
                b = t
                partner = flip(me, b)
                span = 1 << b
                mine = pl.ds((me // span) * span, span)
                theirs = pl.ds((partner // span) * span, span)
                src, dst, land = w.at[mine], w.at[mine], w.at[theirs]
            elif kind == "sum":
                b = t
                partner = flip(me, b)
                src, dst, land = w, r.at[t], r.at[t]
            elif t < bits:
                r = r[0]
                b = bits - 1 - t
                partner = flip(me, b)
                size = w.shape[0] >> (t + 1)
                theirs = pl.ds(pl.multiple_of((partner // (1 << b)) * size, size), size)
                src, dst, land = w.at[theirs], r.at[t, pl.ds(0, size)], r.at[t, pl.ds(0, size)]
            else:
                u = t - bits
                b = u
                partner = flip(me, b)
                gat = r[1]
                size = (w.shape[0] // g) << u
                if u == 0:
                    gat[pl.ds(pl.multiple_of(me * size, size), size)] = w[pl.ds(pl.multiple_of(me * size, size), size)]
                mine = pl.ds(pl.multiple_of((me // (1 << u)) * size, size), size)
                theirs = pl.ds(pl.multiple_of((partner // (1 << u)) * size, size), size)
                src, dst, land = gat.at[mine], gat.at[mine], gat.at[theirs]
            dev = member_coords(digits, partner)
            out = pltpu.make_async_remote_copy(
                src_ref=src, dst_ref=dst, send_sem=ssem.at[t], recv_sem=rsem.at[t],
                device_id=dev, device_id_type=MESH)
            out.start()
            back = pltpu.make_async_remote_copy(
                src_ref=src, dst_ref=land, send_sem=ssem.at[t], recv_sem=rsem.at[t],
                device_id=dev, device_id_type=MESH)
            copies.append((i, kind, t, bits, out, back, me))
        for i, kind, t, bits, out, back, me in copies:
            back.wait_recv()
            out.wait_send()
            w, r, ssem, rsem = state[i]
            if kind == "sum":
                w[...] = w[...] + r[t]
            elif kind == "rsag" and t < bits:
                b = bits - 1 - t
                size = w.shape[0] >> (t + 1)
                mine = pl.ds(pl.multiple_of((me // (1 << b)) * size, size), size)
                w[mine] = w[mine] + r[0][t, pl.ds(0, size)]
    for i, (kind, _) in enumerate(ops):
        outs[i][...] = state[i][1][1][...] if kind == "rsag" else state[i][0][...]


def direct_kernel(ops, groups, *refs):
    n = len(ops)
    ins, outs, scr = refs[:n], refs[n:2 * n], refs[2 * n:]
    barrier = pltpu.get_barrier_semaphore()
    total_peers = 0
    for axes in groups:
        g = group_size(axes)
        me = group_pos(axes)
        total_peers += g - 1

        def greet(k, c, axes=axes, g=g, me=me):
            pl.semaphore_signal(barrier, inc=1, device_id=member_coords(axes, (me + k) % g), device_id_type=MESH)
            return c

        lax.fori_loop(1, g, greet, 0)
    pl.semaphore_wait(barrier, total_peers)

    pos = 0
    pending = []
    for i, (kind, axes) in enumerate(ops):
        g = group_size(axes)
        me = group_pos(axes)
        x_ref, o_ref = ins[i], outs[i]
        if kind in ("gather", "sum"):
            slots, ssem, rsem = scr[pos:pos + 3]
            pos += 3
            slots[me] = x_ref[...]

            def send(k, c, x_ref=x_ref, slots=slots, ssem=ssem, rsem=rsem, axes=axes, g=g, me=me):
                peer = (me + k) % g
                pltpu.make_async_remote_copy(
                    src_ref=x_ref, dst_ref=slots.at[me], send_sem=ssem.at[peer], recv_sem=rsem.at[me],
                    device_id=member_coords(axes, peer), device_id_type=MESH).start()
                return c

            lax.fori_loop(1, g, send, 0)
            pending.append((kind, axes, g, me, x_ref, o_ref, slots, ssem, rsem))
        else:
            rs, ag, ssem, rsem, ssem2, rsem2 = scr[pos:pos + 6]
            pos += 6
            c = x_ref.shape[0] // g
            rs[me] = x_ref[pl.ds(pl.multiple_of(me * c, c), c)]

            def send(k, cc, x_ref=x_ref, rs=rs, ssem=ssem, rsem=rsem, axes=axes, g=g, me=me, c=c):
                peer = (me + k) % g
                pltpu.make_async_remote_copy(
                    src_ref=x_ref.at[pl.ds(pl.multiple_of(peer * c, c), c)], dst_ref=rs.at[me],
                    send_sem=ssem.at[peer], recv_sem=rsem.at[me],
                    device_id=member_coords(axes, peer), device_id_type=MESH).start()
                return cc

            lax.fori_loop(1, g, send, 0)
            pending.append((kind, axes, g, me, x_ref, o_ref, (rs, ag, ssem2, rsem2), ssem, rsem))

    for kind, axes, g, me, x_ref, o_ref, slots, ssem, rsem in pending:
        if kind == "rsag":
            rs, ag, ssem2, rsem2 = slots
            c = rs.shape[1]
        else:
            rs = slots

        def wait(k, cc, x_ref=x_ref, rs=rs, ssem=ssem, rsem=rsem, axes=axes, g=g, me=me, kind=kind):
            src = (me + g - k) % g
            peer = (me + k) % g
            if kind == "rsag":
                c = rs.shape[1]
                src_ref = x_ref.at[pl.ds(0, c)]
            else:
                src_ref = x_ref
            pltpu.make_async_remote_copy(
                src_ref=src_ref, dst_ref=rs.at[src], send_sem=ssem.at[peer], recv_sem=rsem.at[src],
                device_id=member_coords(axes, peer), device_id_type=MESH).wait_recv()
            pltpu.make_async_remote_copy(
                src_ref=src_ref, dst_ref=rs.at[me], send_sem=ssem.at[peer], recv_sem=rsem.at[me],
                device_id=member_coords(axes, peer), device_id_type=MESH).wait_send()
            return cc

        lax.fori_loop(1, g, wait, 0)
        if kind == "gather":
            o_ref[...] = rs[...]
        elif kind == "sum":
            acc = rs[0]
            for s in range(1, g):
                acc = acc + rs[s]
            o_ref[...] = acc
        else:
            acc = rs[0]
            for s in range(1, g):
                acc = acc + rs[s]
            ag[me] = acc

            def send2(k, cc, ag=ag, ssem2=ssem2, rsem2=rsem2, axes=axes, g=g, me=me):
                peer = (me + k) % g
                pltpu.make_async_remote_copy(
                    src_ref=ag.at[me], dst_ref=ag.at[me], send_sem=ssem2.at[peer], recv_sem=rsem2.at[me],
                    device_id=member_coords(axes, peer), device_id_type=MESH).start()
                return cc

            lax.fori_loop(1, g, send2, 0)

            def wait2(k, cc, ag=ag, ssem2=ssem2, rsem2=rsem2, axes=axes, g=g, me=me):
                src = (me + g - k) % g
                peer = (me + k) % g
                pltpu.make_async_remote_copy(
                    src_ref=ag.at[me], dst_ref=ag.at[src], send_sem=ssem2.at[peer], recv_sem=rsem2.at[src],
                    device_id=member_coords(axes, peer), device_id_type=MESH).wait_recv()
                pltpu.make_async_remote_copy(
                    src_ref=ag.at[me], dst_ref=ag.at[me], send_sem=ssem2.at[peer], recv_sem=rsem2.at[me],
                    device_id=member_coords(axes, peer), device_id_type=MESH).wait_send()
                return cc

            lax.fori_loop(1, g, wait2, 0)
            o_ref[...] = ag[...]


def chol_kernel(g_ref, l_ref, inv_ref):
    a = g_ref[...]
    n = a.shape[0]
    rows = lax.broadcasted_iota(jnp.int32, (n, n), 0)
    lanes = lax.broadcasted_iota(jnp.int32, (n, n), 1)
    eye = (rows == lanes).astype(jnp.float32)
    x = eye
    lmat = jnp.zeros_like(a)
    for j in range(n):
        d = jnp.sqrt(a[j:j + 1, j:j + 1])
        col = jnp.where(rows[:, j:j + 1] >= j, a[:, j:j + 1], 0.0) / d
        rowv = jnp.sum(eye * col, axis=0, keepdims=True)
        a = a - col * rowv
        lmat = jnp.where(lanes == j, col, lmat)
        xj = x[j:j + 1, :] / d
        below = jnp.where(rows[:, j:j + 1] > j, col, 0.0)
        x = jnp.where(rows == j, xj, x - below * xj)
    l_ref[...] = lmat
    inv_ref[...] = x

def chol_inv(gram):
    n = gram.shape[0]
    return pl.pallas_call(chol_kernel,
        out_shape=[jax.ShapeDtypeStruct((n, n), jnp.float32)] * 2,
        in_specs=[pl.BlockSpec(memory_space=pltpu.VMEM)],
        out_specs=[pl.BlockSpec(memory_space=pltpu.VMEM)] * 2)(gram)


_IDS = {}


def exchange(ops, xs):
    key = ("direct",) + tuple((k, d, x.shape, str(x.dtype)) for (k, d), x in zip(ops, xs))
    if key not in _IDS:
        _IDS[key] = len(_IDS)
    groups = []
    for _, axes in ops:
        if axes not in groups:
            groups.append(axes)
    out_shapes, scratch = [], []
    for (kind, axes), x in zip(ops, xs):
        g = group_size(axes)
        if kind == "sum":
            out_shapes.append(jax.ShapeDtypeStruct(x.shape, x.dtype))
            scratch += [pltpu.VMEM((g,) + x.shape, x.dtype), pltpu.SemaphoreType.DMA((g,)),
                        pltpu.SemaphoreType.DMA((g,))]
        else:
            c = x.shape[0] // g
            out_shapes.append(jax.ShapeDtypeStruct((g, c) + x.shape[1:], x.dtype))
            scratch += [pltpu.VMEM((g, c) + x.shape[1:], x.dtype), pltpu.VMEM((g, c) + x.shape[1:], x.dtype),
                        pltpu.SemaphoreType.DMA((g,)), pltpu.SemaphoreType.DMA((g,)),
                        pltpu.SemaphoreType.DMA((g,)), pltpu.SemaphoreType.DMA((g,))]
    outs = pl.pallas_call(
        functools.partial(direct_kernel, ops, groups),
        out_shape=out_shapes,
        in_specs=[pl.BlockSpec(memory_space=pltpu.VMEM)] * len(xs),
        out_specs=[pl.BlockSpec(memory_space=pltpu.VMEM)] * len(xs),
        scratch_shapes=scratch,
        compiler_params=pltpu.CompilerParams(collective_id=_IDS[key], has_side_effects=True),
    )(*xs)
    return [o.reshape(x.shape) for o, x in zip(outs, xs)]


def exchange_bfly(ops, xs):
    key = ("bfly",) + tuple((k, d, x.shape, str(x.dtype)) for (k, d), x in zip(ops, xs))
    if key not in _IDS:
        _IDS[key] = len(_IDS)
    out_shapes, scratch = [], []
    for (kind, digits), x in zip(ops, xs):
        g = group_size(digits)
        L = op_rounds(kind, g)
        if kind == "gather":
            out_shapes.append(jax.ShapeDtypeStruct((g,) + x.shape, x.dtype))
            scratch += [pltpu.VMEM((g,) + x.shape, x.dtype), pltpu.VMEM((8, 128), jnp.float32)]
        elif kind == "sum":
            out_shapes.append(jax.ShapeDtypeStruct(x.shape, x.dtype))
            scratch += [pltpu.VMEM(x.shape, x.dtype), pltpu.VMEM((L,) + x.shape, x.dtype)]
        else:
            out_shapes.append(jax.ShapeDtypeStruct(x.shape, x.dtype))
            scratch += [pltpu.VMEM(x.shape, x.dtype),
                        pltpu.VMEM((L // 2, x.shape[0] // 2) + x.shape[1:], x.dtype),
                        pltpu.VMEM(x.shape, x.dtype)]
        scratch += [pltpu.SemaphoreType.DMA((L,)), pltpu.SemaphoreType.DMA((L,))]
    outs = pl.pallas_call(
        functools.partial(exchange_kernel, ops),
        out_shape=out_shapes,
        in_specs=[pl.BlockSpec(memory_space=pltpu.VMEM)] * len(xs),
        out_specs=[pl.BlockSpec(memory_space=pltpu.VMEM)] * len(xs),
        scratch_shapes=scratch,
        compiler_params=pltpu.CompilerParams(collective_id=_IDS[key], has_side_effects=True),
    )(*xs)
    return list(outs)


def make_local(sizes, row_axes, col_axes):
    def local(particles, start_basis):
        shard = particles.shape[0]
        width = particles.shape[1]
        eig = start_basis.shape[1]
        total = shard * math.prod(sizes.values())
        spread = 2.0 * width
        root_total = math.sqrt(float(total))

        dense_basis = start_basis.reshape(shard * eig // 128, 128)
        i_feats, i_basis, j_feats = exchange_bfly(
            [("gather", row_axes), ("gather", row_axes), ("gather", col_axes)],
            [particles, dense_basis, particles])
        gi = group_size(row_axes)
        gj = group_size(col_axes)
        i_feats = i_feats.reshape(gi * shard, width)
        j_feats = j_feats.reshape(gj * shard, width)
        basis_i = i_basis.reshape(gi * shard, eig)

        def block_ids(digits):
            coords = member_coords(digits, jnp.arange(group_size(digits), dtype=jnp.int32))
            flat = jnp.zeros((group_size(digits),), jnp.int32)
            for a, cval in zip(MESH_AXES, coords):
                flat = flat * sizes[a] + cval
            return (flat[:, None] * shard + jnp.arange(shard, dtype=jnp.int32)[None, :]).reshape(-1)

        ids_i = block_ids(row_axes)
        ids_j = block_ids(col_axes)
        sq_i = jnp.sum(jnp.square(i_feats.astype(jnp.float32)), axis=1)
        sq_j = jnp.sum(jnp.square(j_feats.astype(jnp.float32)), axis=1)
        dots = lax.dot_general(i_feats, j_feats, (((1,), (1,)), ((), ())), preferred_element_type=jnp.float32)
        distance = sq_i[:, None] + sq_j[None, :] - 2.0 * dots
        tile = jnp.where(ids_i[:, None] == ids_j[None, :], jnp.float32(0.0), jnp.exp(-distance / spread))

        deg_i, deg_j = exchange(
            [("sum", row_axes), ("sum", col_axes)],
            [jnp.sum(tile, axis=1).reshape(-1, 128), jnp.sum(tile, axis=0).reshape(-1, 128)])
        deg_i = deg_i.reshape(-1)
        deg_j = deg_j.reshape(-1)
        root_i = jnp.sqrt(deg_i)
        root_j = jnp.sqrt(deg_j)
        me_i = group_pos(row_axes)
        scaled_i = basis_i / root_i[:, None]
        prod_j = lax.dot_general(tile, scaled_i, (((0,), (0,)), ((), ())), precision=HIGH)
        extra = jnp.concatenate([jnp.dot(root_i, basis_i, precision=HIGH)[None, :],
                                 jnp.broadcast_to(jnp.sum(deg_i), (1, eig)),
                                 jnp.zeros((6, eig), jnp.float32)], axis=0)
        dense_j, extra = exchange(
            [("rsag", col_axes), ("sum", col_axes)], [prod_j.reshape(-1, 128), extra.reshape(-1, 128)])
        prod_j = dense_j.reshape(-1, eig)
        extra = extra.reshape(-1, eig)
        inv_s = 1.0 / jnp.sqrt(extra[1, 0])
        aligned = extra[0] * inv_s
        defl_j = prod_j / root_j[:, None] - (root_j * inv_s)[:, None] * aligned[None, :]

        gram = lax.dot_general(defl_j, defl_j, (((0,), (0,)), ((), ())), precision=HIGH).reshape(-1, 128)
        q_i = jnp.dot(tile, defl_j / root_j[:, None], precision=HIGH)
        part = jnp.concatenate([jnp.dot(root_j, defl_j, precision=HIGH)[None, :],
                                jnp.zeros((7, eig), jnp.float32)], axis=0)
        gram, q_i, part = exchange(
            [("rsag", row_axes), ("rsag", row_axes), ("sum", row_axes)],
            [gram, q_i.reshape(-1, 128), part.reshape(-1, 128)])
        factor, inverse = chol_inv(gram.reshape(eig, eig))
        q_i = q_i.reshape(-1, eig)
        part = part.reshape(-1, eig)
        prod_i = lax.dot_general(q_i, inverse, (((1,), (1,)), ((), ())), precision=HIGH) * root_total
        aligned = jnp.dot(inverse, part[0], precision=HIGH) * (root_total * inv_s)
        defl_i = prod_i / root_i[:, None] - (root_i * inv_s)[:, None] * aligned[None, :]

        gram = lax.dot_general(defl_i, defl_i, (((0,), (0,)), ((), ())), precision=HIGH).reshape(-1, 128)
        (gram,) = exchange([("sum", col_axes)], [gram])
        factor, inverse = chol_inv(gram.reshape(eig, eig))
        own = lax.dynamic_slice_in_dim(defl_i, me_i * shard, shard, 0)
        basis_own = lax.dot_general(own, inverse, (((1,), (1,)), ((), ())), precision=HIGH) * root_total
        return basis_own, factor

    return local


def solution(mesh):
    sizes = dict(mesh.shape)
    placed = (P(MESH_AXES, None), P(MESH_AXES, None))
    return jax.shard_map(
        make_local(sizes, (("row", 1, 2), ("row", 2, sizes["row"] // 2), ("vec", 1, sizes["vec"])), (("col", 1, sizes["col"]),)),
        mesh=mesh,
        in_specs=placed,
        out_specs=(P(MESH_AXES, None), P()),
        check_vma=False,
    )
```

```python
import functools
import math

import jax
import jax.numpy as jnp
from jax import lax
from jax.experimental import pallas as pl
from jax.experimental.pallas import tpu as pltpu
from jax.sharding import PartitionSpec as P

ITERS = 2
MESH_AXES = ("row", "col", "vec")
MESH = pl.DeviceIdType.MESH
HIGH = lax.Precision.HIGHEST


def group_pos(digits):
    me = 0
    for a, div, mod in digits:
        me = me * mod + (lax.axis_index(a) // div) % mod
    return me


def group_size(digits):
    return math.prod(mod for _, _, mod in digits)


def member_coords(digits, m):
    own = {a: lax.axis_index(a) for a in MESH_AXES}
    coords = dict(own)
    rem = m
    for a, div, mod in reversed(digits):
        d = rem % mod
        rem = rem // mod
        coords[a] = coords[a] - ((own[a] // div) % mod) * div + d * div
    return tuple(coords[a] for a in MESH_AXES)


def flip(me, b):
    return me + (1 - 2 * ((me // (1 << b)) % 2)) * (1 << b)


def op_rounds(kind, g):
    bits = g.bit_length() - 1
    return 2 * bits if kind == "rsag" else bits


def exchange_kernel(ops, *refs):
    n = len(ops)
    ins, outs, scr = refs[:n], refs[n:2 * n], refs[2 * n:]
    barrier = pltpu.get_barrier_semaphore()
    groups = []
    for _, digits in ops:
        if digits not in groups:
            groups.append(digits)
    count = 0
    for digits in groups:
        g = group_size(digits)
        me = group_pos(digits)
        for b in range(g.bit_length() - 1):
            pl.semaphore_signal(barrier, inc=1, device_id=member_coords(digits, flip(me, b)), device_id_type=MESH)
            count += 1
    pl.semaphore_wait(barrier, count)

    state = []
    pos = 0
    for i, (kind, digits) in enumerate(ops):
        x_ref = ins[i]
        if kind == "rsag":
            w, r, gat, ssem, rsem = scr[pos:pos + 5]
            pos += 5
            r = (r, gat)
        else:
            w, r, ssem, rsem = scr[pos:pos + 4]
            pos += 4
        if kind == "gather":
            w[group_pos(digits)] = x_ref[...]
        else:
            w[...] = x_ref[...]
        state.append((w, r, ssem, rsem))

    nrounds = max(op_rounds(kind, group_size(d)) for kind, d in ops)
    for t in range(nrounds):
        copies = []
        for i, (kind, digits) in enumerate(ops):
            g = group_size(digits)
            bits = g.bit_length() - 1
            if t >= op_rounds(kind, g):
                continue
            me = group_pos(digits)
            w, r, ssem, rsem = state[i]
            if kind == "gather":
                b = t
                partner = flip(me, b)
                span = 1 << b
                mine = pl.ds((me // span) * span, span)
                theirs = pl.ds((partner // span) * span, span)
                src, dst, land = w.at[mine], w.at[mine], w.at[theirs]
            elif kind == "sum":
                b = t
                partner = flip(me, b)
                src, dst, land = w, r.at[t], r.at[t]
            elif t < bits:
                r = r[0]
                b = bits - 1 - t
                partner = flip(me, b)
                size = w.shape[0] >> (t + 1)
                theirs = pl.ds(pl.multiple_of((partner // (1 << b)) * size, size), size)
                src, dst, land = w.at[theirs], r.at[t, pl.ds(0, size)], r.at[t, pl.ds(0, size)]
            else:
                u = t - bits
                b = u
                partner = flip(me, b)
                gat = r[1]
                size = (w.shape[0] // g) << u
                if u == 0:
                    gat[pl.ds(pl.multiple_of(me * size, size), size)] = w[pl.ds(pl.multiple_of(me * size, size), size)]
                mine = pl.ds(pl.multiple_of((me // (1 << u)) * size, size), size)
                theirs = pl.ds(pl.multiple_of((partner // (1 << u)) * size, size), size)
                src, dst, land = gat.at[mine], gat.at[mine], gat.at[theirs]
            dev = member_coords(digits, partner)
            out = pltpu.make_async_remote_copy(
                src_ref=src, dst_ref=dst, send_sem=ssem.at[t], recv_sem=rsem.at[t],
                device_id=dev, device_id_type=MESH)
            out.start()
            back = pltpu.make_async_remote_copy(
                src_ref=src, dst_ref=land, send_sem=ssem.at[t], recv_sem=rsem.at[t],
                device_id=dev, device_id_type=MESH)
            copies.append((i, kind, t, bits, out, back, me))
        for i, kind, t, bits, out, back, me in copies:
            back.wait_recv()
            out.wait_send()
            w, r, ssem, rsem = state[i]
            if kind == "sum":
                w[...] = w[...] + r[t]
            elif kind == "rsag" and t < bits:
                b = bits - 1 - t
                size = w.shape[0] >> (t + 1)
                mine = pl.ds(pl.multiple_of((me // (1 << b)) * size, size), size)
                w[mine] = w[mine] + r[0][t, pl.ds(0, size)]
    for i, (kind, _) in enumerate(ops):
        outs[i][...] = state[i][1][1][...] if kind == "rsag" else state[i][0][...]


def direct_kernel(ops, groups, *refs):
    n = len(ops)
    ins, outs, scr = refs[:n], refs[n:2 * n], refs[2 * n:]
    barrier = pltpu.get_barrier_semaphore()
    total_peers = 0
    for axes in groups:
        g = group_size(axes)
        me = group_pos(axes)
        total_peers += g - 1

        def greet(k, c, axes=axes, g=g, me=me):
            pl.semaphore_signal(barrier, inc=1, device_id=member_coords(axes, (me + k) % g), device_id_type=MESH)
            return c

        lax.fori_loop(1, g, greet, 0)
    pl.semaphore_wait(barrier, total_peers)

    pos = 0
    pending = []
    for i, (kind, axes) in enumerate(ops):
        g = group_size(axes)
        me = group_pos(axes)
        x_ref, o_ref = ins[i], outs[i]
        if kind in ("gather", "sum"):
            slots, ssem, rsem = scr[pos:pos + 3]
            pos += 3
            slots[me] = x_ref[...]

            def send(k, c, x_ref=x_ref, slots=slots, ssem=ssem, rsem=rsem, axes=axes, g=g, me=me):
                peer = (me + k) % g
                pltpu.make_async_remote_copy(
                    src_ref=x_ref, dst_ref=slots.at[me], send_sem=ssem.at[peer], recv_sem=rsem.at[me],
                    device_id=member_coords(axes, peer), device_id_type=MESH).start()
                return c

            lax.fori_loop(1, g, send, 0)
            pending.append((kind, axes, g, me, x_ref, o_ref, slots, ssem, rsem))
        else:
            rs, ag, ssem, rsem, ssem2, rsem2 = scr[pos:pos + 6]
            pos += 6
            c = x_ref.shape[0] // g
            rs[me] = x_ref[pl.ds(pl.multiple_of(me * c, c), c)]

            def send(k, cc, x_ref=x_ref, rs=rs, ssem=ssem, rsem=rsem, axes=axes, g=g, me=me, c=c):
                peer = (me + k) % g
                pltpu.make_async_remote_copy(
                    src_ref=x_ref.at[pl.ds(pl.multiple_of(peer * c, c), c)], dst_ref=rs.at[me],
                    send_sem=ssem.at[peer], recv_sem=rsem.at[me],
                    device_id=member_coords(axes, peer), device_id_type=MESH).start()
                return cc

            lax.fori_loop(1, g, send, 0)
            pending.append((kind, axes, g, me, x_ref, o_ref, (rs, ag, ssem2, rsem2), ssem, rsem))

    for kind, axes, g, me, x_ref, o_ref, slots, ssem, rsem in pending:
        if kind == "rsag":
            rs, ag, ssem2, rsem2 = slots
            c = rs.shape[1]
        else:
            rs = slots

        def wait(k, cc, x_ref=x_ref, rs=rs, ssem=ssem, rsem=rsem, axes=axes, g=g, me=me, kind=kind):
            src = (me + g - k) % g
            peer = (me + k) % g
            if kind == "rsag":
                c = rs.shape[1]
                src_ref = x_ref.at[pl.ds(0, c)]
            else:
                src_ref = x_ref
            pltpu.make_async_remote_copy(
                src_ref=src_ref, dst_ref=rs.at[src], send_sem=ssem.at[peer], recv_sem=rsem.at[src],
                device_id=member_coords(axes, peer), device_id_type=MESH).wait_recv()
            pltpu.make_async_remote_copy(
                src_ref=src_ref, dst_ref=rs.at[me], send_sem=ssem.at[peer], recv_sem=rsem.at[me],
                device_id=member_coords(axes, peer), device_id_type=MESH).wait_send()
            return cc

        lax.fori_loop(1, g, wait, 0)
        if kind == "gather":
            o_ref[...] = rs[...]
        elif kind == "sum":
            acc = rs[0]
            for s in range(1, g):
                acc = acc + rs[s]
            o_ref[...] = acc
        else:
            acc = rs[0]
            for s in range(1, g):
                acc = acc + rs[s]
            ag[me] = acc

            def send2(k, cc, ag=ag, ssem2=ssem2, rsem2=rsem2, axes=axes, g=g, me=me):
                peer = (me + k) % g
                pltpu.make_async_remote_copy(
                    src_ref=ag.at[me], dst_ref=ag.at[me], send_sem=ssem2.at[peer], recv_sem=rsem2.at[me],
                    device_id=member_coords(axes, peer), device_id_type=MESH).start()
                return cc

            lax.fori_loop(1, g, send2, 0)

            def wait2(k, cc, ag=ag, ssem2=ssem2, rsem2=rsem2, axes=axes, g=g, me=me):
                src = (me + g - k) % g
                peer = (me + k) % g
                pltpu.make_async_remote_copy(
                    src_ref=ag.at[me], dst_ref=ag.at[src], send_sem=ssem2.at[peer], recv_sem=rsem2.at[src],
                    device_id=member_coords(axes, peer), device_id_type=MESH).wait_recv()
                pltpu.make_async_remote_copy(
                    src_ref=ag.at[me], dst_ref=ag.at[me], send_sem=ssem2.at[peer], recv_sem=rsem2.at[me],
                    device_id=member_coords(axes, peer), device_id_type=MESH).wait_send()
                return cc

            lax.fori_loop(1, g, wait2, 0)
            o_ref[...] = ag[...]


def chol_kernel(g_ref, l_ref, inv_ref):
    a = g_ref[...]
    n = a.shape[0]
    rows = lax.broadcasted_iota(jnp.int32, (n, n), 0)
    lanes = lax.broadcasted_iota(jnp.int32, (n, n), 1)
    eye = (rows == lanes).astype(jnp.float32)
    x = eye
    lmat = jnp.zeros_like(a)
    for j in range(n):
        d = jnp.sqrt(a[j:j + 1, j:j + 1])
        col = jnp.where(rows[:, j:j + 1] >= j, a[:, j:j + 1], 0.0) / d
        rowv = jnp.sum(eye * col, axis=0, keepdims=True)
        a = a - col * rowv
        lmat = jnp.where(lanes == j, col, lmat)
        xj = x[j:j + 1, :] / d
        below = jnp.where(rows[:, j:j + 1] > j, col, 0.0)
        x = jnp.where(rows == j, xj, x - below * xj)
    l_ref[...] = lmat
    inv_ref[...] = x

def chol_inv(gram):
    n = gram.shape[0]
    return pl.pallas_call(chol_kernel,
        out_shape=[jax.ShapeDtypeStruct((n, n), jnp.float32)] * 2,
        in_specs=[pl.BlockSpec(memory_space=pltpu.VMEM)],
        out_specs=[pl.BlockSpec(memory_space=pltpu.VMEM)] * 2)(gram)


_IDS = {}


def exchange(ops, xs):
    key = ("direct",) + tuple((k, d, x.shape, str(x.dtype)) for (k, d), x in zip(ops, xs))
    if key not in _IDS:
        _IDS[key] = len(_IDS)
    groups = []
    for _, axes in ops:
        if axes not in groups:
            groups.append(axes)
    out_shapes, scratch = [], []
    for (kind, axes), x in zip(ops, xs):
        g = group_size(axes)
        if kind == "sum":
            out_shapes.append(jax.ShapeDtypeStruct(x.shape, x.dtype))
            scratch += [pltpu.VMEM((g,) + x.shape, x.dtype), pltpu.SemaphoreType.DMA((g,)),
                        pltpu.SemaphoreType.DMA((g,))]
        else:
            c = x.shape[0] // g
            out_shapes.append(jax.ShapeDtypeStruct((g, c) + x.shape[1:], x.dtype))
            scratch += [pltpu.VMEM((g, c) + x.shape[1:], x.dtype), pltpu.VMEM((g, c) + x.shape[1:], x.dtype),
                        pltpu.SemaphoreType.DMA((g,)), pltpu.SemaphoreType.DMA((g,)),
                        pltpu.SemaphoreType.DMA((g,)), pltpu.SemaphoreType.DMA((g,))]
    outs = pl.pallas_call(
        functools.partial(direct_kernel, ops, groups),
        out_shape=out_shapes,
        in_specs=[pl.BlockSpec(memory_space=pltpu.VMEM)] * len(xs),
        out_specs=[pl.BlockSpec(memory_space=pltpu.VMEM)] * len(xs),
        scratch_shapes=scratch,
        compiler_params=pltpu.CompilerParams(collective_id=_IDS[key], has_side_effects=True),
    )(*xs)
    return [o.reshape(x.shape) for o, x in zip(outs, xs)]


def exchange_bfly(ops, xs):
    key = ("bfly",) + tuple((k, d, x.shape, str(x.dtype)) for (k, d), x in zip(ops, xs))
    if key not in _IDS:
        _IDS[key] = len(_IDS)
    out_shapes, scratch = [], []
    for (kind, digits), x in zip(ops, xs):
        g = group_size(digits)
        L = op_rounds(kind, g)
        if kind == "gather":
            out_shapes.append(jax.ShapeDtypeStruct((g,) + x.shape, x.dtype))
            scratch += [pltpu.VMEM((g,) + x.shape, x.dtype), pltpu.VMEM((8, 128), jnp.float32)]
        elif kind == "sum":
            out_shapes.append(jax.ShapeDtypeStruct(x.shape, x.dtype))
            scratch += [pltpu.VMEM(x.shape, x.dtype), pltpu.VMEM((L,) + x.shape, x.dtype)]
        else:
            out_shapes.append(jax.ShapeDtypeStruct(x.shape, x.dtype))
            scratch += [pltpu.VMEM(x.shape, x.dtype),
                        pltpu.VMEM((L // 2, x.shape[0] // 2) + x.shape[1:], x.dtype),
                        pltpu.VMEM(x.shape, x.dtype)]
        scratch += [pltpu.SemaphoreType.DMA((L,)), pltpu.SemaphoreType.DMA((L,))]
    outs = pl.pallas_call(
        functools.partial(exchange_kernel, ops),
        out_shape=out_shapes,
        in_specs=[pl.BlockSpec(memory_space=pltpu.VMEM)] * len(xs),
        out_specs=[pl.BlockSpec(memory_space=pltpu.VMEM)] * len(xs),
        scratch_shapes=scratch,
        compiler_params=pltpu.CompilerParams(collective_id=_IDS[key], has_side_effects=True),
    )(*xs)
    return list(outs)


def make_local(sizes, row_axes, col_axes):
    def local(particles, start_basis):
        shard = particles.shape[0]
        width = particles.shape[1]
        eig = start_basis.shape[1]
        total = shard * math.prod(sizes.values())
        spread = 2.0 * width
        root_total = math.sqrt(float(total))

        dense_basis = start_basis.reshape(shard * eig // 128, 128)
        i_feats, i_basis, j_feats = exchange_bfly(
            [("gather", row_axes), ("gather", row_axes), ("gather", col_axes)],
            [particles, dense_basis, particles])
        gi = group_size(row_axes)
        gj = group_size(col_axes)
        i_feats = i_feats.reshape(gi * shard, width)
        j_feats = j_feats.reshape(gj * shard, width)
        basis_i = i_basis.reshape(gi * shard, eig)

        def block_ids(digits):
            coords = member_coords(digits, jnp.arange(group_size(digits), dtype=jnp.int32))
            flat = jnp.zeros((group_size(digits),), jnp.int32)
            for a, cval in zip(MESH_AXES, coords):
                flat = flat * sizes[a] + cval
            return (flat[:, None] * shard + jnp.arange(shard, dtype=jnp.int32)[None, :]).reshape(-1)

        ids_i = block_ids(row_axes)
        ids_j = block_ids(col_axes)
        sq_i = jnp.sum(jnp.square(i_feats.astype(jnp.float32)), axis=1)
        sq_j = jnp.sum(jnp.square(j_feats.astype(jnp.float32)), axis=1)
        dots = lax.dot_general(i_feats, j_feats, (((1,), (1,)), ((), ())), preferred_element_type=jnp.float32)
        distance = sq_i[:, None] + sq_j[None, :] - 2.0 * dots
        tile = jnp.where(ids_i[:, None] == ids_j[None, :], jnp.float32(0.0), jnp.exp(-distance / spread))

        deg_i, deg_j = exchange(
            [("sum", row_axes), ("sum", col_axes)],
            [jnp.sum(tile, axis=1).reshape(-1, 128), jnp.sum(tile, axis=0).reshape(-1, 128)])
        deg_i = deg_i.reshape(-1)
        deg_j = deg_j.reshape(-1)
        root_i = jnp.sqrt(deg_i)
        root_j = jnp.sqrt(deg_j)
        me_i = group_pos(row_axes)
        scaled_i = basis_i / root_i[:, None]
        prod_j = lax.dot_general(tile, scaled_i, (((0,), (0,)), ((), ())), precision=HIGH)
        extra = jnp.concatenate([jnp.dot(root_i, basis_i, precision=HIGH)[None, :],
                                 jnp.broadcast_to(jnp.sum(deg_i), (1, eig)),
                                 jnp.zeros((6, eig), jnp.float32)], axis=0)
        dense_j, extra = exchange(
            [("rsag", col_axes), ("sum", col_axes)], [prod_j.reshape(-1, 128), extra.reshape(-1, 128)])
        prod_j = dense_j.reshape(-1, eig)
        extra = extra.reshape(-1, eig)
        inv_s = 1.0 / jnp.sqrt(extra[1, 0])
        aligned = extra[0] * inv_s
        defl_j = prod_j / root_j[:, None] - (root_j * inv_s)[:, None] * aligned[None, :]

        gram = lax.dot_general(defl_j, defl_j, (((0,), (0,)), ((), ())), precision=HIGH).reshape(-1, 128)
        q_i = jnp.dot(tile, defl_j / root_j[:, None], precision=HIGH)
        part = jnp.concatenate([jnp.dot(root_j, defl_j, precision=HIGH)[None, :],
                                jnp.zeros((7, eig), jnp.float32)], axis=0)
        gram, q_i, part = exchange(
            [("rsag", row_axes), ("rsag", row_axes), ("sum", row_axes)],
            [gram, q_i.reshape(-1, 128), part.reshape(-1, 128)])
        factor, inverse = chol_inv(gram.reshape(eig, eig))
        q_i = q_i.reshape(-1, eig)
        part = part.reshape(-1, eig)
        prod_i = lax.dot_general(q_i, inverse, (((1,), (1,)), ((), ())), precision=HIGH) * root_total
        aligned = jnp.dot(inverse, part[0], precision=HIGH) * (root_total * inv_s)
        defl_i = prod_i / root_i[:, None] - (root_i * inv_s)[:, None] * aligned[None, :]

        gram = lax.dot_general(defl_i, defl_i, (((0,), (0,)), ((), ())), precision=HIGH).reshape(-1, 128)
        (gram,) = exchange([("sum", col_axes)], [gram])
        factor, inverse = chol_inv(gram.reshape(eig, eig))
        own = lax.dynamic_slice_in_dim(defl_i, me_i * shard, shard, 0)
        basis_own = lax.dot_general(own, inverse, (((1,), (1,)), ((), ())), precision=HIGH) * root_total
        return basis_own, factor

    return local


def bit_digits(outer, outer_size, inner, inner_size):
    digits = []
    if outer is not None:
        digits.append((outer, 1, 2))
    digits += [(inner, 1 << k, 2) for k in range(inner_size.bit_length() - 1)]
    if outer is not None:
        digits += [(outer, 2 << k, 2) for k in range((outer_size // 2).bit_length() - 1)]
    return tuple(digits)


def solution(mesh):
    sizes = dict(mesh.shape)
    placed = (P(MESH_AXES, None), P(MESH_AXES, None))
    return jax.shard_map(
        make_local(sizes, bit_digits("row", sizes["row"], "vec", sizes["vec"]), bit_digits(None, 1, "col", sizes["col"])),
        mesh=mesh,
        in_specs=placed,
        out_specs=(P(MESH_AXES, None), P()),
        check_vma=False,
    )
```

```python
import functools
import math

import jax
import jax.numpy as jnp
from jax import lax
from jax.experimental import pallas as pl
from jax.experimental.pallas import tpu as pltpu
from jax.sharding import PartitionSpec as P

ITERS = 2
MESH_AXES = ("row", "col", "vec")
MESH = pl.DeviceIdType.MESH
HIGH = lax.Precision.HIGHEST


def group_pos(digits):
    me = 0
    for a, div, mod in digits:
        me = me * mod + (lax.axis_index(a) // div) % mod
    return me


def group_size(digits):
    return math.prod(mod for _, _, mod in digits)


def member_coords(digits, m):
    own = {a: lax.axis_index(a) for a in MESH_AXES}
    coords = dict(own)
    rem = m
    for a, div, mod in reversed(digits):
        d = rem % mod
        rem = rem // mod
        coords[a] = coords[a] - ((own[a] // div) % mod) * div + d * div
    return tuple(coords[a] for a in MESH_AXES)


def flip(me, b):
    return me + (1 - 2 * ((me // (1 << b)) % 2)) * (1 << b)


def op_rounds(kind, g):
    bits = g.bit_length() - 1
    return 2 * bits if kind == "rsag" else bits


def exchange_kernel(ops, *refs):
    n = len(ops)
    ins, outs, scr = refs[:n], refs[n:2 * n], refs[2 * n:]
    barrier = pltpu.get_barrier_semaphore()
    groups = []
    for _, digits in ops:
        if digits not in groups:
            groups.append(digits)
    count = 0
    for digits in groups:
        g = group_size(digits)
        me = group_pos(digits)
        for b in range(g.bit_length() - 1):
            pl.semaphore_signal(barrier, inc=1, device_id=member_coords(digits, flip(me, b)), device_id_type=MESH)
            count += 1
    pl.semaphore_wait(barrier, count)

    state = []
    pos = 0
    for i, (kind, digits) in enumerate(ops):
        x_ref = ins[i]
        if kind == "rsag":
            w, r, gat, ssem, rsem = scr[pos:pos + 5]
            pos += 5
            r = (r, gat)
        else:
            w, r, ssem, rsem = scr[pos:pos + 4]
            pos += 4
        if kind == "gather":
            w[group_pos(digits)] = x_ref[...]
        else:
            w[...] = x_ref[...]
        state.append((w, r, ssem, rsem))

    nrounds = max(op_rounds(kind, group_size(d)) for kind, d in ops)
    for t in range(nrounds):
        copies = []
        for i, (kind, digits) in enumerate(ops):
            g = group_size(digits)
            bits = g.bit_length() - 1
            if t >= op_rounds(kind, g):
                continue
            me = group_pos(digits)
            w, r, ssem, rsem = state[i]
            if kind == "gather":
                b = t
                partner = flip(me, b)
                span = 1 << b
                mine = pl.ds((me // span) * span, span)
                theirs = pl.ds((partner // span) * span, span)
                src, dst, land = w.at[mine], w.at[mine], w.at[theirs]
            elif kind == "sum":
                b = t
                partner = flip(me, b)
                src, dst, land = w, r.at[t], r.at[t]
            elif t < bits:
                r = r[0]
                b = bits - 1 - t
                partner = flip(me, b)
                size = w.shape[0] >> (t + 1)
                theirs = pl.ds(pl.multiple_of((partner // (1 << b)) * size, size), size)
                src, dst, land = w.at[theirs], r.at[t, pl.ds(0, size)], r.at[t, pl.ds(0, size)]
            else:
                u = t - bits
                b = u
                partner = flip(me, b)
                gat = r[1]
                size = (w.shape[0] // g) << u
                if u == 0:
                    gat[pl.ds(pl.multiple_of(me * size, size), size)] = w[pl.ds(pl.multiple_of(me * size, size), size)]
                mine = pl.ds(pl.multiple_of((me // (1 << u)) * size, size), size)
                theirs = pl.ds(pl.multiple_of((partner // (1 << u)) * size, size), size)
                src, dst, land = gat.at[mine], gat.at[mine], gat.at[theirs]
            dev = member_coords(digits, partner)
            out = pltpu.make_async_remote_copy(
                src_ref=src, dst_ref=dst, send_sem=ssem.at[t], recv_sem=rsem.at[t],
                device_id=dev, device_id_type=MESH)
            out.start()
            back = pltpu.make_async_remote_copy(
                src_ref=src, dst_ref=land, send_sem=ssem.at[t], recv_sem=rsem.at[t],
                device_id=dev, device_id_type=MESH)
            copies.append((i, kind, t, bits, out, back, me))
        for i, kind, t, bits, out, back, me in copies:
            back.wait_recv()
            out.wait_send()
            w, r, ssem, rsem = state[i]
            if kind == "sum":
                w[...] = w[...] + r[t]
            elif kind == "rsag" and t < bits:
                b = bits - 1 - t
                size = w.shape[0] >> (t + 1)
                mine = pl.ds(pl.multiple_of((me // (1 << b)) * size, size), size)
                w[mine] = w[mine] + r[0][t, pl.ds(0, size)]
    for i, (kind, _) in enumerate(ops):
        outs[i][...] = state[i][1][1][...] if kind == "rsag" else state[i][0][...]


def direct_kernel(ops, groups, *refs):
    n = len(ops)
    ins, outs, scr = refs[:n], refs[n:2 * n], refs[2 * n:]
    barrier = pltpu.get_barrier_semaphore()
    total_peers = 0
    for axes in groups:
        g = group_size(axes)
        me = group_pos(axes)
        total_peers += g - 1

        def greet(k, c, axes=axes, g=g, me=me):
            pl.semaphore_signal(barrier, inc=1, device_id=member_coords(axes, (me + k) % g), device_id_type=MESH)
            return c

        lax.fori_loop(1, g, greet, 0)
    pl.semaphore_wait(barrier, total_peers)

    pos = 0
    pending = []
    for i, (kind, axes) in enumerate(ops):
        g = group_size(axes)
        me = group_pos(axes)
        x_ref, o_ref = ins[i], outs[i]
        if kind in ("gather", "sum"):
            slots, ssem, rsem = scr[pos:pos + 3]
            pos += 3
            slots[me] = x_ref[...]

            def send(k, c, x_ref=x_ref, slots=slots, ssem=ssem, rsem=rsem, axes=axes, g=g, me=me):
                peer = (me + k) % g
                pltpu.make_async_remote_copy(
                    src_ref=x_ref, dst_ref=slots.at[me], send_sem=ssem.at[peer], recv_sem=rsem.at[me],
                    device_id=member_coords(axes, peer), device_id_type=MESH).start()
                return c

            lax.fori_loop(1, g, send, 0)
            pending.append((kind, axes, g, me, x_ref, o_ref, slots, ssem, rsem))
        else:
            rs, ag, ssem, rsem, ssem2, rsem2 = scr[pos:pos + 6]
            pos += 6
            c = x_ref.shape[0] // g
            rs[me] = x_ref[pl.ds(pl.multiple_of(me * c, c), c)]

            def send(k, cc, x_ref=x_ref, rs=rs, ssem=ssem, rsem=rsem, axes=axes, g=g, me=me, c=c):
                peer = (me + k) % g
                pltpu.make_async_remote_copy(
                    src_ref=x_ref.at[pl.ds(pl.multiple_of(peer * c, c), c)], dst_ref=rs.at[me],
                    send_sem=ssem.at[peer], recv_sem=rsem.at[me],
                    device_id=member_coords(axes, peer), device_id_type=MESH).start()
                return cc

            lax.fori_loop(1, g, send, 0)
            pending.append((kind, axes, g, me, x_ref, o_ref, (rs, ag, ssem2, rsem2), ssem, rsem))

    for kind, axes, g, me, x_ref, o_ref, slots, ssem, rsem in pending:
        if kind == "rsag":
            rs, ag, ssem2, rsem2 = slots
            c = rs.shape[1]
        else:
            rs = slots

        def wait(k, cc, x_ref=x_ref, rs=rs, ssem=ssem, rsem=rsem, axes=axes, g=g, me=me, kind=kind):
            src = (me + g - k) % g
            peer = (me + k) % g
            if kind == "rsag":
                c = rs.shape[1]
                src_ref = x_ref.at[pl.ds(0, c)]
            else:
                src_ref = x_ref
            pltpu.make_async_remote_copy(
                src_ref=src_ref, dst_ref=rs.at[src], send_sem=ssem.at[peer], recv_sem=rsem.at[src],
                device_id=member_coords(axes, peer), device_id_type=MESH).wait_recv()
            pltpu.make_async_remote_copy(
                src_ref=src_ref, dst_ref=rs.at[me], send_sem=ssem.at[peer], recv_sem=rsem.at[me],
                device_id=member_coords(axes, peer), device_id_type=MESH).wait_send()
            return cc

        lax.fori_loop(1, g, wait, 0)
        if kind == "gather":
            o_ref[...] = rs[...]
        elif kind == "sum":
            acc = rs[0]
            for s in range(1, g):
                acc = acc + rs[s]
            o_ref[...] = acc
        else:
            acc = rs[0]
            for s in range(1, g):
                acc = acc + rs[s]
            ag[me] = acc

            def send2(k, cc, ag=ag, ssem2=ssem2, rsem2=rsem2, axes=axes, g=g, me=me):
                peer = (me + k) % g
                pltpu.make_async_remote_copy(
                    src_ref=ag.at[me], dst_ref=ag.at[me], send_sem=ssem2.at[peer], recv_sem=rsem2.at[me],
                    device_id=member_coords(axes, peer), device_id_type=MESH).start()
                return cc

            lax.fori_loop(1, g, send2, 0)

            def wait2(k, cc, ag=ag, ssem2=ssem2, rsem2=rsem2, axes=axes, g=g, me=me):
                src = (me + g - k) % g
                peer = (me + k) % g
                pltpu.make_async_remote_copy(
                    src_ref=ag.at[me], dst_ref=ag.at[src], send_sem=ssem2.at[peer], recv_sem=rsem2.at[src],
                    device_id=member_coords(axes, peer), device_id_type=MESH).wait_recv()
                pltpu.make_async_remote_copy(
                    src_ref=ag.at[me], dst_ref=ag.at[me], send_sem=ssem2.at[peer], recv_sem=rsem2.at[me],
                    device_id=member_coords(axes, peer), device_id_type=MESH).wait_send()
                return cc

            lax.fori_loop(1, g, wait2, 0)
            o_ref[...] = ag[...]


def chol_kernel(g_ref, l_ref, inv_ref):
    a = g_ref[...]
    n = a.shape[0]
    rows = lax.broadcasted_iota(jnp.int32, (n, n), 0)
    lanes = lax.broadcasted_iota(jnp.int32, (n, n), 1)
    eye = (rows == lanes).astype(jnp.float32)
    x = eye
    lmat = jnp.zeros_like(a)
    for j in range(n):
        d = jnp.sqrt(a[j:j + 1, j:j + 1])
        col = jnp.where(rows[:, j:j + 1] >= j, a[:, j:j + 1], 0.0) / d
        rowv = jnp.sum(eye * col, axis=0, keepdims=True)
        a = a - col * rowv
        lmat = jnp.where(lanes == j, col, lmat)
        xj = x[j:j + 1, :] / d
        below = jnp.where(rows[:, j:j + 1] > j, col, 0.0)
        x = jnp.where(rows == j, xj, x - below * xj)
    l_ref[...] = lmat
    inv_ref[...] = x

def chol_inv(gram):
    n = gram.shape[0]
    return pl.pallas_call(chol_kernel,
        out_shape=[jax.ShapeDtypeStruct((n, n), jnp.float32)] * 2,
        in_specs=[pl.BlockSpec(memory_space=pltpu.VMEM)],
        out_specs=[pl.BlockSpec(memory_space=pltpu.VMEM)] * 2)(gram)


_IDS = {}


def exchange(ops, xs):
    key = ("direct",) + tuple((k, d, x.shape, str(x.dtype)) for (k, d), x in zip(ops, xs))
    if key not in _IDS:
        _IDS[key] = len(_IDS)
    groups = []
    for _, axes in ops:
        if axes not in groups:
            groups.append(axes)
    out_shapes, scratch = [], []
    for (kind, axes), x in zip(ops, xs):
        g = group_size(axes)
        if kind == "sum":
            out_shapes.append(jax.ShapeDtypeStruct(x.shape, x.dtype))
            scratch += [pltpu.VMEM((g,) + x.shape, x.dtype), pltpu.SemaphoreType.DMA((g,)),
                        pltpu.SemaphoreType.DMA((g,))]
        else:
            c = x.shape[0] // g
            out_shapes.append(jax.ShapeDtypeStruct((g, c) + x.shape[1:], x.dtype))
            scratch += [pltpu.VMEM((g, c) + x.shape[1:], x.dtype), pltpu.VMEM((g, c) + x.shape[1:], x.dtype),
                        pltpu.SemaphoreType.DMA((g,)), pltpu.SemaphoreType.DMA((g,)),
                        pltpu.SemaphoreType.DMA((g,)), pltpu.SemaphoreType.DMA((g,))]
    outs = pl.pallas_call(
        functools.partial(direct_kernel, ops, groups),
        out_shape=out_shapes,
        in_specs=[pl.BlockSpec(memory_space=pltpu.VMEM)] * len(xs),
        out_specs=[pl.BlockSpec(memory_space=pltpu.VMEM)] * len(xs),
        scratch_shapes=scratch,
        compiler_params=pltpu.CompilerParams(collective_id=_IDS[key], has_side_effects=True),
    )(*xs)
    return [o.reshape(x.shape) for o, x in zip(outs, xs)]


def exchange_bfly(ops, xs):
    key = ("bfly",) + tuple((k, d, x.shape, str(x.dtype)) for (k, d), x in zip(ops, xs))
    if key not in _IDS:
        _IDS[key] = len(_IDS)
    out_shapes, scratch = [], []
    for (kind, digits), x in zip(ops, xs):
        g = group_size(digits)
        L = op_rounds(kind, g)
        if kind == "gather":
            out_shapes.append(jax.ShapeDtypeStruct((g,) + x.shape, x.dtype))
            scratch += [pltpu.VMEM((g,) + x.shape, x.dtype), pltpu.VMEM((8, 128), jnp.float32)]
        elif kind == "sum":
            out_shapes.append(jax.ShapeDtypeStruct(x.shape, x.dtype))
            scratch += [pltpu.VMEM(x.shape, x.dtype), pltpu.VMEM((L,) + x.shape, x.dtype)]
        else:
            out_shapes.append(jax.ShapeDtypeStruct(x.shape, x.dtype))
            scratch += [pltpu.VMEM(x.shape, x.dtype),
                        pltpu.VMEM((L // 2, x.shape[0] // 2) + x.shape[1:], x.dtype),
                        pltpu.VMEM(x.shape, x.dtype)]
        scratch += [pltpu.SemaphoreType.DMA((L,)), pltpu.SemaphoreType.DMA((L,))]
    outs = pl.pallas_call(
        functools.partial(exchange_kernel, ops),
        out_shape=out_shapes,
        in_specs=[pl.BlockSpec(memory_space=pltpu.VMEM)] * len(xs),
        out_specs=[pl.BlockSpec(memory_space=pltpu.VMEM)] * len(xs),
        scratch_shapes=scratch,
        compiler_params=pltpu.CompilerParams(collective_id=_IDS[key], has_side_effects=True),
    )(*xs)
    return list(outs)


def make_local(sizes, row_axes, col_axes):
    def local(particles, start_basis):
        shard = particles.shape[0]
        width = particles.shape[1]
        eig = start_basis.shape[1]
        total = shard * math.prod(sizes.values())
        spread = 2.0 * width
        root_total = math.sqrt(float(total))

        dense_basis = start_basis.reshape(shard * eig // 128, 128)
        i_feats, i_basis, j_feats = exchange_bfly(
            [("gather", row_axes), ("gather", row_axes), ("gather", col_axes)],
            [particles, dense_basis, particles])
        gi = group_size(row_axes)
        gj = group_size(col_axes)
        i_feats = i_feats.reshape(gi * shard, width)
        j_feats = j_feats.reshape(gj * shard, width)
        basis_i = i_basis.reshape(gi * shard, eig)

        def block_ids(digits):
            coords = member_coords(digits, jnp.arange(group_size(digits), dtype=jnp.int32))
            flat = jnp.zeros((group_size(digits),), jnp.int32)
            for a, cval in zip(MESH_AXES, coords):
                flat = flat * sizes[a] + cval
            return (flat[:, None] * shard + jnp.arange(shard, dtype=jnp.int32)[None, :]).reshape(-1)

        ids_i = block_ids(row_axes)
        ids_j = block_ids(col_axes)
        sq_i = jnp.sum(jnp.square(i_feats.astype(jnp.float32)), axis=1)
        sq_j = jnp.sum(jnp.square(j_feats.astype(jnp.float32)), axis=1)
        dots = lax.dot_general(i_feats, j_feats, (((1,), (1,)), ((), ())), preferred_element_type=jnp.float32)
        distance = sq_i[:, None] + sq_j[None, :] - 2.0 * dots
        tile = jnp.where(ids_i[:, None] == ids_j[None, :], jnp.float32(0.0), jnp.exp(-distance / spread))

        deg_i, deg_j = exchange(
            [("sum", row_axes), ("sum", col_axes)],
            [jnp.sum(tile, axis=1).reshape(-1, 128), jnp.sum(tile, axis=0).reshape(-1, 128)])
        deg_i = deg_i.reshape(-1)
        deg_j = deg_j.reshape(-1)
        root_i = jnp.sqrt(deg_i)
        root_j = jnp.sqrt(deg_j)
        me_i = group_pos(row_axes)
        scaled_i = basis_i / root_i[:, None]
        prod_j = lax.dot_general(tile, scaled_i, (((0,), (0,)), ((), ())), precision=HIGH)
        extra = jnp.concatenate([jnp.dot(root_i, basis_i, precision=HIGH)[None, :],
                                 jnp.broadcast_to(jnp.sum(deg_i), (1, eig)),
                                 jnp.zeros((6, eig), jnp.float32)], axis=0)
        dense_j, extra = exchange(
            [("rsag", col_axes), ("sum", col_axes)], [prod_j.reshape(-1, 128), extra.reshape(-1, 128)])
        prod_j = dense_j.reshape(-1, eig)
        extra = extra.reshape(-1, eig)
        inv_s = 1.0 / jnp.sqrt(extra[1, 0])
        aligned = extra[0] * inv_s
        defl_j = prod_j / root_j[:, None] - (root_j * inv_s)[:, None] * aligned[None, :]

        gram = lax.dot_general(defl_j, defl_j, (((0,), (0,)), ((), ())), precision=HIGH).reshape(-1, 128)
        q_i = jnp.dot(tile, defl_j / root_j[:, None], precision=HIGH)
        aligned_part = jnp.pad(jnp.dot(root_j, defl_j, precision=HIGH), (0, 128 - eig))[None, :]
        small = jnp.concatenate([gram, aligned_part,
                                 jnp.zeros((2 * gi - gram.shape[0] - 1, 128), jnp.float32)], axis=0)
        small, q_i = exchange([("rsag", row_axes), ("rsag", row_axes)], [small, q_i.reshape(-1, 128)])
        gram = small[:eig * eig // 128]
        part = small[eig * eig // 128:][:1, :eig]
        factor, inverse = chol_inv(gram.reshape(eig, eig))
        q_i = q_i.reshape(-1, eig)
        prod_i = lax.dot_general(q_i, inverse, (((1,), (1,)), ((), ())), precision=HIGH) * root_total
        aligned = jnp.dot(inverse, part[0], precision=HIGH) * (root_total * inv_s)
        defl_i = prod_i / root_i[:, None] - (root_i * inv_s)[:, None] * aligned[None, :]

        gram = lax.dot_general(defl_i, defl_i, (((0,), (0,)), ((), ())), precision=HIGH).reshape(-1, 128)
        (gram,) = exchange([("sum", col_axes)], [gram])
        factor, inverse = chol_inv(gram.reshape(eig, eig))
        own = lax.dynamic_slice_in_dim(defl_i, me_i * shard, shard, 0)
        basis_own = lax.dot_general(own, inverse, (((1,), (1,)), ((), ())), precision=HIGH) * root_total
        return basis_own, factor

    return local


def bit_digits(outer, outer_size, inner, inner_size):
    digits = []
    if outer is not None:
        digits.append((outer, 1, 2))
    digits += [(inner, 1 << k, 2) for k in range(inner_size.bit_length() - 1)]
    if outer is not None:
        digits += [(outer, 2 << k, 2) for k in range((outer_size // 2).bit_length() - 1)]
    return tuple(digits)


def solution(mesh):
    sizes = dict(mesh.shape)
    placed = (P(MESH_AXES, None), P(MESH_AXES, None))
    return jax.shard_map(
        make_local(sizes, bit_digits("row", sizes["row"], "vec", sizes["vec"]), bit_digits(None, 1, "col", sizes["col"])),
        mesh=mesh,
        in_specs=placed,
        out_specs=(P(MESH_AXES, None), P()),
        check_vma=False,
    )
```

```python
import functools
import math

import jax
import jax.numpy as jnp
from jax import lax
from jax.experimental import pallas as pl
from jax.experimental.pallas import tpu as pltpu
from jax.sharding import PartitionSpec as P

ITERS = 2
MESH_AXES = ("row", "col", "vec")
MESH = pl.DeviceIdType.MESH
HIGH = lax.Precision.HIGHEST


def group_pos(digits):
    me = 0
    for a, div, mod in digits:
        me = me * mod + (lax.axis_index(a) // div) % mod
    return me


def group_size(digits):
    return math.prod(mod for _, _, mod in digits)


def member_coords(digits, m):
    own = {a: lax.axis_index(a) for a in MESH_AXES}
    coords = dict(own)
    rem = m
    for a, div, mod in reversed(digits):
        d = rem % mod
        rem = rem // mod
        coords[a] = coords[a] - ((own[a] // div) % mod) * div + d * div
    return tuple(coords[a] for a in MESH_AXES)


def flip(me, b):
    return me + (1 - 2 * ((me // (1 << b)) % 2)) * (1 << b)


def op_rounds(kind, g):
    bits = g.bit_length() - 1
    return 2 * bits if kind == "rsag" else bits


def exchange_kernel(ops, *refs):
    n = len(ops)
    ins, outs, scr = refs[:n], refs[n:2 * n], refs[2 * n:]
    barrier = pltpu.get_barrier_semaphore()
    groups = []
    for _, digits in ops:
        if digits not in groups:
            groups.append(digits)
    count = 0
    for digits in groups:
        g = group_size(digits)
        me = group_pos(digits)
        for b in range(g.bit_length() - 1):
            pl.semaphore_signal(barrier, inc=1, device_id=member_coords(digits, flip(me, b)), device_id_type=MESH)
            count += 1
    pl.semaphore_wait(barrier, count)

    state = []
    pos = 0
    for i, (kind, digits) in enumerate(ops):
        x_ref = ins[i]
        if kind == "rsag":
            w, r, gat, ssem, rsem = scr[pos:pos + 5]
            pos += 5
            r = (r, gat)
        else:
            w, r, ssem, rsem = scr[pos:pos + 4]
            pos += 4
        if kind == "gather":
            w[group_pos(digits)] = x_ref[...]
        else:
            w[...] = x_ref[...]
        state.append((w, r, ssem, rsem))

    nrounds = max(op_rounds(kind, group_size(d)) for kind, d in ops)
    for t in range(nrounds):
        copies = []
        for i, (kind, digits) in enumerate(ops):
            g = group_size(digits)
            bits = g.bit_length() - 1
            if t >= op_rounds(kind, g):
                continue
            me = group_pos(digits)
            w, r, ssem, rsem = state[i]
            if kind == "gather":
                b = t
                partner = flip(me, b)
                span = 1 << b
                mine = pl.ds((me // span) * span, span)
                theirs = pl.ds((partner // span) * span, span)
                src, dst, land = w.at[mine], w.at[mine], w.at[theirs]
            elif kind == "sum":
                b = t
                partner = flip(me, b)
                src, dst, land = w, r.at[t], r.at[t]
            elif t < bits:
                r = r[0]
                b = bits - 1 - t
                partner = flip(me, b)
                size = w.shape[0] >> (t + 1)
                theirs = pl.ds(pl.multiple_of((partner // (1 << b)) * size, size), size)
                src, dst, land = w.at[theirs], r.at[t, pl.ds(0, size)], r.at[t, pl.ds(0, size)]
            else:
                u = t - bits
                b = u
                partner = flip(me, b)
                gat = r[1]
                size = (w.shape[0] // g) << u
                if u == 0:
                    gat[pl.ds(pl.multiple_of(me * size, size), size)] = w[pl.ds(pl.multiple_of(me * size, size), size)]
                mine = pl.ds(pl.multiple_of((me // (1 << u)) * size, size), size)
                theirs = pl.ds(pl.multiple_of((partner // (1 << u)) * size, size), size)
                src, dst, land = gat.at[mine], gat.at[mine], gat.at[theirs]
            dev = member_coords(digits, partner)
            out = pltpu.make_async_remote_copy(
                src_ref=src, dst_ref=dst, send_sem=ssem.at[t], recv_sem=rsem.at[t],
                device_id=dev, device_id_type=MESH)
            out.start()
            back = pltpu.make_async_remote_copy(
                src_ref=src, dst_ref=land, send_sem=ssem.at[t], recv_sem=rsem.at[t],
                device_id=dev, device_id_type=MESH)
            copies.append((i, kind, t, bits, out, back, me))
        for i, kind, t, bits, out, back, me in copies:
            back.wait_recv()
            out.wait_send()
            w, r, ssem, rsem = state[i]
            if kind == "sum":
                w[...] = w[...] + r[t]
            elif kind == "rsag" and t < bits:
                b = bits - 1 - t
                size = w.shape[0] >> (t + 1)
                mine = pl.ds(pl.multiple_of((me // (1 << b)) * size, size), size)
                w[mine] = w[mine] + r[0][t, pl.ds(0, size)]
    for i, (kind, _) in enumerate(ops):
        outs[i][...] = state[i][1][1][...] if kind == "rsag" else state[i][0][...]


def direct_kernel(ops, groups, *refs):
    n = len(ops)
    ins, outs, scr = refs[:n], refs[n:2 * n], refs[2 * n:]
    barrier = pltpu.get_barrier_semaphore()
    total_peers = 0
    for axes in groups:
        g = group_size(axes)
        me = group_pos(axes)
        total_peers += g - 1

        def greet(k, c, axes=axes, g=g, me=me):
            pl.semaphore_signal(barrier, inc=1, device_id=member_coords(axes, (me + k) % g), device_id_type=MESH)
            return c

        lax.fori_loop(1, g, greet, 0)
    pl.semaphore_wait(barrier, total_peers)

    pos = 0
    pending = []
    for i, (kind, axes) in enumerate(ops):
        g = group_size(axes)
        me = group_pos(axes)
        x_ref, o_ref = ins[i], outs[i]
        if kind in ("gather", "sum"):
            slots, ssem, rsem = scr[pos:pos + 3]
            pos += 3
            slots[me] = x_ref[...]

            def send(k, c, x_ref=x_ref, slots=slots, ssem=ssem, rsem=rsem, axes=axes, g=g, me=me):
                peer = (me + k) % g
                pltpu.make_async_remote_copy(
                    src_ref=x_ref, dst_ref=slots.at[me], send_sem=ssem.at[peer], recv_sem=rsem.at[me],
                    device_id=member_coords(axes, peer), device_id_type=MESH).start()
                return c

            lax.fori_loop(1, g, send, 0)
            pending.append((kind, axes, g, me, x_ref, o_ref, slots, ssem, rsem))
        else:
            rs, ag, ssem, rsem, ssem2, rsem2 = scr[pos:pos + 6]
            pos += 6
            c = x_ref.shape[0] // g
            rs[me] = x_ref[pl.ds(pl.multiple_of(me * c, c), c)]

            def send(k, cc, x_ref=x_ref, rs=rs, ssem=ssem, rsem=rsem, axes=axes, g=g, me=me, c=c):
                peer = (me + k) % g
                pltpu.make_async_remote_copy(
                    src_ref=x_ref.at[pl.ds(pl.multiple_of(peer * c, c), c)], dst_ref=rs.at[me],
                    send_sem=ssem.at[peer], recv_sem=rsem.at[me],
                    device_id=member_coords(axes, peer), device_id_type=MESH).start()
                return cc

            lax.fori_loop(1, g, send, 0)
            pending.append((kind, axes, g, me, x_ref, o_ref, (rs, ag, ssem2, rsem2), ssem, rsem))

    for kind, axes, g, me, x_ref, o_ref, slots, ssem, rsem in pending:
        if kind == "rsag":
            rs, ag, ssem2, rsem2 = slots
            c = rs.shape[1]
        else:
            rs = slots

        def wait(k, cc, x_ref=x_ref, rs=rs, ssem=ssem, rsem=rsem, axes=axes, g=g, me=me, kind=kind):
            src = (me + g - k) % g
            peer = (me + k) % g
            if kind == "rsag":
                c = rs.shape[1]
                src_ref = x_ref.at[pl.ds(0, c)]
            else:
                src_ref = x_ref
            pltpu.make_async_remote_copy(
                src_ref=src_ref, dst_ref=rs.at[src], send_sem=ssem.at[peer], recv_sem=rsem.at[src],
                device_id=member_coords(axes, peer), device_id_type=MESH).wait_recv()
            pltpu.make_async_remote_copy(
                src_ref=src_ref, dst_ref=rs.at[me], send_sem=ssem.at[peer], recv_sem=rsem.at[me],
                device_id=member_coords(axes, peer), device_id_type=MESH).wait_send()
            return cc

        lax.fori_loop(1, g, wait, 0)
        if kind == "gather":
            o_ref[...] = rs[...]
        elif kind == "sum":
            acc = rs[0]
            for s in range(1, g):
                acc = acc + rs[s]
            o_ref[...] = acc
        else:
            acc = rs[0]
            for s in range(1, g):
                acc = acc + rs[s]
            ag[me] = acc

            def send2(k, cc, ag=ag, ssem2=ssem2, rsem2=rsem2, axes=axes, g=g, me=me):
                peer = (me + k) % g
                pltpu.make_async_remote_copy(
                    src_ref=ag.at[me], dst_ref=ag.at[me], send_sem=ssem2.at[peer], recv_sem=rsem2.at[me],
                    device_id=member_coords(axes, peer), device_id_type=MESH).start()
                return cc

            lax.fori_loop(1, g, send2, 0)

            def wait2(k, cc, ag=ag, ssem2=ssem2, rsem2=rsem2, axes=axes, g=g, me=me):
                src = (me + g - k) % g
                peer = (me + k) % g
                pltpu.make_async_remote_copy(
                    src_ref=ag.at[me], dst_ref=ag.at[src], send_sem=ssem2.at[peer], recv_sem=rsem2.at[src],
                    device_id=member_coords(axes, peer), device_id_type=MESH).wait_recv()
                pltpu.make_async_remote_copy(
                    src_ref=ag.at[me], dst_ref=ag.at[me], send_sem=ssem2.at[peer], recv_sem=rsem2.at[me],
                    device_id=member_coords(axes, peer), device_id_type=MESH).wait_send()
                return cc

            lax.fori_loop(1, g, wait2, 0)
            o_ref[...] = ag[...]


def chol_kernel(g_ref, l_ref, inv_ref):
    a = g_ref[...]
    n = a.shape[0]
    rows = lax.broadcasted_iota(jnp.int32, (n, n), 0)
    lanes = lax.broadcasted_iota(jnp.int32, (n, n), 1)
    eye = (rows == lanes).astype(jnp.float32)
    x = eye
    lmat = jnp.zeros_like(a)
    for j in range(n):
        d = jnp.sqrt(a[j:j + 1, j:j + 1])
        col = jnp.where(rows[:, j:j + 1] >= j, a[:, j:j + 1], 0.0) / d
        rowv = jnp.sum(eye * col, axis=0, keepdims=True)
        a = a - col * rowv
        lmat = jnp.where(lanes == j, col, lmat)
        xj = x[j:j + 1, :] / d
        below = jnp.where(rows[:, j:j + 1] > j, col, 0.0)
        x = jnp.where(rows == j, xj, x - below * xj)
    l_ref[...] = lmat
    inv_ref[...] = x

def chol_inv(gram):
    n = gram.shape[0]
    return pl.pallas_call(chol_kernel,
        out_shape=[jax.ShapeDtypeStruct((n, n), jnp.float32)] * 2,
        in_specs=[pl.BlockSpec(memory_space=pltpu.VMEM)],
        out_specs=[pl.BlockSpec(memory_space=pltpu.VMEM)] * 2)(gram)


_IDS = {}


def exchange(ops, xs):
    key = ("direct",) + tuple((k, d, x.shape, str(x.dtype)) for (k, d), x in zip(ops, xs))
    if key not in _IDS:
        _IDS[key] = len(_IDS)
    groups = []
    for _, axes in ops:
        if axes not in groups:
            groups.append(axes)
    out_shapes, scratch = [], []
    for (kind, axes), x in zip(ops, xs):
        g = group_size(axes)
        if kind == "sum":
            out_shapes.append(jax.ShapeDtypeStruct(x.shape, x.dtype))
            scratch += [pltpu.VMEM((g,) + x.shape, x.dtype), pltpu.SemaphoreType.DMA((g,)),
                        pltpu.SemaphoreType.DMA((g,))]
        else:
            c = x.shape[0] // g
            out_shapes.append(jax.ShapeDtypeStruct((g, c) + x.shape[1:], x.dtype))
            scratch += [pltpu.VMEM((g, c) + x.shape[1:], x.dtype), pltpu.VMEM((g, c) + x.shape[1:], x.dtype),
                        pltpu.SemaphoreType.DMA((g,)), pltpu.SemaphoreType.DMA((g,)),
                        pltpu.SemaphoreType.DMA((g,)), pltpu.SemaphoreType.DMA((g,))]
    outs = pl.pallas_call(
        functools.partial(direct_kernel, ops, groups),
        out_shape=out_shapes,
        in_specs=[pl.BlockSpec(memory_space=pltpu.VMEM)] * len(xs),
        out_specs=[pl.BlockSpec(memory_space=pltpu.VMEM)] * len(xs),
        scratch_shapes=scratch,
        compiler_params=pltpu.CompilerParams(collective_id=_IDS[key], has_side_effects=True),
    )(*xs)
    return [o.reshape(x.shape) for o, x in zip(outs, xs)]


def exchange_bfly(ops, xs):
    key = ("bfly",) + tuple((k, d, x.shape, str(x.dtype)) for (k, d), x in zip(ops, xs))
    if key not in _IDS:
        _IDS[key] = len(_IDS)
    out_shapes, scratch = [], []
    for (kind, digits), x in zip(ops, xs):
        g = group_size(digits)
        L = op_rounds(kind, g)
        if kind == "gather":
            out_shapes.append(jax.ShapeDtypeStruct((g,) + x.shape, x.dtype))
            scratch += [pltpu.VMEM((g,) + x.shape, x.dtype), pltpu.VMEM((8, 128), jnp.float32)]
        elif kind == "sum":
            out_shapes.append(jax.ShapeDtypeStruct(x.shape, x.dtype))
            scratch += [pltpu.VMEM(x.shape, x.dtype), pltpu.VMEM((L,) + x.shape, x.dtype)]
        else:
            out_shapes.append(jax.ShapeDtypeStruct(x.shape, x.dtype))
            scratch += [pltpu.VMEM(x.shape, x.dtype),
                        pltpu.VMEM((L // 2, x.shape[0] // 2) + x.shape[1:], x.dtype),
                        pltpu.VMEM(x.shape, x.dtype)]
        scratch += [pltpu.SemaphoreType.DMA((L,)), pltpu.SemaphoreType.DMA((L,))]
    outs = pl.pallas_call(
        functools.partial(exchange_kernel, ops),
        out_shape=out_shapes,
        in_specs=[pl.BlockSpec(memory_space=pltpu.VMEM)] * len(xs),
        out_specs=[pl.BlockSpec(memory_space=pltpu.VMEM)] * len(xs),
        scratch_shapes=scratch,
        compiler_params=pltpu.CompilerParams(collective_id=_IDS[key], has_side_effects=True),
    )(*xs)
    return list(outs)


def make_local(sizes, row_axes, col_axes):
    def local(particles, start_basis):
        shard = particles.shape[0]
        width = particles.shape[1]
        eig = start_basis.shape[1]
        total = shard * math.prod(sizes.values())
        spread = 2.0 * width
        root_total = math.sqrt(float(total))

        dense_basis = start_basis.reshape(shard * eig // 128, 128)
        i_feats, i_basis, j_feats = exchange_bfly(
            [("gather", row_axes), ("gather", row_axes), ("gather", col_axes)],
            [particles, dense_basis, particles])
        gi = group_size(row_axes)
        gj = group_size(col_axes)
        i_feats = i_feats.reshape(gi * shard, width)
        j_feats = j_feats.reshape(gj * shard, width)
        basis_i = i_basis.reshape(gi * shard, eig)

        def block_ids(digits):
            coords = member_coords(digits, jnp.arange(group_size(digits), dtype=jnp.int32))
            flat = jnp.zeros((group_size(digits),), jnp.int32)
            for a, cval in zip(MESH_AXES, coords):
                flat = flat * sizes[a] + cval
            return (flat[:, None] * shard + jnp.arange(shard, dtype=jnp.int32)[None, :]).reshape(-1)

        ids_i = block_ids(row_axes)
        ids_j = block_ids(col_axes)
        sq_i = jnp.sum(jnp.square(i_feats.astype(jnp.float32)), axis=1)
        sq_j = jnp.sum(jnp.square(j_feats.astype(jnp.float32)), axis=1)
        dots = lax.dot_general(i_feats, j_feats, (((1,), (1,)), ((), ())), preferred_element_type=jnp.float32)
        distance = sq_i[:, None] + sq_j[None, :] - 2.0 * dots
        tile = jnp.where(ids_i[:, None] == ids_j[None, :], jnp.float32(0.0), jnp.exp(-distance / spread))

        deg_i, deg_j = exchange(
            [("sum", row_axes), ("sum", col_axes)],
            [jnp.sum(tile, axis=1).reshape(-1, 128), jnp.sum(tile, axis=0).reshape(-1, 128)])
        deg_i = deg_i.reshape(-1)
        deg_j = deg_j.reshape(-1)
        root_i = jnp.sqrt(deg_i)
        root_j = jnp.sqrt(deg_j)
        me_i = group_pos(row_axes)
        scaled_i = basis_i / root_i[:, None]
        prod_j = lax.dot_general(tile, scaled_i, (((0,), (0,)), ((), ())), precision=HIGH)
        extra = jnp.concatenate([jnp.dot(root_i, basis_i, precision=HIGH)[None, :],
                                 jnp.broadcast_to(jnp.sum(deg_i), (1, eig)),
                                 jnp.zeros((6, eig), jnp.float32)], axis=0)
        dense_j, extra = exchange(
            [("rsag", col_axes), ("sum", col_axes)], [prod_j.reshape(-1, 128), extra.reshape(-1, 128)])
        prod_j = dense_j.reshape(-1, eig)
        extra = extra.reshape(-1, eig)
        inv_s = 1.0 / jnp.sqrt(extra[1, 0])
        aligned = extra[0] * inv_s
        defl_j = prod_j / root_j[:, None] - (root_j * inv_s)[:, None] * aligned[None, :]

        gram = lax.dot_general(defl_j, defl_j, (((0,), (0,)), ((), ())), precision=HIGH).reshape(-1, 128)
        q_i = jnp.dot(tile, defl_j / root_j[:, None], precision=HIGH)
        aligned_part = jnp.pad(jnp.dot(root_j, defl_j, precision=HIGH), (0, 128 - eig))[None, :]
        small = jnp.concatenate([gram, aligned_part,
                                 jnp.zeros((2 * gi - gram.shape[0] - 1, 128), jnp.float32)], axis=0)
        small, q_i = exchange([("rsag", row_axes), ("rsag", row_axes)], [small, q_i.reshape(-1, 128)])
        gram = small[:eig * eig // 128]
        part = small[eig * eig // 128:][:1, :eig]
        factor, inverse = chol_inv(gram.reshape(eig, eig))
        q_i = q_i.reshape(-1, eig)
        prod_i = lax.dot_general(q_i, inverse, (((1,), (1,)), ((), ())), precision=HIGH) * root_total
        aligned = jnp.dot(inverse, part[0], precision=HIGH) * (root_total * inv_s)
        defl_i = prod_i / root_i[:, None] - (root_i * inv_s)[:, None] * aligned[None, :]

        gram = lax.dot_general(defl_i, defl_i, (((0,), (0,)), ((), ())), precision=HIGH).reshape(-1, 128)
        (gram,) = exchange([("rsag", col_axes)], [gram])
        factor, inverse = chol_inv(gram.reshape(eig, eig))
        own = lax.dynamic_slice_in_dim(defl_i, me_i * shard, shard, 0)
        basis_own = lax.dot_general(own, inverse, (((1,), (1,)), ((), ())), precision=HIGH) * root_total
        return basis_own, factor

    return local


def bit_digits(outer, outer_size, inner, inner_size):
    digits = []
    if outer is not None:
        digits.append((outer, 1, 2))
    digits += [(inner, 1 << k, 2) for k in range(inner_size.bit_length() - 1)]
    if outer is not None:
        digits += [(outer, 2 << k, 2) for k in range((outer_size // 2).bit_length() - 1)]
    return tuple(digits)


def solution(mesh):
    sizes = dict(mesh.shape)
    placed = (P(MESH_AXES, None), P(MESH_AXES, None))
    return jax.shard_map(
        make_local(sizes, bit_digits("row", sizes["row"], "vec", sizes["vec"]), bit_digits(None, 1, "col", sizes["col"])),
        mesh=mesh,
        in_specs=placed,
        out_specs=(P(MESH_AXES, None), P()),
        check_vma=False,
    )
```

```python
import functools
import math

import jax
import jax.numpy as jnp
from jax import lax
from jax.experimental import pallas as pl
from jax.experimental.pallas import tpu as pltpu
from jax.sharding import PartitionSpec as P

ITERS = 2
MESH_AXES = ("row", "col", "vec")
MESH = pl.DeviceIdType.MESH
HIGH = lax.Precision.HIGHEST


def group_pos(digits):
    me = 0
    for a, div, mod in digits:
        me = me * mod + (lax.axis_index(a) // div) % mod
    return me


def group_size(digits):
    return math.prod(mod for _, _, mod in digits)


def member_coords(digits, m):
    own = {a: lax.axis_index(a) for a in MESH_AXES}
    coords = dict(own)
    rem = m
    for a, div, mod in reversed(digits):
        d = rem % mod
        rem = rem // mod
        coords[a] = coords[a] - ((own[a] // div) % mod) * div + d * div
    return tuple(coords[a] for a in MESH_AXES)


def flip(me, b):
    return me + (1 - 2 * ((me // (1 << b)) % 2)) * (1 << b)


def op_rounds(kind, g):
    bits = g.bit_length() - 1
    return 2 * bits if kind == "rsag" else bits


def exchange_kernel(ops, *refs):
    n = len(ops)
    ins, outs, scr = refs[:n], refs[n:2 * n], refs[2 * n:]
    barrier = pltpu.get_barrier_semaphore()
    groups = []
    for _, digits in ops:
        if digits not in groups:
            groups.append(digits)
    count = 0
    for digits in groups:
        g = group_size(digits)
        me = group_pos(digits)
        for b in range(g.bit_length() - 1):
            pl.semaphore_signal(barrier, inc=1, device_id=member_coords(digits, flip(me, b)), device_id_type=MESH)
            count += 1
    pl.semaphore_wait(barrier, count)

    state = []
    pos = 0
    for i, (kind, digits) in enumerate(ops):
        x_ref = ins[i]
        if kind == "rsag":
            w, r, gat, ssem, rsem = scr[pos:pos + 5]
            pos += 5
            r = (r, gat)
        else:
            w, r, ssem, rsem = scr[pos:pos + 4]
            pos += 4
        if kind == "gather":
            w[group_pos(digits)] = x_ref[...]
        else:
            w[...] = x_ref[...]
        state.append((w, r, ssem, rsem))

    nrounds = max(op_rounds(kind, group_size(d)) for kind, d in ops)
    for t in range(nrounds):
        copies = []
        for i, (kind, digits) in enumerate(ops):
            g = group_size(digits)
            bits = g.bit_length() - 1
            if t >= op_rounds(kind, g):
                continue
            me = group_pos(digits)
            w, r, ssem, rsem = state[i]
            if kind == "gather":
                b = t
                partner = flip(me, b)
                span = 1 << b
                mine = pl.ds((me // span) * span, span)
                theirs = pl.ds((partner // span) * span, span)
                src, dst, land = w.at[mine], w.at[mine], w.at[theirs]
            elif kind == "sum":
                b = t
                partner = flip(me, b)
                src, dst, land = w, r.at[t], r.at[t]
            elif t < bits:
                r = r[0]
                b = bits - 1 - t
                partner = flip(me, b)
                size = w.shape[0] >> (t + 1)
                theirs = pl.ds(pl.multiple_of((partner // (1 << b)) * size, size), size)
                src, dst, land = w.at[theirs], r.at[t, pl.ds(0, size)], r.at[t, pl.ds(0, size)]
            else:
                u = t - bits
                b = u
                partner = flip(me, b)
                gat = r[1]
                size = (w.shape[0] // g) << u
                if u == 0:
                    gat[pl.ds(pl.multiple_of(me * size, size), size)] = w[pl.ds(pl.multiple_of(me * size, size), size)]
                mine = pl.ds(pl.multiple_of((me // (1 << u)) * size, size), size)
                theirs = pl.ds(pl.multiple_of((partner // (1 << u)) * size, size), size)
                src, dst, land = gat.at[mine], gat.at[mine], gat.at[theirs]
            dev = member_coords(digits, partner)
            out = pltpu.make_async_remote_copy(
                src_ref=src, dst_ref=dst, send_sem=ssem.at[t], recv_sem=rsem.at[t],
                device_id=dev, device_id_type=MESH)
            out.start()
            back = pltpu.make_async_remote_copy(
                src_ref=src, dst_ref=land, send_sem=ssem.at[t], recv_sem=rsem.at[t],
                device_id=dev, device_id_type=MESH)
            copies.append((i, kind, t, bits, out, back, me))
        for i, kind, t, bits, out, back, me in copies:
            back.wait_recv()
            out.wait_send()
            w, r, ssem, rsem = state[i]
            if kind == "sum":
                w[...] = w[...] + r[t]
            elif kind == "rsag" and t < bits:
                b = bits - 1 - t
                size = w.shape[0] >> (t + 1)
                mine = pl.ds(pl.multiple_of((me // (1 << b)) * size, size), size)
                w[mine] = w[mine] + r[0][t, pl.ds(0, size)]
    for i, (kind, _) in enumerate(ops):
        outs[i][...] = state[i][1][1][...] if kind == "rsag" else state[i][0][...]


def direct_kernel(ops, groups, *refs):
    n = len(ops)
    ins, outs, scr = refs[:n], refs[n:2 * n], refs[2 * n:]
    barrier = pltpu.get_barrier_semaphore()
    total_peers = 0
    for axes in groups:
        g = group_size(axes)
        me = group_pos(axes)
        total_peers += g - 1

        def greet(k, c, axes=axes, g=g, me=me):
            pl.semaphore_signal(barrier, inc=1, device_id=member_coords(axes, (me + k) % g), device_id_type=MESH)
            return c

        lax.fori_loop(1, g, greet, 0)
    pl.semaphore_wait(barrier, total_peers)

    pos = 0
    pending = []
    for i, (kind, axes) in enumerate(ops):
        g = group_size(axes)
        me = group_pos(axes)
        x_ref, o_ref = ins[i], outs[i]
        if kind in ("gather", "sum"):
            slots, ssem, rsem = scr[pos:pos + 3]
            pos += 3
            slots[me] = x_ref[...]

            def send(k, c, x_ref=x_ref, slots=slots, ssem=ssem, rsem=rsem, axes=axes, g=g, me=me):
                peer = (me + k) % g
                pltpu.make_async_remote_copy(
                    src_ref=x_ref, dst_ref=slots.at[me], send_sem=ssem.at[peer], recv_sem=rsem.at[me],
                    device_id=member_coords(axes, peer), device_id_type=MESH).start()
                return c

            lax.fori_loop(1, g, send, 0)
            pending.append((kind, axes, g, me, x_ref, o_ref, slots, ssem, rsem))
        else:
            rs, ag, ssem, rsem, ssem2, rsem2 = scr[pos:pos + 6]
            pos += 6
            c = x_ref.shape[0] // g
            rs[me] = x_ref[pl.ds(pl.multiple_of(me * c, c), c)]

            def send(k, cc, x_ref=x_ref, rs=rs, ssem=ssem, rsem=rsem, axes=axes, g=g, me=me, c=c):
                peer = (me + k) % g
                pltpu.make_async_remote_copy(
                    src_ref=x_ref.at[pl.ds(pl.multiple_of(peer * c, c), c)], dst_ref=rs.at[me],
                    send_sem=ssem.at[peer], recv_sem=rsem.at[me],
                    device_id=member_coords(axes, peer), device_id_type=MESH).start()
                return cc

            lax.fori_loop(1, g, send, 0)
            pending.append((kind, axes, g, me, x_ref, o_ref, (rs, ag, ssem2, rsem2), ssem, rsem))

    for kind, axes, g, me, x_ref, o_ref, slots, ssem, rsem in pending:
        if kind == "rsag":
            rs, ag, ssem2, rsem2 = slots
            c = rs.shape[1]
        else:
            rs = slots

        def wait(k, cc, x_ref=x_ref, rs=rs, ssem=ssem, rsem=rsem, axes=axes, g=g, me=me, kind=kind):
            src = (me + g - k) % g
            peer = (me + k) % g
            if kind == "rsag":
                c = rs.shape[1]
                src_ref = x_ref.at[pl.ds(0, c)]
            else:
                src_ref = x_ref
            pltpu.make_async_remote_copy(
                src_ref=src_ref, dst_ref=rs.at[src], send_sem=ssem.at[peer], recv_sem=rsem.at[src],
                device_id=member_coords(axes, peer), device_id_type=MESH).wait_recv()
            pltpu.make_async_remote_copy(
                src_ref=src_ref, dst_ref=rs.at[me], send_sem=ssem.at[peer], recv_sem=rsem.at[me],
                device_id=member_coords(axes, peer), device_id_type=MESH).wait_send()
            return cc

        lax.fori_loop(1, g, wait, 0)
        if kind == "gather":
            o_ref[...] = rs[...]
        elif kind == "sum":
            acc = rs[0]
            for s in range(1, g):
                acc = acc + rs[s]
            o_ref[...] = acc
        else:
            acc = rs[0]
            for s in range(1, g):
                acc = acc + rs[s]
            ag[me] = acc

            def send2(k, cc, ag=ag, ssem2=ssem2, rsem2=rsem2, axes=axes, g=g, me=me):
                peer = (me + k) % g
                pltpu.make_async_remote_copy(
                    src_ref=ag.at[me], dst_ref=ag.at[me], send_sem=ssem2.at[peer], recv_sem=rsem2.at[me],
                    device_id=member_coords(axes, peer), device_id_type=MESH).start()
                return cc

            lax.fori_loop(1, g, send2, 0)

            def wait2(k, cc, ag=ag, ssem2=ssem2, rsem2=rsem2, axes=axes, g=g, me=me):
                src = (me + g - k) % g
                peer = (me + k) % g
                pltpu.make_async_remote_copy(
                    src_ref=ag.at[me], dst_ref=ag.at[src], send_sem=ssem2.at[peer], recv_sem=rsem2.at[src],
                    device_id=member_coords(axes, peer), device_id_type=MESH).wait_recv()
                pltpu.make_async_remote_copy(
                    src_ref=ag.at[me], dst_ref=ag.at[me], send_sem=ssem2.at[peer], recv_sem=rsem2.at[me],
                    device_id=member_coords(axes, peer), device_id_type=MESH).wait_send()
                return cc

            lax.fori_loop(1, g, wait2, 0)
            o_ref[...] = ag[...]


def chol_kernel(g_ref, l_ref, inv_ref):
    a = g_ref[...]
    n = a.shape[0]
    rows = lax.broadcasted_iota(jnp.int32, (n, n), 0)
    lanes = lax.broadcasted_iota(jnp.int32, (n, n), 1)
    eye = (rows == lanes).astype(jnp.float32)
    x = eye
    lmat = jnp.zeros_like(a)
    for j in range(n):
        d = jnp.sqrt(a[j:j + 1, j:j + 1])
        col = jnp.where(rows[:, j:j + 1] >= j, a[:, j:j + 1], 0.0) / d
        rowv = jnp.where(lanes[j:j + 1, :] >= j, a[j:j + 1, :], 0.0) / d
        a = a - col * rowv
        lmat = jnp.where(lanes == j, col, lmat)
        xj = x[j:j + 1, :] / d
        below = jnp.where(rows[:, j:j + 1] > j, col, 0.0)
        x = jnp.where(rows == j, xj, x - below * xj)
    l_ref[...] = lmat
    inv_ref[...] = x

def chol_inv(gram):
    n = gram.shape[0]
    gram = jnp.tril(gram) + jnp.tril(gram, -1).T
    return pl.pallas_call(chol_kernel,
        out_shape=[jax.ShapeDtypeStruct((n, n), jnp.float32)] * 2,
        in_specs=[pl.BlockSpec(memory_space=pltpu.VMEM)],
        out_specs=[pl.BlockSpec(memory_space=pltpu.VMEM)] * 2)(gram)


_IDS = {}


def exchange(ops, xs):
    key = ("direct",) + tuple((k, d, x.shape, str(x.dtype)) for (k, d), x in zip(ops, xs))
    if key not in _IDS:
        _IDS[key] = len(_IDS)
    groups = []
    for _, axes in ops:
        if axes not in groups:
            groups.append(axes)
    out_shapes, scratch = [], []
    for (kind, axes), x in zip(ops, xs):
        g = group_size(axes)
        if kind == "sum":
            out_shapes.append(jax.ShapeDtypeStruct(x.shape, x.dtype))
            scratch += [pltpu.VMEM((g,) + x.shape, x.dtype), pltpu.SemaphoreType.DMA((g,)),
                        pltpu.SemaphoreType.DMA((g,))]
        else:
            c = x.shape[0] // g
            out_shapes.append(jax.ShapeDtypeStruct((g, c) + x.shape[1:], x.dtype))
            scratch += [pltpu.VMEM((g, c) + x.shape[1:], x.dtype), pltpu.VMEM((g, c) + x.shape[1:], x.dtype),
                        pltpu.SemaphoreType.DMA((g,)), pltpu.SemaphoreType.DMA((g,)),
                        pltpu.SemaphoreType.DMA((g,)), pltpu.SemaphoreType.DMA((g,))]
    outs = pl.pallas_call(
        functools.partial(direct_kernel, ops, groups),
        out_shape=out_shapes,
        in_specs=[pl.BlockSpec(memory_space=pltpu.VMEM)] * len(xs),
        out_specs=[pl.BlockSpec(memory_space=pltpu.VMEM)] * len(xs),
        scratch_shapes=scratch,
        compiler_params=pltpu.CompilerParams(collective_id=_IDS[key], has_side_effects=True),
    )(*xs)
    return [o.reshape(x.shape) for o, x in zip(outs, xs)]


def exchange_bfly(ops, xs):
    key = ("bfly",) + tuple((k, d, x.shape, str(x.dtype)) for (k, d), x in zip(ops, xs))
    if key not in _IDS:
        _IDS[key] = len(_IDS)
    out_shapes, scratch = [], []
    for (kind, digits), x in zip(ops, xs):
        g = group_size(digits)
        L = op_rounds(kind, g)
        if kind == "gather":
            out_shapes.append(jax.ShapeDtypeStruct((g,) + x.shape, x.dtype))
            scratch += [pltpu.VMEM((g,) + x.shape, x.dtype), pltpu.VMEM((8, 128), jnp.float32)]
        elif kind == "sum":
            out_shapes.append(jax.ShapeDtypeStruct(x.shape, x.dtype))
            scratch += [pltpu.VMEM(x.shape, x.dtype), pltpu.VMEM((L,) + x.shape, x.dtype)]
        else:
            out_shapes.append(jax.ShapeDtypeStruct(x.shape, x.dtype))
            scratch += [pltpu.VMEM(x.shape, x.dtype),
                        pltpu.VMEM((L // 2, x.shape[0] // 2) + x.shape[1:], x.dtype),
                        pltpu.VMEM(x.shape, x.dtype)]
        scratch += [pltpu.SemaphoreType.DMA((L,)), pltpu.SemaphoreType.DMA((L,))]
    outs = pl.pallas_call(
        functools.partial(exchange_kernel, ops),
        out_shape=out_shapes,
        in_specs=[pl.BlockSpec(memory_space=pltpu.VMEM)] * len(xs),
        out_specs=[pl.BlockSpec(memory_space=pltpu.VMEM)] * len(xs),
        scratch_shapes=scratch,
        compiler_params=pltpu.CompilerParams(collective_id=_IDS[key], has_side_effects=True),
    )(*xs)
    return list(outs)


def make_local(sizes, row_axes, col_axes):
    def local(particles, start_basis):
        shard = particles.shape[0]
        width = particles.shape[1]
        eig = start_basis.shape[1]
        total = shard * math.prod(sizes.values())
        spread = 2.0 * width
        root_total = math.sqrt(float(total))

        dense_basis = start_basis.reshape(shard * eig // 128, 128)
        i_feats, i_basis, j_feats = exchange_bfly(
            [("gather", row_axes), ("gather", row_axes), ("gather", col_axes)],
            [particles, dense_basis, particles])
        gi = group_size(row_axes)
        gj = group_size(col_axes)
        i_feats = i_feats.reshape(gi * shard, width)
        j_feats = j_feats.reshape(gj * shard, width)
        basis_i = i_basis.reshape(gi * shard, eig)

        def block_ids(digits):
            coords = member_coords(digits, jnp.arange(group_size(digits), dtype=jnp.int32))
            flat = jnp.zeros((group_size(digits),), jnp.int32)
            for a, cval in zip(MESH_AXES, coords):
                flat = flat * sizes[a] + cval
            return (flat[:, None] * shard + jnp.arange(shard, dtype=jnp.int32)[None, :]).reshape(-1)

        ids_i = block_ids(row_axes)
        ids_j = block_ids(col_axes)
        sq_i = jnp.sum(jnp.square(i_feats.astype(jnp.float32)), axis=1)
        sq_j = jnp.sum(jnp.square(j_feats.astype(jnp.float32)), axis=1)
        dots = lax.dot_general(i_feats, j_feats, (((1,), (1,)), ((), ())), preferred_element_type=jnp.float32)
        distance = sq_i[:, None] + sq_j[None, :] - 2.0 * dots
        tile = jnp.where(ids_i[:, None] == ids_j[None, :], jnp.float32(0.0), jnp.exp(-distance / spread))

        deg_i, deg_j = exchange(
            [("sum", row_axes), ("sum", col_axes)],
            [jnp.sum(tile, axis=1).reshape(-1, 128), jnp.sum(tile, axis=0).reshape(-1, 128)])
        deg_i = deg_i.reshape(-1)
        deg_j = deg_j.reshape(-1)
        root_i = jnp.sqrt(deg_i)
        root_j = jnp.sqrt(deg_j)
        me_i = group_pos(row_axes)
        scaled_i = basis_i / root_i[:, None]
        prod_j = lax.dot_general(tile, scaled_i, (((0,), (0,)), ((), ())), precision=HIGH)
        extra = jnp.concatenate([jnp.dot(root_i, basis_i, precision=HIGH)[None, :],
                                 jnp.broadcast_to(jnp.sum(deg_i), (1, eig)),
                                 jnp.zeros((6, eig), jnp.float32)], axis=0)
        dense_j, extra = exchange(
            [("rsag", col_axes), ("sum", col_axes)], [prod_j.reshape(-1, 128), extra.reshape(-1, 128)])
        prod_j = dense_j.reshape(-1, eig)
        extra = extra.reshape(-1, eig)
        inv_s = 1.0 / jnp.sqrt(extra[1, 0])
        aligned = extra[0] * inv_s
        defl_j = prod_j / root_j[:, None] - (root_j * inv_s)[:, None] * aligned[None, :]

        gram = lax.dot_general(defl_j, defl_j, (((0,), (0,)), ((), ())), precision=HIGH).reshape(-1, 128)
        q_i = jnp.dot(tile, defl_j / root_j[:, None], precision=HIGH)
        aligned_part = jnp.pad(jnp.dot(root_j, defl_j, precision=HIGH), (0, 128 - eig))[None, :]
        small = jnp.concatenate([gram, aligned_part,
                                 jnp.zeros((2 * gi - gram.shape[0] - 1, 128), jnp.float32)], axis=0)
        small, q_i = exchange([("rsag", row_axes), ("rsag", row_axes)], [small, q_i.reshape(-1, 128)])
        gram = small[:eig * eig // 128]
        part = small[eig * eig // 128:][:1, :eig]
        factor, inverse = chol_inv(gram.reshape(eig, eig))
        q_i = q_i.reshape(-1, eig)
        prod_i = lax.dot_general(q_i, inverse, (((1,), (1,)), ((), ())), precision=HIGH) * root_total
        aligned = jnp.dot(inverse, part[0], precision=HIGH) * (root_total * inv_s)
        defl_i = prod_i / root_i[:, None] - (root_i * inv_s)[:, None] * aligned[None, :]

        gram = lax.dot_general(defl_i, defl_i, (((0,), (0,)), ((), ())), precision=HIGH).reshape(-1, 128)
        (gram,) = exchange([("sum", col_axes)], [gram])
        factor, inverse = chol_inv(gram.reshape(eig, eig))
        own = lax.dynamic_slice_in_dim(defl_i, me_i * shard, shard, 0)
        basis_own = lax.dot_general(own, inverse, (((1,), (1,)), ((), ())), precision=HIGH) * root_total
        return basis_own, factor

    return local


def bit_digits(outer, outer_size, inner, inner_size):
    digits = []
    if outer is not None:
        digits.append((outer, 1, 2))
    digits += [(inner, 1 << k, 2) for k in range(inner_size.bit_length() - 1)]
    if outer is not None:
        digits += [(outer, 2 << k, 2) for k in range((outer_size // 2).bit_length() - 1)]
    return tuple(digits)


def solution(mesh):
    sizes = dict(mesh.shape)
    placed = (P(MESH_AXES, None), P(MESH_AXES, None))
    return jax.shard_map(
        make_local(sizes, bit_digits("row", sizes["row"], "vec", sizes["vec"]), bit_digits(None, 1, "col", sizes["col"])),
        mesh=mesh,
        in_specs=placed,
        out_specs=(P(MESH_AXES, None), P()),
        check_vma=False,
    )
```

```python
import functools
import math

import jax
import jax.numpy as jnp
from jax import lax
from jax.experimental import pallas as pl
from jax.experimental.pallas import tpu as pltpu
from jax.sharding import PartitionSpec as P

ITERS = 2
MESH_AXES = ("row", "col", "vec")
MESH = pl.DeviceIdType.MESH
HIGH = lax.Precision.HIGHEST


def group_pos(digits):
    me = 0
    for a, div, mod in digits:
        me = me * mod + (lax.axis_index(a) // div) % mod
    return me


def group_size(digits):
    return math.prod(mod for _, _, mod in digits)


def member_coords(digits, m):
    own = {a: lax.axis_index(a) for a in MESH_AXES}
    coords = dict(own)
    rem = m
    for a, div, mod in reversed(digits):
        d = rem % mod
        rem = rem // mod
        coords[a] = coords[a] - ((own[a] // div) % mod) * div + d * div
    return tuple(coords[a] for a in MESH_AXES)


def op_rounds(kind, g):
    bits = g.bit_length() - 1
    return 2 * bits if kind == "rsag" else bits


def exchange_kernel(ops, *refs):
    n = len(ops)
    ins, outs, scr = refs[:n], refs[n:2 * n], refs[2 * n:]
    barrier = pltpu.get_barrier_semaphore()
    groups = []
    for _, digits in ops:
        if digits not in groups:
            groups.append(digits)
    count = 0
    for digits in groups:
        me = group_pos(digits)
        span = 1
        for _, _, radix in reversed(digits):
            mine = (me // span) % radix
            for dd in range(1, radix):
                partner = me + ((mine + dd) % radix - mine) * span
                pl.semaphore_signal(barrier, inc=1, device_id=member_coords(digits, partner), device_id_type=MESH)
                count += 1
            span *= radix
    pl.semaphore_wait(barrier, count)

    state = []
    for i, (kind, digits) in enumerate(ops):
        w, ssem, rsem = scr[3 * i:3 * i + 3]
        w[group_pos(digits)] = ins[i][...]
        state.append((w, ssem, rsem))

    nrounds = max(len(d) for _, d in ops)
    for t in range(nrounds):
        waits = []
        for i, (kind, digits) in enumerate(ops):
            if t >= len(digits):
                continue
            radices = [mod for _, _, mod in reversed(digits)]
            radix = radices[t]
            span = math.prod(radices[:t])
            me = group_pos(digits)
            mine = (me // span) % radix
            base = (me // span) * span
            w, ssem, rsem = state[i]
            for dd in range(1, radix):
                partner = me + ((mine + dd) % radix - mine) * span
                sender = base + ((mine + radix - dd) % radix - mine) * span
                out = pltpu.make_async_remote_copy(
                    src_ref=w.at[pl.ds(base, span)], dst_ref=w.at[pl.ds(base, span)],
                    send_sem=ssem.at[t, dd], recv_sem=rsem.at[t, dd],
                    device_id=member_coords(digits, partner), device_id_type=MESH)
                out.start()
                back = pltpu.make_async_remote_copy(
                    src_ref=w.at[pl.ds(base, span)], dst_ref=w.at[pl.ds(sender, span)],
                    send_sem=ssem.at[t, dd], recv_sem=rsem.at[t, dd],
                    device_id=member_coords(digits, partner), device_id_type=MESH)
                waits.append((out, back))
        for out, back in waits:
            back.wait_recv()
            out.wait_send()
    for i in range(n):
        outs[i][...] = state[i][0][...]


def direct_kernel(ops, groups, *refs):
    n = len(ops)
    ins, outs, scr = refs[:n], refs[n:2 * n], refs[2 * n:]
    barrier = pltpu.get_barrier_semaphore()
    total_peers = 0
    for axes in groups:
        g = group_size(axes)
        me = group_pos(axes)
        total_peers += g - 1

        def greet(k, c, axes=axes, g=g, me=me):
            pl.semaphore_signal(barrier, inc=1, device_id=member_coords(axes, (me + k) % g), device_id_type=MESH)
            return c

        lax.fori_loop(1, g, greet, 0)
    pl.semaphore_wait(barrier, total_peers)

    pos = 0
    pending = []
    for i, (kind, axes) in enumerate(ops):
        g = group_size(axes)
        me = group_pos(axes)
        x_ref, o_ref = ins[i], outs[i]
        if kind in ("gather", "sum"):
            slots, ssem, rsem = scr[pos:pos + 3]
            pos += 3
            slots[me] = x_ref[...]

            def send(k, c, x_ref=x_ref, slots=slots, ssem=ssem, rsem=rsem, axes=axes, g=g, me=me):
                peer = (me + k) % g
                pltpu.make_async_remote_copy(
                    src_ref=x_ref, dst_ref=slots.at[me], send_sem=ssem.at[peer], recv_sem=rsem.at[me],
                    device_id=member_coords(axes, peer), device_id_type=MESH).start()
                return c

            lax.fori_loop(1, g, send, 0)
            pending.append((kind, axes, g, me, x_ref, o_ref, slots, ssem, rsem))
        else:
            rs, ag, ssem, rsem, ssem2, rsem2 = scr[pos:pos + 6]
            pos += 6
            c = x_ref.shape[0] // g
            rs[me] = x_ref[pl.ds(pl.multiple_of(me * c, c), c)]

            def send(k, cc, x_ref=x_ref, rs=rs, ssem=ssem, rsem=rsem, axes=axes, g=g, me=me, c=c):
                peer = (me + k) % g
                pltpu.make_async_remote_copy(
                    src_ref=x_ref.at[pl.ds(pl.multiple_of(peer * c, c), c)], dst_ref=rs.at[me],
                    send_sem=ssem.at[peer], recv_sem=rsem.at[me],
                    device_id=member_coords(axes, peer), device_id_type=MESH).start()
                return cc

            lax.fori_loop(1, g, send, 0)
            pending.append((kind, axes, g, me, x_ref, o_ref, (rs, ag, ssem2, rsem2), ssem, rsem))

    for kind, axes, g, me, x_ref, o_ref, slots, ssem, rsem in pending:
        if kind == "rsag":
            rs, ag, ssem2, rsem2 = slots
            c = rs.shape[1]
        else:
            rs = slots

        def wait(k, cc, x_ref=x_ref, rs=rs, ssem=ssem, rsem=rsem, axes=axes, g=g, me=me, kind=kind):
            src = (me + g - k) % g
            peer = (me + k) % g
            if kind == "rsag":
                c = rs.shape[1]
                src_ref = x_ref.at[pl.ds(0, c)]
            else:
                src_ref = x_ref
            pltpu.make_async_remote_copy(
                src_ref=src_ref, dst_ref=rs.at[src], send_sem=ssem.at[peer], recv_sem=rsem.at[src],
                device_id=member_coords(axes, peer), device_id_type=MESH).wait_recv()
            pltpu.make_async_remote_copy(
                src_ref=src_ref, dst_ref=rs.at[me], send_sem=ssem.at[peer], recv_sem=rsem.at[me],
                device_id=member_coords(axes, peer), device_id_type=MESH).wait_send()
            return cc

        lax.fori_loop(1, g, wait, 0)
        if kind == "gather":
            o_ref[...] = rs[...]
        elif kind == "sum":
            acc = rs[0]
            for s in range(1, g):
                acc = acc + rs[s]
            o_ref[...] = acc
        else:
            acc = rs[0]
            for s in range(1, g):
                acc = acc + rs[s]
            ag[me] = acc

            def send2(k, cc, ag=ag, ssem2=ssem2, rsem2=rsem2, axes=axes, g=g, me=me):
                peer = (me + k) % g
                pltpu.make_async_remote_copy(
                    src_ref=ag.at[me], dst_ref=ag.at[me], send_sem=ssem2.at[peer], recv_sem=rsem2.at[me],
                    device_id=member_coords(axes, peer), device_id_type=MESH).start()
                return cc

            lax.fori_loop(1, g, send2, 0)

            def wait2(k, cc, ag=ag, ssem2=ssem2, rsem2=rsem2, axes=axes, g=g, me=me):
                src = (me + g - k) % g
                peer = (me + k) % g
                pltpu.make_async_remote_copy(
                    src_ref=ag.at[me], dst_ref=ag.at[src], send_sem=ssem2.at[peer], recv_sem=rsem2.at[src],
                    device_id=member_coords(axes, peer), device_id_type=MESH).wait_recv()
                pltpu.make_async_remote_copy(
                    src_ref=ag.at[me], dst_ref=ag.at[me], send_sem=ssem2.at[peer], recv_sem=rsem2.at[me],
                    device_id=member_coords(axes, peer), device_id_type=MESH).wait_send()
                return cc

            lax.fori_loop(1, g, wait2, 0)
            o_ref[...] = ag[...]


def chol_kernel(g_ref, l_ref, inv_ref):
    a = g_ref[...]
    n = a.shape[0]
    rows = lax.broadcasted_iota(jnp.int32, (n, n), 0)
    lanes = lax.broadcasted_iota(jnp.int32, (n, n), 1)
    eye = (rows == lanes).astype(jnp.float32)
    x = eye
    lmat = jnp.zeros_like(a)
    for j in range(n):
        d = jnp.sqrt(a[j:j + 1, j:j + 1])
        col = jnp.where(rows[:, j:j + 1] >= j, a[:, j:j + 1], 0.0) / d
        rowv = jnp.where(lanes[j:j + 1, :] >= j, a[j:j + 1, :], 0.0) / d
        a = a - col * rowv
        lmat = jnp.where(lanes == j, col, lmat)
        xj = x[j:j + 1, :] / d
        below = jnp.where(rows[:, j:j + 1] > j, col, 0.0)
        x = jnp.where(rows == j, xj, x - below * xj)
    l_ref[...] = lmat
    inv_ref[...] = x

def chol_inv(gram):
    n = gram.shape[0]
    gram = jnp.tril(gram) + jnp.tril(gram, -1).T
    return pl.pallas_call(chol_kernel,
        out_shape=[jax.ShapeDtypeStruct((n, n), jnp.float32)] * 2,
        in_specs=[pl.BlockSpec(memory_space=pltpu.VMEM)],
        out_specs=[pl.BlockSpec(memory_space=pltpu.VMEM)] * 2)(gram)


_IDS = {}


def exchange(ops, xs):
    key = ("direct",) + tuple((k, d, x.shape, str(x.dtype)) for (k, d), x in zip(ops, xs))
    if key not in _IDS:
        _IDS[key] = len(_IDS)
    groups = []
    for _, axes in ops:
        if axes not in groups:
            groups.append(axes)
    out_shapes, scratch = [], []
    for (kind, axes), x in zip(ops, xs):
        g = group_size(axes)
        if kind == "sum":
            out_shapes.append(jax.ShapeDtypeStruct(x.shape, x.dtype))
            scratch += [pltpu.VMEM((g,) + x.shape, x.dtype), pltpu.SemaphoreType.DMA((g,)),
                        pltpu.SemaphoreType.DMA((g,))]
        else:
            c = x.shape[0] // g
            out_shapes.append(jax.ShapeDtypeStruct((g, c) + x.shape[1:], x.dtype))
            scratch += [pltpu.VMEM((g, c) + x.shape[1:], x.dtype), pltpu.VMEM((g, c) + x.shape[1:], x.dtype),
                        pltpu.SemaphoreType.DMA((g,)), pltpu.SemaphoreType.DMA((g,)),
                        pltpu.SemaphoreType.DMA((g,)), pltpu.SemaphoreType.DMA((g,))]
    outs = pl.pallas_call(
        functools.partial(direct_kernel, ops, groups),
        out_shape=out_shapes,
        in_specs=[pl.BlockSpec(memory_space=pltpu.VMEM)] * len(xs),
        out_specs=[pl.BlockSpec(memory_space=pltpu.VMEM)] * len(xs),
        scratch_shapes=scratch,
        compiler_params=pltpu.CompilerParams(collective_id=_IDS[key], has_side_effects=True),
    )(*xs)
    return [o.reshape(x.shape) for o, x in zip(outs, xs)]


def exchange_bfly(ops, xs):
    key = ("bfly",) + tuple((k, d, x.shape, str(x.dtype)) for (k, d), x in zip(ops, xs))
    if key not in _IDS:
        _IDS[key] = len(_IDS)
    out_shapes, scratch = [], []
    for (kind, digits), x in zip(ops, xs):
        g = group_size(digits)
        rmax = max(mod for _, _, mod in digits)
        out_shapes.append(jax.ShapeDtypeStruct((g,) + x.shape, x.dtype))
        scratch += [pltpu.VMEM((g,) + x.shape, x.dtype),
                    pltpu.SemaphoreType.DMA((len(digits), rmax)), pltpu.SemaphoreType.DMA((len(digits), rmax))]
    outs = pl.pallas_call(
        functools.partial(exchange_kernel, ops),
        out_shape=out_shapes,
        in_specs=[pl.BlockSpec(memory_space=pltpu.VMEM)] * len(xs),
        out_specs=[pl.BlockSpec(memory_space=pltpu.VMEM)] * len(xs),
        scratch_shapes=scratch,
        compiler_params=pltpu.CompilerParams(collective_id=_IDS[key], has_side_effects=True),
    )(*xs)
    return list(outs)


def make_local(sizes, row_axes, col_axes):
    def local(particles, start_basis):
        shard = particles.shape[0]
        width = particles.shape[1]
        eig = start_basis.shape[1]
        total = shard * math.prod(sizes.values())
        spread = 2.0 * width
        root_total = math.sqrt(float(total))

        dense_basis = start_basis.reshape(shard * eig // 128, 128)
        i_feats, i_basis, j_feats = exchange_bfly(
            [("gather", row_axes), ("gather", row_axes), ("gather", col_axes)],
            [particles, dense_basis, particles])
        gi = group_size(row_axes)
        gj = group_size(col_axes)
        i_feats = i_feats.reshape(gi * shard, width)
        j_feats = j_feats.reshape(gj * shard, width)
        basis_i = i_basis.reshape(gi * shard, eig)

        def block_ids(digits):
            coords = member_coords(digits, jnp.arange(group_size(digits), dtype=jnp.int32))
            flat = jnp.zeros((group_size(digits),), jnp.int32)
            for a, cval in zip(MESH_AXES, coords):
                flat = flat * sizes[a] + cval
            return (flat[:, None] * shard + jnp.arange(shard, dtype=jnp.int32)[None, :]).reshape(-1)

        ids_i = block_ids(row_axes)
        ids_j = block_ids(col_axes)
        sq_i = jnp.sum(jnp.square(i_feats.astype(jnp.float32)), axis=1)
        sq_j = jnp.sum(jnp.square(j_feats.astype(jnp.float32)), axis=1)
        dots = lax.dot_general(i_feats, j_feats, (((1,), (1,)), ((), ())), preferred_element_type=jnp.float32)
        distance = sq_i[:, None] + sq_j[None, :] - 2.0 * dots
        tile = jnp.where(ids_i[:, None] == ids_j[None, :], jnp.float32(0.0), jnp.exp(-distance / spread))

        deg_i, deg_j = exchange(
            [("sum", row_axes), ("sum", col_axes)],
            [jnp.sum(tile, axis=1).reshape(-1, 128), jnp.sum(tile, axis=0).reshape(-1, 128)])
        deg_i = deg_i.reshape(-1)
        deg_j = deg_j.reshape(-1)
        root_i = jnp.sqrt(deg_i)
        root_j = jnp.sqrt(deg_j)
        me_i = group_pos(row_axes)
        scaled_i = basis_i / root_i[:, None]
        prod_j = lax.dot_general(tile, scaled_i, (((0,), (0,)), ((), ())), precision=HIGH)
        extra = jnp.concatenate([jnp.dot(root_i, basis_i, precision=HIGH)[None, :],
                                 jnp.broadcast_to(jnp.sum(deg_i), (1, eig)),
                                 jnp.zeros((6, eig), jnp.float32)], axis=0)
        dense_j, extra = exchange(
            [("rsag", col_axes), ("sum", col_axes)], [prod_j.reshape(-1, 128), extra.reshape(-1, 128)])
        prod_j = dense_j.reshape(-1, eig)
        extra = extra.reshape(-1, eig)
        inv_s = 1.0 / jnp.sqrt(extra[1, 0])
        aligned = extra[0] * inv_s
        defl_j = prod_j / root_j[:, None] - (root_j * inv_s)[:, None] * aligned[None, :]

        gram = lax.dot_general(defl_j, defl_j, (((0,), (0,)), ((), ())), precision=HIGH).reshape(-1, 128)
        q_i = jnp.dot(tile, defl_j / root_j[:, None], precision=HIGH)
        aligned_part = jnp.pad(jnp.dot(root_j, defl_j, precision=HIGH), (0, 128 - eig))[None, :]
        small = jnp.concatenate([gram, aligned_part,
                                 jnp.zeros((2 * gi - gram.shape[0] - 1, 128), jnp.float32)], axis=0)
        small, q_i = exchange([("rsag", row_axes), ("rsag", row_axes)], [small, q_i.reshape(-1, 128)])
        gram = small[:eig * eig // 128]
        part = small[eig * eig // 128:][:1, :eig]
        factor, inverse = chol_inv(gram.reshape(eig, eig))
        q_i = q_i.reshape(-1, eig)
        prod_i = lax.dot_general(q_i, inverse, (((1,), (1,)), ((), ())), precision=HIGH) * root_total
        aligned = jnp.dot(inverse, part[0], precision=HIGH) * (root_total * inv_s)
        defl_i = prod_i / root_i[:, None] - (root_i * inv_s)[:, None] * aligned[None, :]

        gram = lax.dot_general(defl_i, defl_i, (((0,), (0,)), ((), ())), precision=HIGH).reshape(-1, 128)
        (gram,) = exchange([("sum", col_axes)], [gram])
        factor, inverse = chol_inv(gram.reshape(eig, eig))
        own = lax.dynamic_slice_in_dim(defl_i, me_i * shard, shard, 0)
        basis_own = lax.dot_general(own, inverse, (((1,), (1,)), ((), ())), precision=HIGH) * root_total
        return basis_own, factor

    return local


def solution(mesh):
    sizes = dict(mesh.shape)
    placed = (P(MESH_AXES, None), P(MESH_AXES, None))
    return jax.shard_map(
        make_local(sizes, (("row", 1, 2), ("vec", 1, sizes["vec"]), ("row", 2, sizes["row"] // 2)),
                   (("col", 1, 2), ("col", 2, 2), ("col", 4, sizes["col"] // 4))),
        mesh=mesh,
        in_specs=placed,
        out_specs=(P(MESH_AXES, None), P()),
        check_vma=False,
    )
```

```python
import functools
import math

import jax
import jax.numpy as jnp
from jax import lax
from jax.experimental import pallas as pl
from jax.experimental.pallas import tpu as pltpu
from jax.sharding import PartitionSpec as P

ITERS = 2
MESH_AXES = ("row", "col", "vec")
MESH = pl.DeviceIdType.MESH
HIGH = lax.Precision.HIGHEST


def group_pos(digits):
    me = 0
    for a, div, mod in digits:
        me = me * mod + (lax.axis_index(a) // div) % mod
    return me


def group_size(digits):
    return math.prod(mod for _, _, mod in digits)


def member_coords(digits, m):
    own = {a: lax.axis_index(a) for a in MESH_AXES}
    coords = dict(own)
    rem = m
    for a, div, mod in reversed(digits):
        d = rem % mod
        rem = rem // mod
        coords[a] = coords[a] - ((own[a] // div) % mod) * div + d * div
    return tuple(coords[a] for a in MESH_AXES)


def op_rounds(kind, g):
    bits = g.bit_length() - 1
    return 2 * bits if kind == "rsag" else bits


def exchange_kernel(ops, *refs):
    n = len(ops)
    ins, outs, scr = refs[:n], refs[n:2 * n], refs[2 * n:]
    barrier = pltpu.get_barrier_semaphore()
    groups = []
    for _, digits in ops:
        if digits not in groups:
            groups.append(digits)
    count = 0
    for digits in groups:
        me = group_pos(digits)
        span = 1
        for _, _, radix in reversed(digits):
            mine = (me // span) % radix
            for dd in range(1, radix):
                partner = me + ((mine + dd) % radix - mine) * span
                pl.semaphore_signal(barrier, inc=1, device_id=member_coords(digits, partner), device_id_type=MESH)
                count += 1
            span *= radix
    pl.semaphore_wait(barrier, count)

    state = []
    for i, (kind, digits) in enumerate(ops):
        w, ssem, rsem = scr[3 * i:3 * i + 3]
        w[group_pos(digits)] = ins[i][...]
        state.append((w, ssem, rsem))

    nrounds = max(len(d) for _, d in ops)
    for t in range(nrounds):
        waits = []
        for i, (kind, digits) in enumerate(ops):
            if t >= len(digits):
                continue
            radices = [mod for _, _, mod in reversed(digits)]
            radix = radices[t]
            span = math.prod(radices[:t])
            me = group_pos(digits)
            mine = (me // span) % radix
            base = (me // span) * span
            w, ssem, rsem = state[i]
            for dd in range(1, radix):
                partner = me + ((mine + dd) % radix - mine) * span
                sender = base + ((mine + radix - dd) % radix - mine) * span
                out = pltpu.make_async_remote_copy(
                    src_ref=w.at[pl.ds(base, span)], dst_ref=w.at[pl.ds(base, span)],
                    send_sem=ssem.at[t, dd], recv_sem=rsem.at[t, dd],
                    device_id=member_coords(digits, partner), device_id_type=MESH)
                out.start()
                back = pltpu.make_async_remote_copy(
                    src_ref=w.at[pl.ds(base, span)], dst_ref=w.at[pl.ds(sender, span)],
                    send_sem=ssem.at[t, dd], recv_sem=rsem.at[t, dd],
                    device_id=member_coords(digits, partner), device_id_type=MESH)
                waits.append((out, back))
        for out, back in waits:
            back.wait_recv()
            out.wait_send()
    for i in range(n):
        outs[i][...] = state[i][0][...]


def direct_kernel(ops, groups, *refs):
    n = len(ops)
    ins, outs, scr = refs[:n], refs[n:2 * n], refs[2 * n:]
    barrier = pltpu.get_barrier_semaphore()
    total_peers = 0
    for axes in groups:
        g = group_size(axes)
        me = group_pos(axes)
        total_peers += g - 1

        def greet(k, c, axes=axes, g=g, me=me):
            pl.semaphore_signal(barrier, inc=1, device_id=member_coords(axes, (me + k) % g), device_id_type=MESH)
            return c

        lax.fori_loop(1, g, greet, 0)
    pl.semaphore_wait(barrier, total_peers)

    pos = 0
    pending = []
    for i, (kind, axes) in enumerate(ops):
        g = group_size(axes)
        me = group_pos(axes)
        x_ref, o_ref = ins[i], outs[i]
        if kind in ("gather", "sum"):
            slots, ssem, rsem = scr[pos:pos + 3]
            pos += 3
            slots[me] = x_ref[...]

            def send(k, c, x_ref=x_ref, slots=slots, ssem=ssem, rsem=rsem, axes=axes, g=g, me=me):
                peer = (me + k) % g
                pltpu.make_async_remote_copy(
                    src_ref=x_ref, dst_ref=slots.at[me], send_sem=ssem.at[peer], recv_sem=rsem.at[me],
                    device_id=member_coords(axes, peer), device_id_type=MESH).start()
                return c

            lax.fori_loop(1, g, send, 0)
            pending.append((kind, axes, g, me, x_ref, o_ref, slots, ssem, rsem))
        else:
            rs, ag, ssem, rsem, ssem2, rsem2 = scr[pos:pos + 6]
            pos += 6
            c = x_ref.shape[0] // g
            rs[me] = x_ref[pl.ds(pl.multiple_of(me * c, c), c)]

            def send(k, cc, x_ref=x_ref, rs=rs, ssem=ssem, rsem=rsem, axes=axes, g=g, me=me, c=c):
                peer = (me + k) % g
                pltpu.make_async_remote_copy(
                    src_ref=x_ref.at[pl.ds(pl.multiple_of(peer * c, c), c)], dst_ref=rs.at[me],
                    send_sem=ssem.at[peer], recv_sem=rsem.at[me],
                    device_id=member_coords(axes, peer), device_id_type=MESH).start()
                return cc

            lax.fori_loop(1, g, send, 0)
            pending.append((kind, axes, g, me, x_ref, o_ref, (rs, ag, ssem2, rsem2), ssem, rsem))

    for kind, axes, g, me, x_ref, o_ref, slots, ssem, rsem in pending:
        if kind == "rsag":
            rs, ag, ssem2, rsem2 = slots
            c = rs.shape[1]
        else:
            rs = slots

        def wait(k, cc, x_ref=x_ref, rs=rs, ssem=ssem, rsem=rsem, axes=axes, g=g, me=me, kind=kind):
            src = (me + g - k) % g
            peer = (me + k) % g
            if kind == "rsag":
                c = rs.shape[1]
                src_ref = x_ref.at[pl.ds(0, c)]
            else:
                src_ref = x_ref
            pltpu.make_async_remote_copy(
                src_ref=src_ref, dst_ref=rs.at[src], send_sem=ssem.at[peer], recv_sem=rsem.at[src],
                device_id=member_coords(axes, peer), device_id_type=MESH).wait_recv()
            pltpu.make_async_remote_copy(
                src_ref=src_ref, dst_ref=rs.at[me], send_sem=ssem.at[peer], recv_sem=rsem.at[me],
                device_id=member_coords(axes, peer), device_id_type=MESH).wait_send()
            return cc

        lax.fori_loop(1, g, wait, 0)
        if kind == "gather":
            o_ref[...] = rs[...]
        elif kind == "sum":
            acc = rs[0]
            for s in range(1, g):
                acc = acc + rs[s]
            o_ref[...] = acc
        else:
            acc = rs[0]
            for s in range(1, g):
                acc = acc + rs[s]
            ag[me] = acc

            def send2(k, cc, ag=ag, ssem2=ssem2, rsem2=rsem2, axes=axes, g=g, me=me):
                peer = (me + k) % g
                pltpu.make_async_remote_copy(
                    src_ref=ag.at[me], dst_ref=ag.at[me], send_sem=ssem2.at[peer], recv_sem=rsem2.at[me],
                    device_id=member_coords(axes, peer), device_id_type=MESH).start()
                return cc

            lax.fori_loop(1, g, send2, 0)

            def wait2(k, cc, ag=ag, ssem2=ssem2, rsem2=rsem2, axes=axes, g=g, me=me):
                src = (me + g - k) % g
                peer = (me + k) % g
                pltpu.make_async_remote_copy(
                    src_ref=ag.at[me], dst_ref=ag.at[src], send_sem=ssem2.at[peer], recv_sem=rsem2.at[src],
                    device_id=member_coords(axes, peer), device_id_type=MESH).wait_recv()
                pltpu.make_async_remote_copy(
                    src_ref=ag.at[me], dst_ref=ag.at[me], send_sem=ssem2.at[peer], recv_sem=rsem2.at[me],
                    device_id=member_coords(axes, peer), device_id_type=MESH).wait_send()
                return cc

            lax.fori_loop(1, g, wait2, 0)
            o_ref[...] = ag[...]


def chol_kernel(g_ref, l_ref, inv_ref):
    a = g_ref[...]
    n = a.shape[0]
    rows = lax.broadcasted_iota(jnp.int32, (n, n), 0)
    lanes = lax.broadcasted_iota(jnp.int32, (n, n), 1)
    eye = (rows == lanes).astype(jnp.float32)
    x = eye
    lmat = jnp.zeros_like(a)
    for j in range(n):
        d = jnp.sqrt(a[j:j + 1, j:j + 1])
        col = jnp.where(rows[:, j:j + 1] >= j, a[:, j:j + 1], 0.0) / d
        rowv = jnp.where(lanes[j:j + 1, :] >= j, a[j:j + 1, :], 0.0) / d
        a = a - col * rowv
        lmat = jnp.where(lanes == j, col, lmat)
        xj = x[j:j + 1, :] / d
        below = jnp.where(rows[:, j:j + 1] > j, col, 0.0)
        x = jnp.where(rows == j, xj, x - below * xj)
    l_ref[...] = lmat
    inv_ref[...] = x

def chol_inv(gram):
    n = gram.shape[0]
    gram = jnp.tril(gram) + jnp.tril(gram, -1).T
    return pl.pallas_call(chol_kernel,
        out_shape=[jax.ShapeDtypeStruct((n, n), jnp.float32)] * 2,
        in_specs=[pl.BlockSpec(memory_space=pltpu.VMEM)],
        out_specs=[pl.BlockSpec(memory_space=pltpu.VMEM)] * 2)(gram)


_IDS = {}


def exchange(ops, xs):
    key = ("direct",) + tuple((k, d, x.shape, str(x.dtype)) for (k, d), x in zip(ops, xs))
    if key not in _IDS:
        _IDS[key] = len(_IDS)
    groups = []
    for _, axes in ops:
        if axes not in groups:
            groups.append(axes)
    out_shapes, scratch = [], []
    for (kind, axes), x in zip(ops, xs):
        g = group_size(axes)
        if kind == "sum":
            out_shapes.append(jax.ShapeDtypeStruct(x.shape, x.dtype))
            scratch += [pltpu.VMEM((g,) + x.shape, x.dtype), pltpu.SemaphoreType.DMA((g,)),
                        pltpu.SemaphoreType.DMA((g,))]
        else:
            c = x.shape[0] // g
            out_shapes.append(jax.ShapeDtypeStruct((g, c) + x.shape[1:], x.dtype))
            scratch += [pltpu.VMEM((g, c) + x.shape[1:], x.dtype), pltpu.VMEM((g, c) + x.shape[1:], x.dtype),
                        pltpu.SemaphoreType.DMA((g,)), pltpu.SemaphoreType.DMA((g,)),
                        pltpu.SemaphoreType.DMA((g,)), pltpu.SemaphoreType.DMA((g,))]
    outs = pl.pallas_call(
        functools.partial(direct_kernel, ops, groups),
        out_shape=out_shapes,
        in_specs=[pl.BlockSpec(memory_space=pltpu.VMEM)] * len(xs),
        out_specs=[pl.BlockSpec(memory_space=pltpu.VMEM)] * len(xs),
        scratch_shapes=scratch,
        compiler_params=pltpu.CompilerParams(collective_id=_IDS[key], has_side_effects=True),
    )(*xs)
    return [o.reshape(x.shape) for o, x in zip(outs, xs)]


def exchange_bfly(ops, xs):
    key = ("bfly",) + tuple((k, d, x.shape, str(x.dtype)) for (k, d), x in zip(ops, xs))
    if key not in _IDS:
        _IDS[key] = len(_IDS)
    out_shapes, scratch = [], []
    for (kind, digits), x in zip(ops, xs):
        g = group_size(digits)
        rmax = max(mod for _, _, mod in digits)
        out_shapes.append(jax.ShapeDtypeStruct((g,) + x.shape, x.dtype))
        scratch += [pltpu.VMEM((g,) + x.shape, x.dtype),
                    pltpu.SemaphoreType.DMA((len(digits), rmax)), pltpu.SemaphoreType.DMA((len(digits), rmax))]
    outs = pl.pallas_call(
        functools.partial(exchange_kernel, ops),
        out_shape=out_shapes,
        in_specs=[pl.BlockSpec(memory_space=pltpu.VMEM)] * len(xs),
        out_specs=[pl.BlockSpec(memory_space=pltpu.VMEM)] * len(xs),
        scratch_shapes=scratch,
        compiler_params=pltpu.CompilerParams(collective_id=_IDS[key], has_side_effects=True),
    )(*xs)
    return list(outs)


def make_local(sizes, row_axes, col_axes):
    def local(particles, start_basis):
        shard = particles.shape[0]
        width = particles.shape[1]
        eig = start_basis.shape[1]
        total = shard * math.prod(sizes.values())
        spread = 2.0 * width
        root_total = math.sqrt(float(total))

        dense_basis = start_basis.reshape(shard * eig // 128, 128)
        i_feats, i_basis, j_feats = exchange_bfly(
            [("gather", row_axes), ("gather", row_axes), ("gather", col_axes)],
            [particles, dense_basis, particles])
        gi = group_size(row_axes)
        gj = group_size(col_axes)
        i_feats = i_feats.reshape(gi * shard, width)
        j_feats = j_feats.reshape(gj * shard, width)
        basis_i = i_basis.reshape(gi * shard, eig)

        def block_ids(digits):
            coords = member_coords(digits, jnp.arange(group_size(digits), dtype=jnp.int32))
            flat = jnp.zeros((group_size(digits),), jnp.int32)
            for a, cval in zip(MESH_AXES, coords):
                flat = flat * sizes[a] + cval
            return (flat[:, None] * shard + jnp.arange(shard, dtype=jnp.int32)[None, :]).reshape(-1)

        ids_i = block_ids(row_axes)
        ids_j = block_ids(col_axes)
        sq_i = jnp.sum(jnp.square(i_feats.astype(jnp.float32)), axis=1)
        sq_j = jnp.sum(jnp.square(j_feats.astype(jnp.float32)), axis=1)
        dots = lax.dot_general(i_feats, j_feats, (((1,), (1,)), ((), ())), preferred_element_type=jnp.float32)
        distance = sq_i[:, None] + sq_j[None, :] - 2.0 * dots
        tile = jnp.where(ids_i[:, None] == ids_j[None, :], jnp.float32(0.0), jnp.exp(-distance / spread))

        deg_i, deg_j = exchange(
            [("sum", row_axes), ("sum", col_axes)],
            [jnp.sum(tile, axis=1).reshape(-1, 128), jnp.sum(tile, axis=0).reshape(-1, 128)])
        deg_i = deg_i.reshape(-1)
        deg_j = deg_j.reshape(-1)
        root_i = jnp.sqrt(deg_i)
        root_j = jnp.sqrt(deg_j)
        me_i = group_pos(row_axes)
        scaled_i = basis_i / root_i[:, None]
        prod_j = lax.dot_general(tile, scaled_i, (((0,), (0,)), ((), ())), precision=HIGH)
        extra = jnp.concatenate([jnp.dot(root_i, basis_i, precision=HIGH)[None, :],
                                 jnp.broadcast_to(jnp.sum(deg_i), (1, eig)),
                                 jnp.zeros((6, eig), jnp.float32)], axis=0)
        dense_j, extra = exchange(
            [("rsag", col_axes), ("sum", col_axes)], [prod_j.reshape(-1, 128), extra.reshape(-1, 128)])
        prod_j = dense_j.reshape(-1, eig)
        extra = extra.reshape(-1, eig)
        inv_s = 1.0 / jnp.sqrt(extra[1, 0])
        aligned = extra[0] * inv_s
        defl_j = prod_j / root_j[:, None] - (root_j * inv_s)[:, None] * aligned[None, :]

        gram = lax.dot_general(defl_j, defl_j, (((0,), (0,)), ((), ())), precision=HIGH).reshape(-1, 128)
        q_i = jnp.dot(tile, defl_j / root_j[:, None], precision=HIGH)
        aligned_part = jnp.pad(jnp.dot(root_j, defl_j, precision=HIGH), (0, 128 - eig))[None, :]
        small = jnp.concatenate([gram, aligned_part,
                                 jnp.zeros((2 * gi - gram.shape[0] - 1, 128), jnp.float32)], axis=0)
        small, q_i = exchange([("rsag", row_axes), ("rsag", row_axes)], [small, q_i.reshape(-1, 128)])
        gram = small[:eig * eig // 128]
        part = small[eig * eig // 128:][:1, :eig]
        factor, inverse = chol_inv(gram.reshape(eig, eig))
        q_i = q_i.reshape(-1, eig)
        prod_i = lax.dot_general(q_i, inverse, (((1,), (1,)), ((), ())), precision=HIGH) * root_total
        aligned = jnp.dot(inverse, part[0], precision=HIGH) * (root_total * inv_s)
        defl_i = prod_i / root_i[:, None] - (root_i * inv_s)[:, None] * aligned[None, :]

        gram = lax.dot_general(defl_i, defl_i, (((0,), (0,)), ((), ())), precision=HIGH).reshape(-1, 128)
        (gram,) = exchange([("sum", col_axes)], [gram])
        factor, inverse = chol_inv(gram.reshape(eig, eig))
        own = lax.dynamic_slice_in_dim(defl_i, me_i * shard, shard, 0)
        basis_own = lax.dot_general(own, inverse, (((1,), (1,)), ((), ())), precision=HIGH) * root_total
        return basis_own, factor

    return local


def solution(mesh):
    sizes = dict(mesh.shape)
    placed = (P(MESH_AXES, None), P(MESH_AXES, None))
    return jax.shard_map(
        make_local(sizes, (("row", 1, 2), ("vec", 1, sizes["vec"]), ("row", 2, sizes["row"] // 2)),
                   (("col", 1, 2), ("col", 2, sizes["col"] // 2))),
        mesh=mesh,
        in_specs=placed,
        out_specs=(P(MESH_AXES, None), P()),
        check_vma=False,
    )
```

```python
import functools
import math

import jax
import jax.numpy as jnp
from jax import lax
from jax.experimental import pallas as pl
from jax.experimental.pallas import tpu as pltpu
from jax.sharding import PartitionSpec as P

ITERS = 2
MESH_AXES = ("row", "col", "vec")
MESH = pl.DeviceIdType.MESH
HIGH = lax.Precision.HIGHEST


def group_pos(digits):
    me = 0
    for a, div, mod in digits:
        me = me * mod + (lax.axis_index(a) // div) % mod
    return me


def group_size(digits):
    return math.prod(mod for _, _, mod in digits)


def member_coords(digits, m):
    own = {a: lax.axis_index(a) for a in MESH_AXES}
    coords = dict(own)
    rem = m
    for a, div, mod in reversed(digits):
        d = rem % mod
        rem = rem // mod
        coords[a] = coords[a] - ((own[a] // div) % mod) * div + d * div
    return tuple(coords[a] for a in MESH_AXES)


def op_rounds(kind, g):
    bits = g.bit_length() - 1
    return 2 * bits if kind == "rsag" else bits


def exchange_kernel(ops, *refs):
    n = len(ops)
    ins, outs, scr = refs[:n], refs[n:2 * n], refs[2 * n:]
    barrier = pltpu.get_barrier_semaphore()
    groups = []
    for _, digits in ops:
        if digits not in groups:
            groups.append(digits)
    count = 0
    for digits in groups:
        me = group_pos(digits)
        span = 1
        for _, _, radix in reversed(digits):
            mine = (me // span) % radix
            for dd in range(1, radix):
                partner = me + ((mine + dd) % radix - mine) * span
                pl.semaphore_signal(barrier, inc=1, device_id=member_coords(digits, partner), device_id_type=MESH)
                count += 1
            span *= radix
    pl.semaphore_wait(barrier, count)

    state = []
    for i, (kind, digits) in enumerate(ops):
        w, ssem, rsem = scr[3 * i:3 * i + 3]
        w[group_pos(digits)] = ins[i][...]
        state.append((w, ssem, rsem))

    nrounds = max(len(d) for _, d in ops)
    for t in range(nrounds):
        waits = []
        for i, (kind, digits) in enumerate(ops):
            if t >= len(digits):
                continue
            radices = [mod for _, _, mod in reversed(digits)]
            radix = radices[t]
            span = math.prod(radices[:t])
            me = group_pos(digits)
            mine = (me // span) % radix
            base = (me // span) * span
            w, ssem, rsem = state[i]
            for dd in range(1, radix):
                partner = me + ((mine + dd) % radix - mine) * span
                sender = base + ((mine + radix - dd) % radix - mine) * span
                out = pltpu.make_async_remote_copy(
                    src_ref=w.at[pl.ds(base, span)], dst_ref=w.at[pl.ds(base, span)],
                    send_sem=ssem.at[t, dd], recv_sem=rsem.at[t, dd],
                    device_id=member_coords(digits, partner), device_id_type=MESH)
                out.start()
                back = pltpu.make_async_remote_copy(
                    src_ref=w.at[pl.ds(base, span)], dst_ref=w.at[pl.ds(sender, span)],
                    send_sem=ssem.at[t, dd], recv_sem=rsem.at[t, dd],
                    device_id=member_coords(digits, partner), device_id_type=MESH)
                waits.append((out, back))
        for out, back in waits:
            back.wait_recv()
            out.wait_send()
    for i in range(n):
        outs[i][...] = state[i][0][...]


def direct_kernel(ops, groups, *refs):
    n = len(ops)
    ins, outs, scr = refs[:n], refs[n:2 * n], refs[2 * n:]
    barrier = pltpu.get_barrier_semaphore()
    total_peers = 0
    for axes in groups:
        g = group_size(axes)
        me = group_pos(axes)
        total_peers += g - 1

        def greet(k, c, axes=axes, g=g, me=me):
            pl.semaphore_signal(barrier, inc=1, device_id=member_coords(axes, (me + k) % g), device_id_type=MESH)
            return c

        lax.fori_loop(1, g, greet, 0)
    pl.semaphore_wait(barrier, total_peers)

    pos = 0
    pending = []
    for i, (kind, axes) in enumerate(ops):
        g = group_size(axes)
        me = group_pos(axes)
        x_ref, o_ref = ins[i], outs[i]
        if kind in ("gather", "sum"):
            slots, ssem, rsem = scr[pos:pos + 3]
            pos += 3
            slots[me] = x_ref[...]

            def send(k, c, x_ref=x_ref, slots=slots, ssem=ssem, rsem=rsem, axes=axes, g=g, me=me):
                peer = (me + k) % g
                pltpu.make_async_remote_copy(
                    src_ref=x_ref, dst_ref=slots.at[me], send_sem=ssem.at[peer], recv_sem=rsem.at[me],
                    device_id=member_coords(axes, peer), device_id_type=MESH).start()
                return c

            lax.fori_loop(1, g, send, 0)
            pending.append((kind, axes, g, me, x_ref, o_ref, slots, ssem, rsem))
        else:
            rs, ag, ssem, rsem, ssem2, rsem2 = scr[pos:pos + 6]
            pos += 6
            c = x_ref.shape[0] // g
            rs[me] = x_ref[pl.ds(pl.multiple_of(me * c, c), c)]

            def send(k, cc, x_ref=x_ref, rs=rs, ssem=ssem, rsem=rsem, axes=axes, g=g, me=me, c=c):
                peer = (me + k) % g
                pltpu.make_async_remote_copy(
                    src_ref=x_ref.at[pl.ds(pl.multiple_of(peer * c, c), c)], dst_ref=rs.at[me],
                    send_sem=ssem.at[peer], recv_sem=rsem.at[me],
                    device_id=member_coords(axes, peer), device_id_type=MESH).start()
                return cc

            lax.fori_loop(1, g, send, 0)
            pending.append((kind, axes, g, me, x_ref, o_ref, (rs, ag, ssem2, rsem2), ssem, rsem))

    for kind, axes, g, me, x_ref, o_ref, slots, ssem, rsem in pending:
        if kind == "rsag":
            rs, ag, ssem2, rsem2 = slots
            c = rs.shape[1]
        else:
            rs = slots

        def wait(k, cc, x_ref=x_ref, rs=rs, ssem=ssem, rsem=rsem, axes=axes, g=g, me=me, kind=kind):
            src = (me + g - k) % g
            peer = (me + k) % g
            if kind == "rsag":
                c = rs.shape[1]
                src_ref = x_ref.at[pl.ds(0, c)]
            else:
                src_ref = x_ref
            pltpu.make_async_remote_copy(
                src_ref=src_ref, dst_ref=rs.at[src], send_sem=ssem.at[peer], recv_sem=rsem.at[src],
                device_id=member_coords(axes, peer), device_id_type=MESH).wait_recv()
            pltpu.make_async_remote_copy(
                src_ref=src_ref, dst_ref=rs.at[me], send_sem=ssem.at[peer], recv_sem=rsem.at[me],
                device_id=member_coords(axes, peer), device_id_type=MESH).wait_send()
            return cc

        lax.fori_loop(1, g, wait, 0)
        if kind == "gather":
            o_ref[...] = rs[...]
        elif kind == "sum":
            acc = rs[0]
            for s in range(1, g):
                acc = acc + rs[s]
            o_ref[...] = acc
        else:
            acc = rs[0]
            for s in range(1, g):
                acc = acc + rs[s]
            ag[me] = acc

            def send2(k, cc, ag=ag, ssem2=ssem2, rsem2=rsem2, axes=axes, g=g, me=me):
                peer = (me + k) % g
                pltpu.make_async_remote_copy(
                    src_ref=ag.at[me], dst_ref=ag.at[me], send_sem=ssem2.at[peer], recv_sem=rsem2.at[me],
                    device_id=member_coords(axes, peer), device_id_type=MESH).start()
                return cc

            lax.fori_loop(1, g, send2, 0)

            def wait2(k, cc, ag=ag, ssem2=ssem2, rsem2=rsem2, axes=axes, g=g, me=me):
                src = (me + g - k) % g
                peer = (me + k) % g
                pltpu.make_async_remote_copy(
                    src_ref=ag.at[me], dst_ref=ag.at[src], send_sem=ssem2.at[peer], recv_sem=rsem2.at[src],
                    device_id=member_coords(axes, peer), device_id_type=MESH).wait_recv()
                pltpu.make_async_remote_copy(
                    src_ref=ag.at[me], dst_ref=ag.at[me], send_sem=ssem2.at[peer], recv_sem=rsem2.at[me],
                    device_id=member_coords(axes, peer), device_id_type=MESH).wait_send()
                return cc

            lax.fori_loop(1, g, wait2, 0)
            o_ref[...] = ag[...]


def chol_kernel(g_ref, l_ref, inv_ref):
    a = g_ref[...]
    n = a.shape[0]
    rows = lax.broadcasted_iota(jnp.int32, (n, n), 0)
    lanes = lax.broadcasted_iota(jnp.int32, (n, n), 1)
    eye = (rows == lanes).astype(jnp.float32)
    x = eye
    lmat = jnp.zeros_like(a)
    for j in range(n):
        d = jnp.sqrt(a[j:j + 1, j:j + 1])
        r = 1.0 / d
        col = jnp.where(rows[:, j:j + 1] >= j, a[:, j:j + 1], 0.0) * r
        rowv = jnp.where(lanes[j:j + 1, :] >= j, a[j:j + 1, :], 0.0) * r
        a = a - col * rowv
        lmat = jnp.where(lanes == j, col, lmat)
        xj = x[j:j + 1, :] * r
        below = jnp.where(rows[:, j:j + 1] > j, col, 0.0)
        x = jnp.where(rows == j, xj, x - below * xj)
    l_ref[...] = lmat
    inv_ref[...] = x

def chol_inv(gram):
    n = gram.shape[0]
    gram = jnp.tril(gram) + jnp.tril(gram, -1).T
    return pl.pallas_call(chol_kernel,
        out_shape=[jax.ShapeDtypeStruct((n, n), jnp.float32)] * 2,
        in_specs=[pl.BlockSpec(memory_space=pltpu.VMEM)],
        out_specs=[pl.BlockSpec(memory_space=pltpu.VMEM)] * 2)(gram)


_IDS = {}


def exchange(ops, xs):
    key = ("direct",) + tuple((k, d, x.shape, str(x.dtype)) for (k, d), x in zip(ops, xs))
    if key not in _IDS:
        _IDS[key] = len(_IDS)
    groups = []
    for _, axes in ops:
        if axes not in groups:
            groups.append(axes)
    out_shapes, scratch = [], []
    for (kind, axes), x in zip(ops, xs):
        g = group_size(axes)
        if kind == "sum":
            out_shapes.append(jax.ShapeDtypeStruct(x.shape, x.dtype))
            scratch += [pltpu.VMEM((g,) + x.shape, x.dtype), pltpu.SemaphoreType.DMA((g,)),
                        pltpu.SemaphoreType.DMA((g,))]
        else:
            c = x.shape[0] // g
            out_shapes.append(jax.ShapeDtypeStruct((g, c) + x.shape[1:], x.dtype))
            scratch += [pltpu.VMEM((g, c) + x.shape[1:], x.dtype), pltpu.VMEM((g, c) + x.shape[1:], x.dtype),
                        pltpu.SemaphoreType.DMA((g,)), pltpu.SemaphoreType.DMA((g,)),
                        pltpu.SemaphoreType.DMA((g,)), pltpu.SemaphoreType.DMA((g,))]
    outs = pl.pallas_call(
        functools.partial(direct_kernel, ops, groups),
        out_shape=out_shapes,
        in_specs=[pl.BlockSpec(memory_space=pltpu.VMEM)] * len(xs),
        out_specs=[pl.BlockSpec(memory_space=pltpu.VMEM)] * len(xs),
        scratch_shapes=scratch,
        compiler_params=pltpu.CompilerParams(collective_id=_IDS[key], has_side_effects=True),
    )(*xs)
    return [o.reshape(x.shape) for o, x in zip(outs, xs)]


def exchange_bfly(ops, xs):
    key = ("bfly",) + tuple((k, d, x.shape, str(x.dtype)) for (k, d), x in zip(ops, xs))
    if key not in _IDS:
        _IDS[key] = len(_IDS)
    out_shapes, scratch = [], []
    for (kind, digits), x in zip(ops, xs):
        g = group_size(digits)
        rmax = max(mod for _, _, mod in digits)
        out_shapes.append(jax.ShapeDtypeStruct((g,) + x.shape, x.dtype))
        scratch += [pltpu.VMEM((g,) + x.shape, x.dtype),
                    pltpu.SemaphoreType.DMA((len(digits), rmax)), pltpu.SemaphoreType.DMA((len(digits), rmax))]
    outs = pl.pallas_call(
        functools.partial(exchange_kernel, ops),
        out_shape=out_shapes,
        in_specs=[pl.BlockSpec(memory_space=pltpu.VMEM)] * len(xs),
        out_specs=[pl.BlockSpec(memory_space=pltpu.VMEM)] * len(xs),
        scratch_shapes=scratch,
        compiler_params=pltpu.CompilerParams(collective_id=_IDS[key], has_side_effects=True),
    )(*xs)
    return list(outs)


def make_local(sizes, row_axes, col_axes):
    def local(particles, start_basis):
        shard = particles.shape[0]
        width = particles.shape[1]
        eig = start_basis.shape[1]
        total = shard * math.prod(sizes.values())
        spread = 2.0 * width
        root_total = math.sqrt(float(total))

        dense_basis = start_basis.reshape(shard * eig // 128, 128)
        i_feats, i_basis, j_feats = exchange_bfly(
            [("gather", row_axes), ("gather", row_axes), ("gather", col_axes)],
            [particles, dense_basis, particles])
        gi = group_size(row_axes)
        gj = group_size(col_axes)
        i_feats = i_feats.reshape(gi * shard, width)
        j_feats = j_feats.reshape(gj * shard, width)
        basis_i = i_basis.reshape(gi * shard, eig)

        def block_ids(digits):
            coords = member_coords(digits, jnp.arange(group_size(digits), dtype=jnp.int32))
            flat = jnp.zeros((group_size(digits),), jnp.int32)
            for a, cval in zip(MESH_AXES, coords):
                flat = flat * sizes[a] + cval
            return (flat[:, None] * shard + jnp.arange(shard, dtype=jnp.int32)[None, :]).reshape(-1)

        ids_i = block_ids(row_axes)
        ids_j = block_ids(col_axes)
        sq_i = jnp.sum(jnp.square(i_feats.astype(jnp.float32)), axis=1)
        sq_j = jnp.sum(jnp.square(j_feats.astype(jnp.float32)), axis=1)
        dots = lax.dot_general(i_feats, j_feats, (((1,), (1,)), ((), ())), preferred_element_type=jnp.float32)
        distance = sq_i[:, None] + sq_j[None, :] - 2.0 * dots
        tile = jnp.where(ids_i[:, None] == ids_j[None, :], jnp.float32(0.0), jnp.exp(-distance / spread))

        deg_i, deg_j = exchange(
            [("sum", row_axes), ("sum", col_axes)],
            [jnp.sum(tile, axis=1).reshape(-1, 128), jnp.sum(tile, axis=0).reshape(-1, 128)])
        deg_i = deg_i.reshape(-1)
        deg_j = deg_j.reshape(-1)
        root_i = jnp.sqrt(deg_i)
        root_j = jnp.sqrt(deg_j)
        me_i = group_pos(row_axes)
        scaled_i = basis_i / root_i[:, None]
        prod_j = lax.dot_general(tile, scaled_i, (((0,), (0,)), ((), ())), precision=HIGH)
        extra = jnp.concatenate([jnp.dot(root_i, basis_i, precision=HIGH)[None, :],
                                 jnp.broadcast_to(jnp.sum(deg_i), (1, eig)),
                                 jnp.zeros((6, eig), jnp.float32)], axis=0)
        dense_j, extra = exchange(
            [("rsag", col_axes), ("sum", col_axes)], [prod_j.reshape(-1, 128), extra.reshape(-1, 128)])
        prod_j = dense_j.reshape(-1, eig)
        extra = extra.reshape(-1, eig)
        inv_s = 1.0 / jnp.sqrt(extra[1, 0])
        aligned = extra[0] * inv_s
        defl_j = prod_j / root_j[:, None] - (root_j * inv_s)[:, None] * aligned[None, :]

        gram = lax.dot_general(defl_j, defl_j, (((0,), (0,)), ((), ())), precision=HIGH).reshape(-1, 128)
        q_i = jnp.dot(tile, defl_j / root_j[:, None], precision=HIGH)
        aligned_part = jnp.pad(jnp.dot(root_j, defl_j, precision=HIGH), (0, 128 - eig))[None, :]
        small = jnp.concatenate([gram, aligned_part,
                                 jnp.zeros((2 * gi - gram.shape[0] - 1, 128), jnp.float32)], axis=0)
        small, q_i = exchange([("rsag", row_axes), ("rsag", row_axes)], [small, q_i.reshape(-1, 128)])
        gram = small[:eig * eig // 128]
        part = small[eig * eig // 128:][:1, :eig]
        factor, inverse = chol_inv(gram.reshape(eig, eig))
        q_i = q_i.reshape(-1, eig)
        prod_i = lax.dot_general(q_i, inverse, (((1,), (1,)), ((), ())), precision=HIGH) * root_total
        aligned = jnp.dot(inverse, part[0], precision=HIGH) * (root_total * inv_s)
        defl_i = prod_i / root_i[:, None] - (root_i * inv_s)[:, None] * aligned[None, :]

        gram = lax.dot_general(defl_i, defl_i, (((0,), (0,)), ((), ())), precision=HIGH).reshape(-1, 128)
        (gram,) = exchange([("sum", col_axes)], [gram])
        factor, inverse = chol_inv(gram.reshape(eig, eig))
        own = lax.dynamic_slice_in_dim(defl_i, me_i * shard, shard, 0)
        basis_own = lax.dot_general(own, inverse, (((1,), (1,)), ((), ())), precision=HIGH) * root_total
        return basis_own, factor

    return local


def solution(mesh):
    sizes = dict(mesh.shape)
    placed = (P(MESH_AXES, None), P(MESH_AXES, None))
    return jax.shard_map(
        make_local(sizes, (("row", 1, 2), ("vec", 1, sizes["vec"]), ("row", 2, sizes["row"] // 2)),
                   (("col", 1, 2), ("col", 2, sizes["col"] // 2))),
        mesh=mesh,
        in_specs=placed,
        out_specs=(P(MESH_AXES, None), P()),
        check_vma=False,
    )
```

```python
import functools
import math

import jax
import jax.numpy as jnp
from jax import lax
from jax.experimental import pallas as pl
from jax.experimental.pallas import tpu as pltpu
from jax.sharding import PartitionSpec as P

ITERS = 2
MESH_AXES = ("row", "col", "vec")
MESH = pl.DeviceIdType.MESH
HIGH = lax.Precision.HIGHEST


def group_pos(digits):
    me = 0
    for a, div, mod in digits:
        me = me * mod + (lax.axis_index(a) // div) % mod
    return me


def group_size(digits):
    return math.prod(mod for _, _, mod in digits)


def member_coords(digits, m):
    own = {a: lax.axis_index(a) for a in MESH_AXES}
    coords = dict(own)
    rem = m
    for a, div, mod in reversed(digits):
        d = rem % mod
        rem = rem // mod
        coords[a] = coords[a] - ((own[a] // div) % mod) * div + d * div
    return tuple(coords[a] for a in MESH_AXES)


def op_rounds(kind, g):
    bits = g.bit_length() - 1
    return 2 * bits if kind == "rsag" else bits


def exchange_kernel(ops, *refs):
    n = len(ops)
    ins, outs, scr = refs[:n], refs[n:2 * n], refs[2 * n:]
    barrier = pltpu.get_barrier_semaphore()
    groups = []
    for _, digits in ops:
        if digits not in groups:
            groups.append(digits)
    count = 0
    for digits in groups:
        me = group_pos(digits)
        span = 1
        for _, _, radix in reversed(digits):
            mine = (me // span) % radix
            for dd in range(1, radix):
                partner = me + ((mine + dd) % radix - mine) * span
                pl.semaphore_signal(barrier, inc=1, device_id=member_coords(digits, partner), device_id_type=MESH)
                count += 1
            span *= radix
    pl.semaphore_wait(barrier, count)

    state = []
    for i, (kind, digits) in enumerate(ops):
        w, ssem, rsem = scr[3 * i:3 * i + 3]
        w[group_pos(digits)] = ins[i][...]
        state.append((w, ssem, rsem))

    nrounds = max(len(d) for _, d in ops)
    for t in range(nrounds):
        waits = []
        for i, (kind, digits) in enumerate(ops):
            if t >= len(digits):
                continue
            radices = [mod for _, _, mod in reversed(digits)]
            radix = radices[t]
            span = math.prod(radices[:t])
            me = group_pos(digits)
            mine = (me // span) % radix
            base = (me // span) * span
            w, ssem, rsem = state[i]
            for dd in range(1, radix):
                partner = me + ((mine + dd) % radix - mine) * span
                sender = base + ((mine + radix - dd) % radix - mine) * span
                out = pltpu.make_async_remote_copy(
                    src_ref=w.at[pl.ds(base, span)], dst_ref=w.at[pl.ds(base, span)],
                    send_sem=ssem.at[t, dd], recv_sem=rsem.at[t, dd],
                    device_id=member_coords(digits, partner), device_id_type=MESH)
                out.start()
                back = pltpu.make_async_remote_copy(
                    src_ref=w.at[pl.ds(base, span)], dst_ref=w.at[pl.ds(sender, span)],
                    send_sem=ssem.at[t, dd], recv_sem=rsem.at[t, dd],
                    device_id=member_coords(digits, partner), device_id_type=MESH)
                waits.append((out, back))
        for out, back in waits:
            back.wait_recv()
            out.wait_send()
    for i in range(n):
        outs[i][...] = state[i][0][...]


def direct_kernel(ops, groups, *refs):
    n = len(ops)
    ins, outs, scr = refs[:n], refs[n:2 * n], refs[2 * n:]
    barrier = pltpu.get_barrier_semaphore()
    total_peers = 0
    for axes in groups:
        g = group_size(axes)
        me = group_pos(axes)
        total_peers += g - 1

        def greet(k, c, axes=axes, g=g, me=me):
            pl.semaphore_signal(barrier, inc=1, device_id=member_coords(axes, (me + k) % g), device_id_type=MESH)
            return c

        lax.fori_loop(1, g, greet, 0)
    pl.semaphore_wait(barrier, total_peers)

    pos = 0
    pending = []
    for i, (kind, axes) in enumerate(ops):
        g = group_size(axes)
        me = group_pos(axes)
        x_ref, o_ref = ins[i], outs[i]
        if kind in ("gather", "sum"):
            slots, ssem, rsem = scr[pos:pos + 3]
            pos += 3
            slots[me] = x_ref[...]

            def send(k, c, x_ref=x_ref, slots=slots, ssem=ssem, rsem=rsem, axes=axes, g=g, me=me):
                peer = (me + k) % g
                pltpu.make_async_remote_copy(
                    src_ref=x_ref, dst_ref=slots.at[me], send_sem=ssem.at[peer], recv_sem=rsem.at[me],
                    device_id=member_coords(axes, peer), device_id_type=MESH).start()
                return c

            lax.fori_loop(1, g, send, 0)
            pending.append((kind, axes, g, me, x_ref, o_ref, slots, ssem, rsem))
        else:
            rs, ag, ssem, rsem, ssem2, rsem2 = scr[pos:pos + 6]
            pos += 6
            c = x_ref.shape[0] // g
            rs[me] = x_ref[pl.ds(pl.multiple_of(me * c, c), c)]

            def send(k, cc, x_ref=x_ref, rs=rs, ssem=ssem, rsem=rsem, axes=axes, g=g, me=me, c=c):
                peer = (me + k) % g
                pltpu.make_async_remote_copy(
                    src_ref=x_ref.at[pl.ds(pl.multiple_of(peer * c, c), c)], dst_ref=rs.at[me],
                    send_sem=ssem.at[peer], recv_sem=rsem.at[me],
                    device_id=member_coords(axes, peer), device_id_type=MESH).start()
                return cc

            lax.fori_loop(1, g, send, 0)
            pending.append((kind, axes, g, me, x_ref, o_ref, (rs, ag, ssem2, rsem2), ssem, rsem))

    second = []
    for kind, axes, g, me, x_ref, o_ref, slots, ssem, rsem in pending:
        if kind == "rsag":
            rs, ag, ssem2, rsem2 = slots
            c = rs.shape[1]
        else:
            rs = slots

        def wait(k, cc, x_ref=x_ref, rs=rs, ssem=ssem, rsem=rsem, axes=axes, g=g, me=me, kind=kind):
            src = (me + g - k) % g
            peer = (me + k) % g
            if kind == "rsag":
                c = rs.shape[1]
                src_ref = x_ref.at[pl.ds(0, c)]
            else:
                src_ref = x_ref
            pltpu.make_async_remote_copy(
                src_ref=src_ref, dst_ref=rs.at[src], send_sem=ssem.at[peer], recv_sem=rsem.at[src],
                device_id=member_coords(axes, peer), device_id_type=MESH).wait_recv()
            pltpu.make_async_remote_copy(
                src_ref=src_ref, dst_ref=rs.at[me], send_sem=ssem.at[peer], recv_sem=rsem.at[me],
                device_id=member_coords(axes, peer), device_id_type=MESH).wait_send()
            return cc

        lax.fori_loop(1, g, wait, 0)
        if kind == "gather":
            o_ref[...] = rs[...]
        elif kind == "sum":
            acc = rs[0]
            for s in range(1, g):
                acc = acc + rs[s]
            o_ref[...] = acc
        else:
            acc = rs[0]
            for s in range(1, g):
                acc = acc + rs[s]
            ag[me] = acc

            def send2(k, cc, ag=ag, ssem2=ssem2, rsem2=rsem2, axes=axes, g=g, me=me):
                peer = (me + k) % g
                pltpu.make_async_remote_copy(
                    src_ref=ag.at[me], dst_ref=ag.at[me], send_sem=ssem2.at[peer], recv_sem=rsem2.at[me],
                    device_id=member_coords(axes, peer), device_id_type=MESH).start()
                return cc

            lax.fori_loop(1, g, send2, 0)
            second.append((axes, g, me, o_ref, ag, ssem2, rsem2))

    for axes, g, me, o_ref, ag, ssem2, rsem2 in second:
        if g > 1:

            def wait2(k, cc, ag=ag, ssem2=ssem2, rsem2=rsem2, axes=axes, g=g, me=me):
                src = (me + g - k) % g
                peer = (me + k) % g
                pltpu.make_async_remote_copy(
                    src_ref=ag.at[me], dst_ref=ag.at[src], send_sem=ssem2.at[peer], recv_sem=rsem2.at[src],
                    device_id=member_coords(axes, peer), device_id_type=MESH).wait_recv()
                pltpu.make_async_remote_copy(
                    src_ref=ag.at[me], dst_ref=ag.at[me], send_sem=ssem2.at[peer], recv_sem=rsem2.at[me],
                    device_id=member_coords(axes, peer), device_id_type=MESH).wait_send()
                return cc

            lax.fori_loop(1, g, wait2, 0)
            o_ref[...] = ag[...]


def chol_kernel(g_ref, l_ref, inv_ref):
    a = g_ref[...]
    n = a.shape[0]
    rows = lax.broadcasted_iota(jnp.int32, (n, n), 0)
    lanes = lax.broadcasted_iota(jnp.int32, (n, n), 1)
    eye = (rows == lanes).astype(jnp.float32)
    x = eye
    lmat = jnp.zeros_like(a)
    for j in range(n):
        d = jnp.sqrt(a[j:j + 1, j:j + 1])
        r = 1.0 / d
        col = jnp.where(rows[:, j:j + 1] >= j, a[:, j:j + 1], 0.0) * r
        rowv = jnp.where(lanes[j:j + 1, :] >= j, a[j:j + 1, :], 0.0) * r
        a = a - col * rowv
        lmat = jnp.where(lanes == j, col, lmat)
        xj = x[j:j + 1, :] * r
        below = jnp.where(rows[:, j:j + 1] > j, col, 0.0)
        x = jnp.where(rows == j, xj, x - below * xj)
    l_ref[...] = lmat
    inv_ref[...] = x

def chol_inv(gram):
    n = gram.shape[0]
    gram = jnp.tril(gram) + jnp.tril(gram, -1).T
    return pl.pallas_call(chol_kernel,
        out_shape=[jax.ShapeDtypeStruct((n, n), jnp.float32)] * 2,
        in_specs=[pl.BlockSpec(memory_space=pltpu.VMEM)],
        out_specs=[pl.BlockSpec(memory_space=pltpu.VMEM)] * 2)(gram)


_IDS = {}


def exchange(ops, xs):
    key = ("direct",) + tuple((k, d, x.shape, str(x.dtype)) for (k, d), x in zip(ops, xs))
    if key not in _IDS:
        _IDS[key] = len(_IDS)
    groups = []
    for _, axes in ops:
        if axes not in groups:
            groups.append(axes)
    out_shapes, scratch = [], []
    for (kind, axes), x in zip(ops, xs):
        g = group_size(axes)
        if kind == "sum":
            out_shapes.append(jax.ShapeDtypeStruct(x.shape, x.dtype))
            scratch += [pltpu.VMEM((g,) + x.shape, x.dtype), pltpu.SemaphoreType.DMA((g,)),
                        pltpu.SemaphoreType.DMA((g,))]
        else:
            c = x.shape[0] // g
            out_shapes.append(jax.ShapeDtypeStruct((g, c) + x.shape[1:], x.dtype))
            scratch += [pltpu.VMEM((g, c) + x.shape[1:], x.dtype), pltpu.VMEM((g, c) + x.shape[1:], x.dtype),
                        pltpu.SemaphoreType.DMA((g,)), pltpu.SemaphoreType.DMA((g,)),
                        pltpu.SemaphoreType.DMA((g,)), pltpu.SemaphoreType.DMA((g,))]
    outs = pl.pallas_call(
        functools.partial(direct_kernel, ops, groups),
        out_shape=out_shapes,
        in_specs=[pl.BlockSpec(memory_space=pltpu.VMEM)] * len(xs),
        out_specs=[pl.BlockSpec(memory_space=pltpu.VMEM)] * len(xs),
        scratch_shapes=scratch,
        compiler_params=pltpu.CompilerParams(collective_id=_IDS[key], has_side_effects=True),
    )(*xs)
    return [o.reshape(x.shape) for o, x in zip(outs, xs)]


def exchange_bfly(ops, xs):
    key = ("bfly",) + tuple((k, d, x.shape, str(x.dtype)) for (k, d), x in zip(ops, xs))
    if key not in _IDS:
        _IDS[key] = len(_IDS)
    out_shapes, scratch = [], []
    for (kind, digits), x in zip(ops, xs):
        g = group_size(digits)
        rmax = max(mod for _, _, mod in digits)
        out_shapes.append(jax.ShapeDtypeStruct((g,) + x.shape, x.dtype))
        scratch += [pltpu.VMEM((g,) + x.shape, x.dtype),
                    pltpu.SemaphoreType.DMA((len(digits), rmax)), pltpu.SemaphoreType.DMA((len(digits), rmax))]
    outs = pl.pallas_call(
        functools.partial(exchange_kernel, ops),
        out_shape=out_shapes,
        in_specs=[pl.BlockSpec(memory_space=pltpu.VMEM)] * len(xs),
        out_specs=[pl.BlockSpec(memory_space=pltpu.VMEM)] * len(xs),
        scratch_shapes=scratch,
        compiler_params=pltpu.CompilerParams(collective_id=_IDS[key], has_side_effects=True),
    )(*xs)
    return list(outs)


def make_local(sizes, row_axes, col_axes):
    def local(particles, start_basis):
        shard = particles.shape[0]
        width = particles.shape[1]
        eig = start_basis.shape[1]
        total = shard * math.prod(sizes.values())
        spread = 2.0 * width
        root_total = math.sqrt(float(total))

        dense_basis = start_basis.reshape(shard * eig // 128, 128)
        i_feats, i_basis, j_feats = exchange_bfly(
            [("gather", row_axes), ("gather", row_axes), ("gather", col_axes)],
            [particles, dense_basis, particles])
        gi = group_size(row_axes)
        gj = group_size(col_axes)
        i_feats = i_feats.reshape(gi * shard, width)
        j_feats = j_feats.reshape(gj * shard, width)
        basis_i = i_basis.reshape(gi * shard, eig)

        def block_ids(digits):
            coords = member_coords(digits, jnp.arange(group_size(digits), dtype=jnp.int32))
            flat = jnp.zeros((group_size(digits),), jnp.int32)
            for a, cval in zip(MESH_AXES, coords):
                flat = flat * sizes[a] + cval
            return (flat[:, None] * shard + jnp.arange(shard, dtype=jnp.int32)[None, :]).reshape(-1)

        ids_i = block_ids(row_axes)
        ids_j = block_ids(col_axes)
        sq_i = jnp.sum(jnp.square(i_feats.astype(jnp.float32)), axis=1)
        sq_j = jnp.sum(jnp.square(j_feats.astype(jnp.float32)), axis=1)
        dots = lax.dot_general(i_feats, j_feats, (((1,), (1,)), ((), ())), preferred_element_type=jnp.float32)
        distance = sq_i[:, None] + sq_j[None, :] - 2.0 * dots
        tile = jnp.where(ids_i[:, None] == ids_j[None, :], jnp.float32(0.0), jnp.exp(-distance / spread))

        deg_i, deg_j = exchange(
            [("sum", row_axes), ("sum", col_axes)],
            [jnp.sum(tile, axis=1).reshape(-1, 128), jnp.sum(tile, axis=0).reshape(-1, 128)])
        deg_i = deg_i.reshape(-1)
        deg_j = deg_j.reshape(-1)
        root_i = jnp.sqrt(deg_i)
        root_j = jnp.sqrt(deg_j)
        me_i = group_pos(row_axes)
        scaled_i = basis_i / root_i[:, None]
        prod_j = lax.dot_general(tile, scaled_i, (((0,), (0,)), ((), ())), precision=HIGH)
        extra = jnp.concatenate([jnp.dot(root_i, basis_i, precision=HIGH)[None, :],
                                 jnp.broadcast_to(jnp.sum(deg_i), (1, eig)),
                                 jnp.zeros((6, eig), jnp.float32)], axis=0)
        dense_j, extra = exchange(
            [("rsag", col_axes), ("sum", col_axes)], [prod_j.reshape(-1, 128), extra.reshape(-1, 128)])
        prod_j = dense_j.reshape(-1, eig)
        extra = extra.reshape(-1, eig)
        inv_s = 1.0 / jnp.sqrt(extra[1, 0])
        aligned = extra[0] * inv_s
        defl_j = prod_j / root_j[:, None] - (root_j * inv_s)[:, None] * aligned[None, :]

        gram = lax.dot_general(defl_j, defl_j, (((0,), (0,)), ((), ())), precision=HIGH).reshape(-1, 128)
        q_i = jnp.dot(tile, defl_j / root_j[:, None], precision=HIGH)
        aligned_part = jnp.pad(jnp.dot(root_j, defl_j, precision=HIGH), (0, 128 - eig))[None, :]
        small = jnp.concatenate([gram, aligned_part,
                                 jnp.zeros((2 * gi - gram.shape[0] - 1, 128), jnp.float32)], axis=0)
        small, q_i = exchange([("rsag", row_axes), ("rsag", row_axes)], [small, q_i.reshape(-1, 128)])
        gram = small[:eig * eig // 128]
        part = small[eig * eig // 128:][:1, :eig]
        factor, inverse = chol_inv(gram.reshape(eig, eig))
        q_i = q_i.reshape(-1, eig)
        prod_i = lax.dot_general(q_i, inverse, (((1,), (1,)), ((), ())), precision=HIGH) * root_total
        aligned = jnp.dot(inverse, part[0], precision=HIGH) * (root_total * inv_s)
        defl_i = prod_i / root_i[:, None] - (root_i * inv_s)[:, None] * aligned[None, :]

        gram = lax.dot_general(defl_i, defl_i, (((0,), (0,)), ((), ())), precision=HIGH).reshape(-1, 128)
        (gram,) = exchange([("sum", col_axes)], [gram])
        factor, inverse = chol_inv(gram.reshape(eig, eig))
        own = lax.dynamic_slice_in_dim(defl_i, me_i * shard, shard, 0)
        basis_own = lax.dot_general(own, inverse, (((1,), (1,)), ((), ())), precision=HIGH) * root_total
        return basis_own, factor

    return local


def solution(mesh):
    sizes = dict(mesh.shape)
    placed = (P(MESH_AXES, None), P(MESH_AXES, None))
    return jax.shard_map(
        make_local(sizes, (("row", 1, 2), ("vec", 1, sizes["vec"]), ("row", 2, sizes["row"] // 2)),
                   (("col", 1, 2), ("col", 2, sizes["col"] // 2))),
        mesh=mesh,
        in_specs=placed,
        out_specs=(P(MESH_AXES, None), P()),
        check_vma=False,
    )
```

```python
import functools
import math

import jax
import jax.numpy as jnp
from jax import lax
from jax.experimental import pallas as pl
from jax.experimental.pallas import tpu as pltpu
from jax.sharding import PartitionSpec as P

ITERS = 2
MESH_AXES = ("row", "col", "vec")
MESH = pl.DeviceIdType.MESH
HIGH = lax.Precision.HIGHEST


def group_pos(digits):
    me = 0
    for a, div, mod in digits:
        me = me * mod + (lax.axis_index(a) // div) % mod
    return me


def group_size(digits):
    return math.prod(mod for _, _, mod in digits)


def member_coords(digits, m):
    own = {a: lax.axis_index(a) for a in MESH_AXES}
    coords = dict(own)
    rem = m
    for a, div, mod in reversed(digits):
        d = rem % mod
        rem = rem // mod
        coords[a] = coords[a] - ((own[a] // div) % mod) * div + d * div
    return tuple(coords[a] for a in MESH_AXES)


def op_rounds(kind, g):
    bits = g.bit_length() - 1
    return 2 * bits if kind == "rsag" else bits


def exchange_kernel(ops, *refs):
    n = len(ops)
    ins, outs, scr = refs[:n], refs[n:2 * n], refs[2 * n:]
    barrier = pltpu.get_barrier_semaphore()
    groups = []
    for _, digits in ops:
        if digits not in groups:
            groups.append(digits)
    count = 0
    for digits in groups:
        me = group_pos(digits)
        span = 1
        for _, _, radix in reversed(digits):
            mine = (me // span) % radix
            for dd in range(1, radix):
                partner = me + ((mine + dd) % radix - mine) * span
                pl.semaphore_signal(barrier, inc=1, device_id=member_coords(digits, partner), device_id_type=MESH)
                count += 1
            span *= radix
    pl.semaphore_wait(barrier, count)

    state = []
    for i, (kind, digits) in enumerate(ops):
        w, ssem, rsem = scr[3 * i:3 * i + 3]
        w[group_pos(digits)] = ins[i][...]
        state.append((w, ssem, rsem))

    nrounds = max(len(d) for _, d in ops)
    for t in range(nrounds):
        waits = []
        for i, (kind, digits) in enumerate(ops):
            if t >= len(digits):
                continue
            radices = [mod for _, _, mod in reversed(digits)]
            radix = radices[t]
            span = math.prod(radices[:t])
            me = group_pos(digits)
            mine = (me // span) % radix
            base = (me // span) * span
            w, ssem, rsem = state[i]
            for dd in range(1, radix):
                partner = me + ((mine + dd) % radix - mine) * span
                sender = base + ((mine + radix - dd) % radix - mine) * span
                out = pltpu.make_async_remote_copy(
                    src_ref=w.at[pl.ds(base, span)], dst_ref=w.at[pl.ds(base, span)],
                    send_sem=ssem.at[t, dd], recv_sem=rsem.at[t, dd],
                    device_id=member_coords(digits, partner), device_id_type=MESH)
                out.start()
                back = pltpu.make_async_remote_copy(
                    src_ref=w.at[pl.ds(base, span)], dst_ref=w.at[pl.ds(sender, span)],
                    send_sem=ssem.at[t, dd], recv_sem=rsem.at[t, dd],
                    device_id=member_coords(digits, partner), device_id_type=MESH)
                waits.append((out, back))
        for out, back in waits:
            back.wait_recv()
            out.wait_send()
    for i in range(n):
        outs[i][...] = state[i][0][...]


def direct_kernel(ops, groups, *refs):
    n = len(ops)
    ins, outs, scr = refs[:n], refs[n:2 * n], refs[2 * n:]
    barrier = pltpu.get_barrier_semaphore()
    total_peers = 0
    for axes in groups:
        g = group_size(axes)
        me = group_pos(axes)
        total_peers += g - 1

        def greet(k, c, axes=axes, g=g, me=me):
            pl.semaphore_signal(barrier, inc=1, device_id=member_coords(axes, (me + k) % g), device_id_type=MESH)
            return c

        lax.fori_loop(1, g, greet, 0)
    pl.semaphore_wait(barrier, total_peers)

    pos = 0
    pending = []
    for i, (kind, axes) in enumerate(ops):
        g = group_size(axes)
        me = group_pos(axes)
        x_ref, o_ref = ins[i], outs[i]
        if kind in ("gather", "sum"):
            slots, ssem, rsem = scr[pos:pos + 3]
            pos += 3
            slots[me] = x_ref[...]

            def send(k, c, x_ref=x_ref, slots=slots, ssem=ssem, rsem=rsem, axes=axes, g=g, me=me):
                peer = (me + k) % g
                pltpu.make_async_remote_copy(
                    src_ref=x_ref, dst_ref=slots.at[me], send_sem=ssem.at[peer], recv_sem=rsem.at[me],
                    device_id=member_coords(axes, peer), device_id_type=MESH).start()
                return c

            lax.fori_loop(1, g, send, 0)
            pending.append((kind, axes, g, me, x_ref, o_ref, slots, ssem, rsem))
        else:
            rs, ag, ssem, rsem, ssem2, rsem2 = scr[pos:pos + 6]
            pos += 6
            c = x_ref.shape[0] // g
            rs[me] = x_ref[pl.ds(pl.multiple_of(me * c, c), c)]

            def send(k, cc, x_ref=x_ref, rs=rs, ssem=ssem, rsem=rsem, axes=axes, g=g, me=me, c=c):
                peer = (me + k) % g
                pltpu.make_async_remote_copy(
                    src_ref=x_ref.at[pl.ds(pl.multiple_of(peer * c, c), c)], dst_ref=rs.at[me],
                    send_sem=ssem.at[peer], recv_sem=rsem.at[me],
                    device_id=member_coords(axes, peer), device_id_type=MESH).start()
                return cc

            lax.fori_loop(1, g, send, 0)
            pending.append((kind, axes, g, me, x_ref, o_ref, (rs, ag, ssem2, rsem2), ssem, rsem))

    second = []
    for kind, axes, g, me, x_ref, o_ref, slots, ssem, rsem in pending:
        if kind == "rsag":
            rs, ag, ssem2, rsem2 = slots
            c = rs.shape[1]
        else:
            rs = slots

        def wait(k, cc, x_ref=x_ref, rs=rs, ssem=ssem, rsem=rsem, axes=axes, g=g, me=me, kind=kind):
            src = (me + g - k) % g
            peer = (me + k) % g
            if kind == "rsag":
                c = rs.shape[1]
                src_ref = x_ref.at[pl.ds(0, c)]
            else:
                src_ref = x_ref
            pltpu.make_async_remote_copy(
                src_ref=src_ref, dst_ref=rs.at[src], send_sem=ssem.at[peer], recv_sem=rsem.at[src],
                device_id=member_coords(axes, peer), device_id_type=MESH).wait_recv()
            pltpu.make_async_remote_copy(
                src_ref=src_ref, dst_ref=rs.at[me], send_sem=ssem.at[peer], recv_sem=rsem.at[me],
                device_id=member_coords(axes, peer), device_id_type=MESH).wait_send()
            return cc

        lax.fori_loop(1, g, wait, 0)
        if kind == "gather":
            o_ref[...] = rs[...]
        elif kind == "sum":
            acc = rs[0]
            for s in range(1, g):
                acc = acc + rs[s]
            o_ref[...] = acc
        else:
            acc = rs[0]
            for s in range(1, g):
                acc = acc + rs[s]
            ag[me] = acc

            def send2(k, cc, ag=ag, ssem2=ssem2, rsem2=rsem2, axes=axes, g=g, me=me):
                peer = (me + k) % g
                pltpu.make_async_remote_copy(
                    src_ref=ag.at[me], dst_ref=ag.at[me], send_sem=ssem2.at[peer], recv_sem=rsem2.at[me],
                    device_id=member_coords(axes, peer), device_id_type=MESH).start()
                return cc

            lax.fori_loop(1, g, send2, 0)
            second.append((axes, g, me, o_ref, ag, ssem2, rsem2))

    for axes, g, me, o_ref, ag, ssem2, rsem2 in second:
        if g > 1:

            def wait2(k, cc, ag=ag, ssem2=ssem2, rsem2=rsem2, axes=axes, g=g, me=me):
                src = (me + g - k) % g
                peer = (me + k) % g
                pltpu.make_async_remote_copy(
                    src_ref=ag.at[me], dst_ref=ag.at[src], send_sem=ssem2.at[peer], recv_sem=rsem2.at[src],
                    device_id=member_coords(axes, peer), device_id_type=MESH).wait_recv()
                pltpu.make_async_remote_copy(
                    src_ref=ag.at[me], dst_ref=ag.at[me], send_sem=ssem2.at[peer], recv_sem=rsem2.at[me],
                    device_id=member_coords(axes, peer), device_id_type=MESH).wait_send()
                return cc

            lax.fori_loop(1, g, wait2, 0)
            o_ref[...] = ag[...]


def chol_kernel(g_ref, l_ref, inv_ref):
    a = g_ref[...]
    n = a.shape[0]
    rows = lax.broadcasted_iota(jnp.int32, (n, n), 0)
    lanes = lax.broadcasted_iota(jnp.int32, (n, n), 1)
    eye = (rows == lanes).astype(jnp.float32)
    x = eye
    lmat = jnp.zeros_like(a)
    for j in range(n):
        d = jnp.sqrt(a[j:j + 1, j:j + 1])
        r = 1.0 / d
        col = jnp.where(rows[:, j:j + 1] >= j, a[:, j:j + 1], 0.0) * r
        rowv = jnp.where(lanes[j:j + 1, :] >= j, a[j:j + 1, :], 0.0) * r
        a = a - col * rowv
        lmat = jnp.where(lanes == j, col, lmat)
        xj = x[j:j + 1, :] * r
        below = jnp.where(rows[:, j:j + 1] > j, col, 0.0)
        x = jnp.where(rows == j, xj, x - below * xj)
    l_ref[...] = lmat
    inv_ref[...] = x

def chol_inv(gram):
    n = gram.shape[0]
    gram = jnp.tril(gram) + jnp.tril(gram, -1).T
    return pl.pallas_call(chol_kernel,
        out_shape=[jax.ShapeDtypeStruct((n, n), jnp.float32)] * 2,
        in_specs=[pl.BlockSpec(memory_space=pltpu.VMEM)],
        out_specs=[pl.BlockSpec(memory_space=pltpu.VMEM)] * 2)(gram)


_IDS = {}


def exchange(ops, xs):
    key = ("direct",) + tuple((k, d, x.shape, str(x.dtype)) for (k, d), x in zip(ops, xs))
    if key not in _IDS:
        _IDS[key] = len(_IDS)
    groups = []
    for _, axes in ops:
        if axes not in groups:
            groups.append(axes)
    out_shapes, scratch = [], []
    for (kind, axes), x in zip(ops, xs):
        g = group_size(axes)
        if kind == "sum":
            out_shapes.append(jax.ShapeDtypeStruct(x.shape, x.dtype))
            scratch += [pltpu.VMEM((g,) + x.shape, x.dtype), pltpu.SemaphoreType.DMA((g,)),
                        pltpu.SemaphoreType.DMA((g,))]
        else:
            c = x.shape[0] // g
            out_shapes.append(jax.ShapeDtypeStruct((g, c) + x.shape[1:], x.dtype))
            scratch += [pltpu.VMEM((g, c) + x.shape[1:], x.dtype), pltpu.VMEM((g, c) + x.shape[1:], x.dtype),
                        pltpu.SemaphoreType.DMA((g,)), pltpu.SemaphoreType.DMA((g,)),
                        pltpu.SemaphoreType.DMA((g,)), pltpu.SemaphoreType.DMA((g,))]
    outs = pl.pallas_call(
        functools.partial(direct_kernel, ops, groups),
        out_shape=out_shapes,
        in_specs=[pl.BlockSpec(memory_space=pltpu.VMEM)] * len(xs),
        out_specs=[pl.BlockSpec(memory_space=pltpu.VMEM)] * len(xs),
        scratch_shapes=scratch,
        compiler_params=pltpu.CompilerParams(collective_id=_IDS[key], has_side_effects=True),
    )(*xs)
    return [o.reshape(x.shape) for o, x in zip(outs, xs)]


def exchange_bfly(ops, xs):
    key = ("bfly",) + tuple((k, d, x.shape, str(x.dtype)) for (k, d), x in zip(ops, xs))
    if key not in _IDS:
        _IDS[key] = len(_IDS)
    out_shapes, scratch = [], []
    for (kind, digits), x in zip(ops, xs):
        g = group_size(digits)
        rmax = max(mod for _, _, mod in digits)
        out_shapes.append(jax.ShapeDtypeStruct((g,) + x.shape, x.dtype))
        scratch += [pltpu.VMEM((g,) + x.shape, x.dtype),
                    pltpu.SemaphoreType.DMA((len(digits), rmax)), pltpu.SemaphoreType.DMA((len(digits), rmax))]
    outs = pl.pallas_call(
        functools.partial(exchange_kernel, ops),
        out_shape=out_shapes,
        in_specs=[pl.BlockSpec(memory_space=pltpu.VMEM)] * len(xs),
        out_specs=[pl.BlockSpec(memory_space=pltpu.VMEM)] * len(xs),
        scratch_shapes=scratch,
        compiler_params=pltpu.CompilerParams(collective_id=_IDS[key], has_side_effects=True),
    )(*xs)
    return list(outs)


def make_local(sizes, row_axes, col_axes):
    def local(particles, start_basis):
        shard = particles.shape[0]
        width = particles.shape[1]
        eig = start_basis.shape[1]
        total = shard * math.prod(sizes.values())
        spread = 2.0 * width
        root_total = math.sqrt(float(total))

        dense_basis = start_basis.reshape(shard * eig // 128, 128)
        i_feats, i_basis, j_feats = exchange_bfly(
            [("gather", row_axes), ("gather", row_axes), ("gather", col_axes)],
            [particles, dense_basis, particles])
        gi = group_size(row_axes)
        gj = group_size(col_axes)
        i_feats = i_feats.reshape(gi * shard, width)
        j_feats = j_feats.reshape(gj * shard, width)
        basis_i = i_basis.reshape(gi * shard, eig)

        def block_ids(digits):
            coords = member_coords(digits, jnp.arange(group_size(digits), dtype=jnp.int32))
            flat = jnp.zeros((group_size(digits),), jnp.int32)
            for a, cval in zip(MESH_AXES, coords):
                flat = flat * sizes[a] + cval
            return (flat[:, None] * shard + jnp.arange(shard, dtype=jnp.int32)[None, :]).reshape(-1)

        ids_i = block_ids(row_axes)
        ids_j = block_ids(col_axes)
        sq_i = jnp.sum(jnp.square(i_feats.astype(jnp.float32)), axis=1)
        sq_j = jnp.sum(jnp.square(j_feats.astype(jnp.float32)), axis=1)
        dots = lax.dot_general(i_feats, j_feats, (((1,), (1,)), ((), ())), preferred_element_type=jnp.float32)
        distance = sq_i[:, None] + sq_j[None, :] - 2.0 * dots
        tile = jnp.where(ids_i[:, None] == ids_j[None, :], jnp.float32(0.0), jnp.exp(-distance / spread))

        deg_i, deg_j = exchange(
            [("sum", row_axes), ("sum", col_axes)],
            [jnp.sum(tile, axis=1).reshape(-1, 128), jnp.sum(tile, axis=0).reshape(-1, 128)])
        deg_i = deg_i.reshape(-1)
        deg_j = deg_j.reshape(-1)
        root_i = jnp.sqrt(deg_i)
        root_j = jnp.sqrt(deg_j)
        me_i = group_pos(row_axes)
        scaled_i = basis_i / root_i[:, None]
        prod_j = lax.dot_general(tile, scaled_i, (((0,), (0,)), ((), ())), precision=HIGH)
        extra = jnp.concatenate([jnp.dot(root_i, basis_i, precision=HIGH)[None, :],
                                 jnp.broadcast_to(jnp.sum(deg_i), (1, eig)),
                                 jnp.zeros((6, eig), jnp.float32)], axis=0)
        dense_j, extra = exchange(
            [("rsag", col_axes), ("sum", col_axes)], [prod_j.reshape(-1, 128), extra.reshape(-1, 128)])
        prod_j = dense_j.reshape(-1, eig)
        extra = extra.reshape(-1, eig)
        inv_s = 1.0 / jnp.sqrt(extra[1, 0])
        aligned = extra[0] * inv_s
        defl_j = prod_j / root_j[:, None] - (root_j * inv_s)[:, None] * aligned[None, :]

        gram = lax.dot_general(defl_j, defl_j, (((0,), (0,)), ((), ())), precision=HIGH).reshape(-1, 128)
        q_i = jnp.dot(tile, defl_j / root_j[:, None], precision=HIGH)
        aligned_part = jnp.pad(jnp.dot(root_j, defl_j, precision=HIGH), (0, 128 - eig))[None, :]
        small = jnp.concatenate([gram, aligned_part,
                                 jnp.zeros((2 * gi - gram.shape[0] - 1, 128), jnp.float32)], axis=0)
        q_i, small = exchange([("rsag", row_axes), ("rsag", row_axes)], [q_i.reshape(-1, 128), small])
        gram = small[:eig * eig // 128]
        part = small[eig * eig // 128:][:1, :eig]
        factor, inverse = chol_inv(gram.reshape(eig, eig))
        q_i = q_i.reshape(-1, eig)
        prod_i = lax.dot_general(q_i, inverse, (((1,), (1,)), ((), ())), precision=HIGH) * root_total
        aligned = jnp.dot(inverse, part[0], precision=HIGH) * (root_total * inv_s)
        defl_i = prod_i / root_i[:, None] - (root_i * inv_s)[:, None] * aligned[None, :]

        gram = lax.dot_general(defl_i, defl_i, (((0,), (0,)), ((), ())), precision=HIGH).reshape(-1, 128)
        (gram,) = exchange([("sum", col_axes)], [gram])
        factor, inverse = chol_inv(gram.reshape(eig, eig))
        own = lax.dynamic_slice_in_dim(defl_i, me_i * shard, shard, 0)
        basis_own = lax.dot_general(own, inverse, (((1,), (1,)), ((), ())), precision=HIGH) * root_total
        return basis_own, factor

    return local


def solution(mesh):
    sizes = dict(mesh.shape)
    placed = (P(MESH_AXES, None), P(MESH_AXES, None))
    return jax.shard_map(
        make_local(sizes, (("row", 1, 2), ("vec", 1, sizes["vec"]), ("row", 2, sizes["row"] // 2)),
                   (("col", 1, 2), ("col", 2, sizes["col"] // 2))),
        mesh=mesh,
        in_specs=placed,
        out_specs=(P(MESH_AXES, None), P()),
        check_vma=False,
    )
```

```python
import functools
import math

import jax
import jax.numpy as jnp
from jax import lax
from jax.experimental import pallas as pl
from jax.experimental.pallas import tpu as pltpu
from jax.sharding import PartitionSpec as P

ITERS = 2
MESH_AXES = ("row", "col", "vec")
MESH = pl.DeviceIdType.MESH
HIGH = lax.Precision.HIGHEST


def group_pos(digits):
    me = 0
    for a, div, mod in digits:
        me = me * mod + (lax.axis_index(a) // div) % mod
    return me


def group_size(digits):
    return math.prod(mod for _, _, mod in digits)


def member_coords(digits, m):
    own = {a: lax.axis_index(a) for a in MESH_AXES}
    coords = dict(own)
    rem = m
    for a, div, mod in reversed(digits):
        d = rem % mod
        rem = rem // mod
        coords[a] = coords[a] - ((own[a] // div) % mod) * div + d * div
    return tuple(coords[a] for a in MESH_AXES)


def op_rounds(kind, g):
    bits = g.bit_length() - 1
    return 2 * bits if kind == "rsag" else bits


def exchange_kernel(ops, *refs):
    n = len(ops)
    ins, outs, scr = refs[:n], refs[n:2 * n], refs[2 * n:]
    barrier = pltpu.get_barrier_semaphore()
    groups = []
    for _, digits in ops:
        if digits not in groups:
            groups.append(digits)
    count = 0
    for digits in groups:
        me = group_pos(digits)
        span = 1
        for _, _, radix in reversed(digits):
            mine = (me // span) % radix
            for dd in range(1, radix):
                partner = me + ((mine + dd) % radix - mine) * span
                pl.semaphore_signal(barrier, inc=1, device_id=member_coords(digits, partner), device_id_type=MESH)
                count += 1
            span *= radix
    pl.semaphore_wait(barrier, count)

    state = []
    for i, (kind, digits) in enumerate(ops):
        w, ssem, rsem = scr[3 * i:3 * i + 3]
        w[group_pos(digits)] = ins[i][...]
        state.append((w, ssem, rsem))

    nrounds = max(len(d) for _, d in ops)
    for t in range(nrounds):
        waits = []
        for i, (kind, digits) in enumerate(ops):
            if t >= len(digits):
                continue
            radices = [mod for _, _, mod in reversed(digits)]
            radix = radices[t]
            span = math.prod(radices[:t])
            me = group_pos(digits)
            mine = (me // span) % radix
            base = (me // span) * span
            w, ssem, rsem = state[i]
            for dd in range(1, radix):
                partner = me + ((mine + dd) % radix - mine) * span
                sender = base + ((mine + radix - dd) % radix - mine) * span
                out = pltpu.make_async_remote_copy(
                    src_ref=w.at[pl.ds(base, span)], dst_ref=w.at[pl.ds(base, span)],
                    send_sem=ssem.at[t, dd], recv_sem=rsem.at[t, dd],
                    device_id=member_coords(digits, partner), device_id_type=MESH)
                out.start()
                back = pltpu.make_async_remote_copy(
                    src_ref=w.at[pl.ds(base, span)], dst_ref=w.at[pl.ds(sender, span)],
                    send_sem=ssem.at[t, dd], recv_sem=rsem.at[t, dd],
                    device_id=member_coords(digits, partner), device_id_type=MESH)
                waits.append((out, back))
        for out, back in waits:
            back.wait_recv()
            out.wait_send()
    for i in range(n):
        outs[i][...] = state[i][0][...]


def direct_kernel(ops, groups, *refs):
    n = len(ops)
    ins, outs, scr = refs[:n], refs[n:2 * n], refs[2 * n:]
    barrier = pltpu.get_barrier_semaphore()
    total_peers = 0
    for axes in groups:
        g = group_size(axes)
        me = group_pos(axes)
        total_peers += g - 1

        def greet(k, c, axes=axes, g=g, me=me):
            pl.semaphore_signal(barrier, inc=1, device_id=member_coords(axes, (me + k) % g), device_id_type=MESH)
            return c

        lax.fori_loop(1, g, greet, 0)
    pl.semaphore_wait(barrier, total_peers)

    pos = 0
    pending = []
    for i, (kind, axes) in enumerate(ops):
        g = group_size(axes)
        me = group_pos(axes)
        x_ref, o_ref = ins[i], outs[i]
        if kind in ("gather", "sum"):
            slots, ssem, rsem = scr[pos:pos + 3]
            pos += 3
            slots[me] = x_ref[...]

            def send(k, c, x_ref=x_ref, slots=slots, ssem=ssem, rsem=rsem, axes=axes, g=g, me=me):
                peer = (me + k) % g
                pltpu.make_async_remote_copy(
                    src_ref=x_ref, dst_ref=slots.at[me], send_sem=ssem.at[peer], recv_sem=rsem.at[me],
                    device_id=member_coords(axes, peer), device_id_type=MESH).start()
                return c

            lax.fori_loop(1, g, send, 0)
            pending.append((kind, axes, g, me, x_ref, o_ref, slots, ssem, rsem))
        else:
            rs, ag, ssem, rsem, ssem2, rsem2 = scr[pos:pos + 6]
            pos += 6
            c = x_ref.shape[0] // g
            rs[me] = x_ref[pl.ds(pl.multiple_of(me * c, c), c)]

            def send(k, cc, x_ref=x_ref, rs=rs, ssem=ssem, rsem=rsem, axes=axes, g=g, me=me, c=c):
                peer = (me + k) % g
                pltpu.make_async_remote_copy(
                    src_ref=x_ref.at[pl.ds(pl.multiple_of(peer * c, c), c)], dst_ref=rs.at[me],
                    send_sem=ssem.at[peer], recv_sem=rsem.at[me],
                    device_id=member_coords(axes, peer), device_id_type=MESH).start()
                return cc

            lax.fori_loop(1, g, send, 0)
            pending.append((kind, axes, g, me, x_ref, o_ref, (rs, ag, ssem2, rsem2), ssem, rsem))

    second = []
    for kind, axes, g, me, x_ref, o_ref, slots, ssem, rsem in pending:
        if kind == "rsag":
            rs, ag, ssem2, rsem2 = slots
            c = rs.shape[1]
        else:
            rs = slots

        def wait(k, cc, x_ref=x_ref, rs=rs, ssem=ssem, rsem=rsem, axes=axes, g=g, me=me, kind=kind):
            src = (me + g - k) % g
            peer = (me + k) % g
            if kind == "rsag":
                c = rs.shape[1]
                src_ref = x_ref.at[pl.ds(0, c)]
            else:
                src_ref = x_ref
            pltpu.make_async_remote_copy(
                src_ref=src_ref, dst_ref=rs.at[src], send_sem=ssem.at[peer], recv_sem=rsem.at[src],
                device_id=member_coords(axes, peer), device_id_type=MESH).wait_recv()
            pltpu.make_async_remote_copy(
                src_ref=src_ref, dst_ref=rs.at[me], send_sem=ssem.at[peer], recv_sem=rsem.at[me],
                device_id=member_coords(axes, peer), device_id_type=MESH).wait_send()
            return cc

        lax.fori_loop(1, g, wait, 0)
        if kind == "gather":
            o_ref[...] = rs[...]
        elif kind == "sum":
            acc = rs[0]
            for s in range(1, g):
                acc = acc + rs[s]
            o_ref[...] = acc
        else:
            acc = rs[0]
            for s in range(1, g):
                acc = acc + rs[s]
            ag[me] = acc

            def send2(k, cc, ag=ag, ssem2=ssem2, rsem2=rsem2, axes=axes, g=g, me=me):
                peer = (me + k) % g
                pltpu.make_async_remote_copy(
                    src_ref=ag.at[me], dst_ref=ag.at[me], send_sem=ssem2.at[peer], recv_sem=rsem2.at[me],
                    device_id=member_coords(axes, peer), device_id_type=MESH).start()
                return cc

            lax.fori_loop(1, g, send2, 0)
            second.append((axes, g, me, o_ref, ag, ssem2, rsem2))

    for axes, g, me, o_ref, ag, ssem2, rsem2 in second:
        if g > 1:

            def wait2(k, cc, ag=ag, ssem2=ssem2, rsem2=rsem2, axes=axes, g=g, me=me):
                src = (me + g - k) % g
                peer = (me + k) % g
                pltpu.make_async_remote_copy(
                    src_ref=ag.at[me], dst_ref=ag.at[src], send_sem=ssem2.at[peer], recv_sem=rsem2.at[src],
                    device_id=member_coords(axes, peer), device_id_type=MESH).wait_recv()
                pltpu.make_async_remote_copy(
                    src_ref=ag.at[me], dst_ref=ag.at[me], send_sem=ssem2.at[peer], recv_sem=rsem2.at[me],
                    device_id=member_coords(axes, peer), device_id_type=MESH).wait_send()
                return cc

            lax.fori_loop(1, g, wait2, 0)
            o_ref[...] = ag[...]


def chol_kernel(g_ref, l_ref, inv_ref):
    a = g_ref[...]
    n = a.shape[0]
    rows = lax.broadcasted_iota(jnp.int32, (n, n), 0)
    lanes = lax.broadcasted_iota(jnp.int32, (n, n), 1)
    eye = (rows == lanes).astype(jnp.float32)
    x = eye
    lmat = jnp.zeros_like(a)
    for j in range(n):
        d = jnp.sqrt(a[j:j + 1, j:j + 1])
        r = 1.0 / d
        col = jnp.where(rows[:, j:j + 1] >= j, a[:, j:j + 1], 0.0) * r
        rowv = jnp.where(lanes[j:j + 1, :] >= j, a[j:j + 1, :], 0.0) * r
        a = a - col * rowv
        lmat = jnp.where(lanes == j, col, lmat)
        xj = x[j:j + 1, :] * r
        below = jnp.where(rows[:, j:j + 1] > j, col, 0.0)
        x = jnp.where(rows == j, xj, x - below * xj)
    l_ref[...] = lmat
    inv_ref[...] = x

def chol_inv(gram):
    n = gram.shape[0]
    gram = jnp.tril(gram) + jnp.tril(gram, -1).T
    return pl.pallas_call(chol_kernel,
        out_shape=[jax.ShapeDtypeStruct((n, n), jnp.float32)] * 2,
        in_specs=[pl.BlockSpec(memory_space=pltpu.VMEM)],
        out_specs=[pl.BlockSpec(memory_space=pltpu.VMEM)] * 2)(gram)


_IDS = {}


def exchange(ops, xs):
    key = ("direct",) + tuple((k, d, x.shape, str(x.dtype)) for (k, d), x in zip(ops, xs))
    if key not in _IDS:
        _IDS[key] = len(_IDS)
    groups = []
    for _, axes in ops:
        if axes not in groups:
            groups.append(axes)
    out_shapes, scratch = [], []
    for (kind, axes), x in zip(ops, xs):
        g = group_size(axes)
        if kind == "sum":
            out_shapes.append(jax.ShapeDtypeStruct(x.shape, x.dtype))
            scratch += [pltpu.VMEM((g,) + x.shape, x.dtype), pltpu.SemaphoreType.DMA((g,)),
                        pltpu.SemaphoreType.DMA((g,))]
        else:
            c = x.shape[0] // g
            out_shapes.append(jax.ShapeDtypeStruct((g, c) + x.shape[1:], x.dtype))
            scratch += [pltpu.VMEM((g, c) + x.shape[1:], x.dtype), pltpu.VMEM((g, c) + x.shape[1:], x.dtype),
                        pltpu.SemaphoreType.DMA((g,)), pltpu.SemaphoreType.DMA((g,)),
                        pltpu.SemaphoreType.DMA((g,)), pltpu.SemaphoreType.DMA((g,))]
    outs = pl.pallas_call(
        functools.partial(direct_kernel, ops, groups),
        out_shape=out_shapes,
        in_specs=[pl.BlockSpec(memory_space=pltpu.VMEM)] * len(xs),
        out_specs=[pl.BlockSpec(memory_space=pltpu.VMEM)] * len(xs),
        scratch_shapes=scratch,
        compiler_params=pltpu.CompilerParams(collective_id=_IDS[key], has_side_effects=True),
    )(*xs)
    return [o.reshape(x.shape) for o, x in zip(outs, xs)]


def exchange_bfly(ops, xs):
    key = ("bfly",) + tuple((k, d, x.shape, str(x.dtype)) for (k, d), x in zip(ops, xs))
    if key not in _IDS:
        _IDS[key] = len(_IDS)
    out_shapes, scratch = [], []
    for (kind, digits), x in zip(ops, xs):
        g = group_size(digits)
        rmax = max(mod for _, _, mod in digits)
        out_shapes.append(jax.ShapeDtypeStruct((g,) + x.shape, x.dtype))
        scratch += [pltpu.VMEM((g,) + x.shape, x.dtype),
                    pltpu.SemaphoreType.DMA((len(digits), rmax)), pltpu.SemaphoreType.DMA((len(digits), rmax))]
    outs = pl.pallas_call(
        functools.partial(exchange_kernel, ops),
        out_shape=out_shapes,
        in_specs=[pl.BlockSpec(memory_space=pltpu.VMEM)] * len(xs),
        out_specs=[pl.BlockSpec(memory_space=pltpu.VMEM)] * len(xs),
        scratch_shapes=scratch,
        compiler_params=pltpu.CompilerParams(collective_id=_IDS[key], has_side_effects=True),
    )(*xs)
    return list(outs)


def make_local(sizes, row_axes, col_axes):
    def local(particles, start_basis):
        shard = particles.shape[0]
        width = particles.shape[1]
        eig = start_basis.shape[1]
        total = shard * math.prod(sizes.values())
        spread = 2.0 * width
        root_total = math.sqrt(float(total))

        dense_basis = start_basis
        i_feats, i_basis, j_feats = exchange_bfly(
            [("gather", row_axes), ("gather", row_axes), ("gather", col_axes)],
            [particles, dense_basis, particles])
        gi = group_size(row_axes)
        gj = group_size(col_axes)
        i_feats = i_feats.reshape(gi * shard, width)
        j_feats = j_feats.reshape(gj * shard, width)
        basis_i = i_basis.reshape(gi * shard, eig)

        def block_ids(digits):
            coords = member_coords(digits, jnp.arange(group_size(digits), dtype=jnp.int32))
            flat = jnp.zeros((group_size(digits),), jnp.int32)
            for a, cval in zip(MESH_AXES, coords):
                flat = flat * sizes[a] + cval
            return (flat[:, None] * shard + jnp.arange(shard, dtype=jnp.int32)[None, :]).reshape(-1)

        ids_i = block_ids(row_axes)
        ids_j = block_ids(col_axes)
        sq_i = jnp.sum(jnp.square(i_feats.astype(jnp.float32)), axis=1)
        sq_j = jnp.sum(jnp.square(j_feats.astype(jnp.float32)), axis=1)
        dots = lax.dot_general(i_feats, j_feats, (((1,), (1,)), ((), ())), preferred_element_type=jnp.float32)
        distance = sq_i[:, None] + sq_j[None, :] - 2.0 * dots
        tile = jnp.where(ids_i[:, None] == ids_j[None, :], jnp.float32(0.0), jnp.exp(-distance / spread))

        deg_i, deg_j = exchange(
            [("sum", row_axes), ("sum", col_axes)],
            [jnp.sum(tile, axis=1).reshape(-1, 128), jnp.sum(tile, axis=0).reshape(-1, 128)])
        deg_i = deg_i.reshape(-1)
        deg_j = deg_j.reshape(-1)
        root_i = jnp.sqrt(deg_i)
        root_j = jnp.sqrt(deg_j)
        me_i = group_pos(row_axes)
        scaled_i = basis_i / root_i[:, None]
        prod_j = lax.dot_general(tile, scaled_i, (((0,), (0,)), ((), ())), precision=HIGH)
        extra = jnp.concatenate([jnp.dot(root_i, basis_i, precision=HIGH)[None, :],
                                 jnp.broadcast_to(jnp.sum(deg_i), (1, eig)),
                                 jnp.zeros((6, eig), jnp.float32)], axis=0)
        dense_j, extra = exchange(
            [("rsag", col_axes), ("sum", col_axes)], [prod_j.reshape(-1, 128), extra.reshape(-1, 128)])
        prod_j = dense_j.reshape(-1, eig)
        extra = extra.reshape(-1, eig)
        inv_s = 1.0 / jnp.sqrt(extra[1, 0])
        aligned = extra[0] * inv_s
        defl_j = prod_j / root_j[:, None] - (root_j * inv_s)[:, None] * aligned[None, :]

        gram = lax.dot_general(defl_j, defl_j, (((0,), (0,)), ((), ())), precision=HIGH).reshape(-1, 128)
        q_i = jnp.dot(tile, defl_j / root_j[:, None], precision=HIGH)
        aligned_part = jnp.pad(jnp.dot(root_j, defl_j, precision=HIGH), (0, 128 - eig))[None, :]
        small = jnp.concatenate([gram, aligned_part,
                                 jnp.zeros((2 * gi - gram.shape[0] - 1, 128), jnp.float32)], axis=0)
        small, q_i = exchange([("rsag", row_axes), ("rsag", row_axes)], [small, q_i.reshape(-1, 128)])
        gram = small[:eig * eig // 128]
        part = small[eig * eig // 128:][:1, :eig]
        factor, inverse = chol_inv(gram.reshape(eig, eig))
        q_i = q_i.reshape(-1, eig)
        prod_i = lax.dot_general(q_i, inverse, (((1,), (1,)), ((), ())), precision=HIGH) * root_total
        aligned = jnp.dot(inverse, part[0], precision=HIGH) * (root_total * inv_s)
        defl_i = prod_i / root_i[:, None] - (root_i * inv_s)[:, None] * aligned[None, :]

        gram = lax.dot_general(defl_i, defl_i, (((0,), (0,)), ((), ())), precision=HIGH).reshape(-1, 128)
        (gram,) = exchange([("sum", col_axes)], [gram])
        factor, inverse = chol_inv(gram.reshape(eig, eig))
        own = lax.dynamic_slice_in_dim(defl_i, me_i * shard, shard, 0)
        basis_own = lax.dot_general(own, inverse, (((1,), (1,)), ((), ())), precision=HIGH) * root_total
        return basis_own, factor

    return local


def solution(mesh):
    sizes = dict(mesh.shape)
    placed = (P(MESH_AXES, None), P(MESH_AXES, None))
    return jax.shard_map(
        make_local(sizes, (("row", 1, 2), ("vec", 1, sizes["vec"]), ("row", 2, sizes["row"] // 2)),
                   (("col", 1, 2), ("col", 2, sizes["col"] // 2))),
        mesh=mesh,
        in_specs=placed,
        out_specs=(P(MESH_AXES, None), P()),
        check_vma=False,
    )
```
